128 devices in a mesh: req: 16 (over x, y), exp: 8 (over z, core).
Axes of the slice: x: 4, y: 4, z: 4, core: 2. Of those that a mesh axis runs over, the one named last changes fastest.
Arguments:
- tokens: bfloat16 [16384, 2048], P(('req', 'exp')), may hold values from -6 to 6
- attn_gain: float32 [2048], replicated, may hold values from 0.1 to 1.9
- w_query: bfloat16 [2048, 2048], P(None, 'exp'), may hold values from -0.25 to 0.25
- w_key: bfloat16 [2048, 2048], P(None, 'exp'), may hold values from -0.125 to 0.125
- w_value: bfloat16 [2048, 2048], P(None, 'exp'), may hold values from -0.125 to 0.125
- w_out: bfloat16 [2048, 2048], P('exp'), may hold values from -0.375 to 0.375
- prefix_cache: bfloat16 [8, 1024, 2, 2048], P(None, 'req', None, 'exp'), may hold values from -205 to 205
- group_of: int32 [16], replicated, may hold values from 0 to 7
- lengths: int32 [16], replicated, may hold values from 1 to 1024, 10240 in all
- moe_gain: float32 [2048], replicated, may hold values from 0.1 to 1.9
- w_gate: bfloat16 [128, 2048, 512], P(('req', 'exp')), may hold values from -0.125 to 0.125
- w_up: bfloat16 [128, 2048, 512], P(('req', 'exp')), may hold values from -0.125 to 0.125
- w_down: bfloat16 [128, 512, 2048], P(('req', 'exp')), may hold values from -0.25 to 0.25
- routes: int32 [16384, 8], P(('req', 'exp')), may hold values from 0 to 63, all different within a row; in each aligned block of 128 rows (0 to 127, 128 to 255, ...) at most 18 rows name the same one
- route_weights: float32 [16384, 8], P(('req', 'exp')), may hold values from 0.1 to 0.4
Outputs:
- layer_out: bfloat16 [16384, 2048], P(('req', 'exp'))
The draws below stay inside these ranges and needn't reach their ends.
Inputs may be any that keep to these rules, and one draw needn't show every extreme that they name: `routes`: in the rows of one device no expert is named more than 18 times.
All inputs are finite; a program needn't handle non-finite values.
Results may differ from the reference program's by a relative error of at most 0.017.
Values may be sent and summed in bfloat16 or wider, within the bound.
No kernel may reach another device: no remote copies, remote signals or barrier semaphores. Data moves between devices by JAX's collectives and lax.ppermute only.
A program may use at most 192 MiB of HBM per device.

```python
import math
import jax
import jax.numpy as jnp
import numpy as np
from jax import lax

D = 2048
HEADS = 16
HD = 128
FF = 1024
TOP = 8
TOK_DEV = 128
PREFIX = 1024
EXPERTS = 64
GROUPS = 8
SLOTS = 1024
ROWS = 16384
CAP = 18
N_REQ = 16
N_EXP = 8


def draw_prefix_cache(key, part):
    base_key = jax.random.fold_in(jax.random.fold_in(key, 11), 0)
    shape = (GROUPS, PREFIX, 2, HEADS * HD)
    base = jnp.clip(jax.random.normal(base_key, shape, jnp.float32), -6.0, 6.0)
    return base.astype(jnp.bfloat16)


def plant(values, key, low, high):
    longest = values.shape.index(max(values.shape))
    spots = []
    for shift in (0, 1):
        where = [jax.random.randint(jax.random.fold_in(key, axis), (), 0, length) for axis, length in enumerate(values.shape)]
        where[longest] = (where[longest] + shift) % values.shape[longest]
        spots.append(tuple(where))
    return values.at[spots[0]].set(low).at[spots[1]].set(high)


def block_levels(key, extent, shards, smallest, top_value):
    factor_of = 1.0
    for axis_at, shards_of in shards:
        heights = jax.random.uniform(jax.random.fold_in(jax.random.fold_in(key, 6), axis_at), (shards_of,), jnp.float32, smallest / len(shards), top_value / len(shards))
        factor_of = factor_of * jnp.repeat(jnp.exp(heights), extent[axis_at] // shards_of).reshape((-1,) + (1,) * (len(extent) - 1 - axis_at))
    return factor_of


def split_up(amount, total, reach, lean):
    loads = [(1 << 20) // math.isqrt(grade ** lean) + 1 for grade in range(2, amount + 1)]
    spare, holding = total - reach - (amount - 1), [1] * (amount - 1)
    while spare > 0:
        free = [i for i in range(amount - 1) if holding[i] < reach]
        mass, left = sum([loads[i] for i in free]), spare
        for i in free:
            extra = min(reach - holding[i], max(1, left * loads[i] // mass), spare)
            holding[i] = holding[i] + extra
            spare = spare - extra
    return np.array([reach] + holding)


def ragged(stream_key, amount, total, most, lean):
    if amount == 2:
        one = jax.random.randint(stream_key, (), max(1, total - most), min(most, total - 1) + 1)
        return jnp.stack([one, total - one])
    sizes = jnp.asarray(split_up(amount, total, most, lean), jnp.int32)
    pairs = (amount - 1) // 2
    source_of, receiver = sizes[1:1 + 2 * pairs:2], sizes[2:2 + 2 * pairs:2]
    slack = jnp.minimum(source_of - 1, most - receiver)
    moved = jax.random.randint(jax.random.fold_in(stream_key, 1), (pairs,), 0, 1 << 20) % (slack + 1)
    sizes = sizes.at[1:1 + 2 * pairs:2].set(source_of - moved).at[2:2 + 2 * pairs:2].set(receiver + moved)
    return sizes[jax.random.permutation(jax.random.fold_in(stream_key, 2), amount)]


def routed_block(key, own, number, rows, number_of, top, reach, slope):
    order = jax.random.permutation(key, number_of)
    packed, ordinary = shares(number_of, rows * top, reach, slope, True), shares(number_of, rows * top, reach, slope, False)
    places = jnp.arange(number_of)

    def named(sizes, offset_by):
        used = int((sizes > 0).sum())
        fixed = max(1, used // 4)
        passed = fixed + (places - fixed + offset_by * (used - fixed)) % max(1, number_of - fixed)
        return jnp.zeros((number_of,), jnp.int32).at[order[jnp.where(places < fixed, places, passed)]].set(jnp.asarray(sizes, jnp.int32))

    sizes = jnp.where(number % 4 == 0, named(packed, number // 4), named(ordinary, number - number // 4 - 1))
    mixed = jax.random.permutation(jax.random.fold_in(own, 3), number_of)
    source_of, taker = mixed[0:number_of // 2 * 2:2], mixed[1:number_of // 2 * 2:2]
    room = jnp.minimum(sizes[source_of] - 1, reach - sizes[taker]) // 2
    room = jnp.where((source_of == order[0]) | (taker == order[0]) | (sizes[taker] == 0), 0, jnp.maximum(room, 0))
    passed = jax.random.randint(jax.random.fold_in(own, 4), (number_of // 2,), 0, 1 << 20) % (room + 1)
    sizes = sizes.at[source_of].add(-passed).at[taker].add(passed)
    items = jnp.searchsorted(jnp.cumsum(sizes), jnp.arange(rows * top), side="right").astype(jnp.int32)
    listing = items.reshape(top, rows).T
    listing = listing[jax.random.permutation(jax.random.fold_in(own, 1), rows)]
    offset_by = jax.random.randint(jax.random.fold_in(own, 2), (rows, 1), 0, top)
    return jnp.take_along_axis(listing, (jnp.arange(top)[None, :] + offset_by) % top, axis=1)


def shares(count, total, bound, skew, full):
    loads = [(1 << 20) // math.isqrt(rank ** skew) + 1 for rank in range(1, count + 1)]
    largest = bound if full else min(bound, max(-(-total // count), total * loads[0] // sum(loads)))
    least = 1 if total - largest >= count - 1 else 0
    given, surplus = [largest] + [least] * (count - 1), total - largest - least * (count - 1)
    while surplus > 0:
        candidates = [i for i in range(1, count) if given[i] < largest] or [i for i in range(1, count) if given[i] < bound]
        whole, left = sum([loads[i] for i in candidates]), surplus
        for i in candidates:
            more = min(bound - given[i], max(1, left * loads[i] // whole), surplus)
            given[i] = given[i] + more
            surplus = surplus - more
    return np.array(given)


def noise(own_key, dims, deviation, bound, cuts=(), kind=jnp.bfloat16):
    factor_of = block_levels(own_key, dims, cuts, -0.22, 0.18) if cuts else 1.0
    values = jax.random.normal(own_key, dims, jnp.float32) * deviation * factor_of
    return jnp.minimum(jnp.maximum(values, -bound), bound).astype(kind)


def setup_inputs(seed: int = 0) -> dict:
    arg_keys = jax.random.split(jax.random.key(seed), 16)
    tokens = noise(arg_keys[0], (ROWS, D), 1.0, 6.0, ((0, 128),))
    attn_gain = jnp.clip(1.0 + 0.18 * jax.random.normal(arg_keys[1], (D,), jnp.float32), 0.1, 1.9)
    w_query = noise(arg_keys[2], (D, HEADS * HD), (D // 4) ** -0.5, 0.25, ((1, 8),))
    w_key = noise(arg_keys[3], (D, HEADS * HD), D ** -0.5, 0.125, ((1, 8),))
    w_value = noise(arg_keys[4], (D, HEADS * HD), D ** -0.5, 0.125, ((1, 8),))
    w_out = noise(arg_keys[5], (HEADS * HD, D), (HEADS * HD // 8) ** -0.5, 0.375, ((0, 8),))
    prefix_cache = draw_prefix_cache(jax.random.fold_in(arg_keys[15], 71), 0)
    group_of = plant(jax.random.randint(arg_keys[7], (N_REQ,), 0, GROUPS), jax.random.fold_in(arg_keys[7], 1), 0, GROUPS - 1).astype(jnp.int32)
    lengths = ragged(arg_keys[8], N_REQ, N_REQ * SLOTS * 5 // 8, SLOTS, 2).astype(jnp.int32)
    moe_gain = jnp.clip(1.0 + 0.18 * jax.random.normal(arg_keys[9], (D,), jnp.float32), 0.1, 1.9)
    w_gate = noise(arg_keys[10], (2 * EXPERTS, D, FF // 2), D ** -0.5, 0.125, ((0, 128),))
    w_up = noise(arg_keys[11], (2 * EXPERTS, D, FF // 2), D ** -0.5, 0.125, ((0, 128),))
    w_down = noise(arg_keys[12], (2 * EXPERTS, FF // 2, D), (FF // 2) ** -0.5, 0.25, ((0, 128),))
    routes_keys = jax.random.split(jax.random.fold_in(arg_keys[13], 1), ROWS // TOK_DEV)
    routes_turns = jax.random.permutation(jax.random.fold_in(arg_keys[13], 3), ROWS // TOK_DEV)
    routes = jax.vmap(lambda own, number: routed_block(jax.random.fold_in(arg_keys[13], 2), own, number, TOK_DEV, EXPERTS, TOP, CAP, 1))(routes_keys, routes_turns).reshape((ROWS, TOP))
    route_weights = jnp.clip(0.1 + 0.3 * jax.random.uniform(arg_keys[14], (ROWS, TOP), jnp.float32) ** block_levels(arg_keys[14], (ROWS, TOP), ((0, 128),), -0.2, 0.2), 0.1, 0.4)
    return {"tokens": tokens, "attn_gain": attn_gain, "w_query": w_query, "w_key": w_key, "w_value": w_value, "w_out": w_out, "prefix_cache": prefix_cache, "group_of": group_of, "lengths": lengths, "moe_gain": moe_gain, "w_gate": w_gate, "w_up": w_up, "w_down": w_down, "routes": routes, "route_weights": route_weights}


def norm_rows(values, gain):
    wide = values.astype(jnp.float32)
    return wide * lax.rsqrt(lax.optimization_barrier(jnp.mean(wide * wide, axis=-1, keepdims=True)) + 1e-05) * gain

def rotate(vectors, places):
    half = vectors.shape[-1] // 2
    freqs = 10000.0 ** (-(jnp.arange(half, dtype=jnp.float32) * 2.0) / vectors.shape[-1])
    angles = places[:, None] * freqs[None, :]
    cosine = jnp.cos(angles)[:, None, :]
    sine = jnp.sin(angles)[:, None, :]
    first = vectors[..., :half]
    second = vectors[..., half:]
    return jnp.concatenate([first * cosine - second * sine, first * sine + second * cosine], axis=-1)

def reference(tokens, attn_gain, w_query, w_key, w_value, w_out, prefix_cache, group_of, lengths, moe_gain, w_gate, w_up, w_down, routes, route_weights):
    places = (PREFIX + jnp.arange(SLOTS, dtype=jnp.int32)).astype(jnp.float32)

    def one_request(request):
        rows_in = lax.dynamic_slice_in_dim(tokens, request * SLOTS, SLOTS, 0)
        normed = norm_rows(rows_in, attn_gain).astype(jnp.bfloat16)
        query = jnp.dot(normed, w_query, preferred_element_type=jnp.float32).reshape(SLOTS, HEADS, HD)
        query = rotate(query, places).astype(jnp.bfloat16)
        key = jnp.dot(normed, w_key, preferred_element_type=jnp.float32).reshape(SLOTS, HEADS, HD)
        key = rotate(key, places).astype(jnp.bfloat16)
        value = jnp.dot(normed, w_value, preferred_element_type=jnp.float32).astype(jnp.bfloat16).reshape(SLOTS, HEADS, HD)
        cached = jnp.take(prefix_cache, group_of[request], axis=0)
        keys = jnp.concatenate([cached[:, 0].reshape(PREFIX, HEADS, HD), key], axis=0)
        values = jnp.concatenate([cached[:, 1].reshape(PREFIX, HEADS, HD), value], axis=0)
        scores = jnp.einsum('qhd,khd->hqk', query.astype(jnp.float32), keys.astype(jnp.float32)) / math.sqrt(HD)
        live = jnp.concatenate([jnp.ones((PREFIX,), bool), jnp.arange(SLOTS, dtype=jnp.int32) < lengths[request]])
        scores = jnp.where(live[None, None, :], scores, -1e+30)
        top_score = lax.optimization_barrier(jnp.max(scores, axis=-1, keepdims=True))
        raised = jnp.exp(scores - top_score)
        probs = (raised / lax.optimization_barrier(jnp.sum(raised, axis=-1, keepdims=True))).astype(jnp.bfloat16)
        attn = jnp.einsum('hqk,khd->qhd', probs.astype(jnp.float32), values.astype(jnp.float32)).astype(jnp.bfloat16)
        attn_out = jnp.dot(attn.reshape(SLOTS, HEADS * HD), w_out, preferred_element_type=jnp.float32)
        return (rows_in.astype(jnp.float32) + attn_out).astype(jnp.bfloat16)
    hidden_state = lax.map(one_request, jnp.arange(N_REQ, dtype=jnp.int32)).reshape(ROWS, D)
    normed2 = norm_rows(hidden_state, moe_gain).astype(jnp.bfloat16)
    flat = routes.reshape(-1).astype(jnp.int32)
    order = jnp.argsort(flat, stable=True).astype(jnp.int32)
    sorted_ids = flat[order]
    starts = jnp.searchsorted(sorted_ids, jnp.arange(EXPERTS, dtype=jnp.int32)).astype(jnp.int32)
    ends = jnp.concatenate([starts[1:], jnp.array([ROWS * TOP], dtype=jnp.int32)])
    counts = ends - starts
    most_rows = N_REQ * N_EXP * CAP
    flat_weights = route_weights.reshape(-1)

    def expert_step(total, expert):
        offsets = jnp.arange(most_rows, dtype=jnp.int32)
        valid = offsets < counts[expert]
        index = jnp.minimum(starts[expert] + offsets, ROWS * TOP - 1)
        pair = order[index]
        source = pair // TOP
        rows_in = normed2[source]
        result = jnp.zeros((most_rows, D), jnp.float32)
        for half in range(2):
            gate = jnp.dot(rows_in, w_gate[2 * expert + half], preferred_element_type=jnp.float32)
            upper = jnp.dot(rows_in, w_up[2 * expert + half], preferred_element_type=jnp.float32)
            act = (jax.nn.silu(gate) * upper).astype(jnp.bfloat16)
            result = result + jnp.dot(act, w_down[2 * expert + half], preferred_element_type=jnp.float32)
        part = lax.optimization_barrier(result.astype(jnp.bfloat16))
        scale = jnp.where(valid, flat_weights[pair], 0.0)
        return (total.at[source].add(part.astype(jnp.float32) * scale[:, None]), None)
    moe, _ = lax.scan(expert_step, jnp.zeros((ROWS, D), jnp.float32), jnp.arange(EXPERTS, dtype=jnp.int32))
    slot_index = jnp.arange(ROWS, dtype=jnp.int32)
    live_rows = slot_index % SLOTS < lengths[slot_index // SLOTS]
    return jnp.where(live_rows[:, None], hidden_state.astype(jnp.float32) + moe, 0.0).astype(jnp.bfloat16)
```

```python
import math

import jax
import jax.numpy as jnp
import numpy as np
from jax import lax
from jax.experimental import pallas as pl
from jax.experimental.pallas import tpu as pltpu
from jax.sharding import Mesh
from jax.sharding import PartitionSpec as P

HD = 128
PREFIX = 1024
BF = jnp.bfloat16
F32 = jnp.float32
SUB = 8


def vmem():
    return pl.BlockSpec(memory_space=pltpu.VMEM)


def call(kernel, out_shape, n_in, **kw):
    outs = jax.tree.map(lambda _: vmem(), out_shape)
    return pl.pallas_call(
        kernel, out_shape=out_shape, in_specs=[vmem()] * n_in, out_specs=outs, **kw
    )


def shape(dims, dtype):
    return jax.ShapeDtypeStruct(dims, dtype)


def dot(a, b):
    return jnp.dot(a, b, preferred_element_type=F32)


def rms(wide, gain):
    return wide * lax.rsqrt(jnp.mean(wide * wide, axis=-1, keepdims=True) + 1e-05) * gain


def norm_kernel(x_ref, g_ref, o_ref):
    o_ref[...] = rms(x_ref[...].astype(F32), g_ref[...]).astype(BF)


def route_kernel(r_ref, rt_ref, w_ref, dt_ref, wm_ref, wx_ref):
    rows, top = r_ref.shape
    experts = dt_ref.shape[0] // (2 * (SUB + 1))
    wide = experts * SUB
    row_i = lax.broadcasted_iota(jnp.int32, (rows, rows), 0)
    col_i = lax.broadcasted_iota(jnp.int32, (rows, rows), 1)
    e_t = lax.broadcasted_iota(jnp.int32, (experts, rows), 0)
    named_t = jnp.zeros((experts, rows), F32)
    for k in range(top):
        named_t += jnp.where(rt_ref[k : k + 1, :] == e_t, 1.0, 0.0)
    rank_t = dot(named_t.astype(BF), jnp.where(row_i < col_i, 1.0, 0.0).astype(BF))
    rank_t = jnp.where(named_t > 0.5, rank_t, -1.0)
    j_t = lax.broadcasted_iota(jnp.int32, (wide, experts), 0)
    spread_t = jnp.where(
        j_t // SUB == lax.broadcasted_iota(jnp.int32, (wide, experts), 1), 1.0, 0.0
    ).astype(BF)
    big_t = dot(spread_t, rank_t.astype(BF))
    slot_t = (lax.broadcasted_iota(jnp.int32, (wide, rows), 0) % SUB).astype(F32)
    for c in range(2):
        first = float(c * (SUB + 1))
        at = c * (wide + experts)
        dt_ref[at : at + wide, :] = jnp.where(big_t == slot_t + first, 1.0, 0.0).astype(BF)
        dt_ref[at + wide : at + wide + experts, :] = jnp.where(
            rank_t == first + SUB, 1.0, 0.0
        ).astype(BF)
    e_n = lax.broadcasted_iota(jnp.int32, (rows, experts), 1)
    named = jnp.zeros((rows, experts), F32)
    weight = jnp.zeros((rows, experts), F32)
    for k in range(top):
        hit = r_ref[:, k : k + 1] == e_n
        named += jnp.where(hit, 1.0, 0.0)
        weight += jnp.where(hit, w_ref[:, k : k + 1], 0.0)
    rank = dot(jnp.where(col_i < row_i, 1.0, 0.0).astype(BF), named.astype(BF))
    rank = jnp.where(named > 0.5, rank, -1.0)
    high = weight.astype(BF)
    low = (weight - high.astype(F32)).astype(BF)
    j_n = lax.broadcasted_iota(jnp.int32, (experts, wide), 1)
    spread = jnp.where(
        j_n // SUB == lax.broadcasted_iota(jnp.int32, (experts, wide), 0), 1.0, 0.0
    ).astype(BF)
    big = dot(rank.astype(BF), spread)
    big_high = dot(high, spread)
    big_low = dot(low, spread)
    slot = (lax.broadcasted_iota(jnp.int32, (rows, wide), 1) % SUB).astype(F32)
    for c in range(2):
        first = float(c * (SUB + 1))
        hit = big == slot + first
        wm_ref[:rows, c * wide : (c + 1) * wide] = jnp.where(hit, big_high, 0.0).astype(BF)
        wm_ref[rows:, c * wide : (c + 1) * wide] = jnp.where(hit, big_low, 0.0).astype(BF)
        hit = rank == first + SUB
        wx_ref[c, :rows, :] = jnp.where(hit, high.astype(F32), 0.0).astype(BF)
        wx_ref[c, rows:, :] = jnp.where(hit, low.astype(F32), 0.0).astype(BF)


def prefix_kernel(group_ref, x_ref, o_ref):
    width = x_ref.shape[-1]
    x = x_ref[0].astype(F32)
    o_ref[:, :width] = x[:, 0, :].astype(BF)
    o_ref[:, width:] = x[:, 1, :].astype(BF)


def qkv_kernel(count, *refs):
    pieces = refs[:count]
    wq_ref, wk_ref, wv_ref, cos_ref, sin_ref, q_ref, k_ref, v_ref = refs[count:]
    at = 0
    for piece in pieces:
        rows = piece.shape[0]
        x = piece[...]
        cosine = cos_ref[at : at + rows, :]
        sine = sin_ref[at : at + rows, :]
        for w_ref, o_ref in ((wq_ref, q_ref), (wk_ref, k_ref)):
            mixed = dot(x, w_ref[...])
            for h in range(mixed.shape[1] // HD):
                v = mixed[:, h * HD : (h + 1) * HD]
                turned = v * cosine + pltpu.roll(v, HD // 2, 1) * sine
                o_ref[at : at + rows, h * HD : (h + 1) * HD] = turned.astype(BF)
        v_ref[at : at + rows, :] = dot(x, wv_ref[...]).astype(BF)
        at += rows


def attn_kernel(scale, q_ref, k_ref, v_ref, pre_ref, bias_ref, mine_ref, other_ref):
    width = q_ref.shape[1]
    nt = (((1,), (1,)), ((), ()))
    half = q_ref.shape[0] // 2
    for h in range(width // HD):
        cols = slice(h * HD, (h + 1) * HD)
        vcols = slice(width + h * HD, width + (h + 1) * HD)
        q = q_ref[:, cols]
        s1 = lax.dot_general(q, pre_ref[:, cols], nt, preferred_element_type=F32)
        s2 = lax.dot_general(q, k_ref[:, cols], nt, preferred_element_type=F32)
        s2 = s2 + bias_ref[...]
        top = jnp.maximum(
            jnp.max(s1, axis=-1, keepdims=True), jnp.max(s2, axis=-1, keepdims=True)
        )
        e1 = jnp.exp2((s1 - top) * scale)
        e2 = jnp.exp2((s2 - top) * scale)
        total = jnp.sum(e1, axis=-1, keepdims=True) + jnp.sum(e2, axis=-1, keepdims=True)
        o = dot(e1.astype(BF), pre_ref[:, vcols]) + dot(e2.astype(BF), v_ref[:, cols])
        o = (o / total).astype(BF)
        mine_ref[:, cols] = o[:half]
        other_ref[:, cols] = o[half:]


def proj_kernel(a_ref, b_ref, wa_ref, wb_ref, own_ref, *outs):
    total = dot(a_ref[...], wa_ref[...]) + dot(b_ref[...], wb_ref[...])
    rows = own_ref.shape[0]
    own_ref[...] = total[:rows]
    at = rows
    for o_ref in outs:
        n = o_ref.shape[0]
        o_ref[...] = total[at : at + n].astype(BF)
        at += n


def pack(o_ref, scratch, main, extra):
    width = main.shape[1]
    part = width // SUB
    blocks = extra.shape[0]
    o_ref[:, :width] = main.astype(BF)
    for b in range(SUB):
        piece = extra[:, b * part : (b + 1) * part]
        for i in range(part // 128):
            scratch[i, pl.ds(b, blocks, stride=SUB), :] = piece[:, i * 128 : (i + 1) * 128]
    for i in range(part // 128):
        o_ref[:, width + i * 128 : width + (i + 1) * 128] = scratch[i].astype(BF)


def unpack_extra(x_ref, scratch, width):
    part = width // SUB
    blocks = x_ref.shape[0] // SUB
    for i in range(part // 128):
        scratch[i] = x_ref[:, width + i * 128 : width + (i + 1) * 128].astype(F32)
    parts = []
    for b in range(SUB):
        for i in range(part // 128):
            parts.append(scratch[i, pl.ds(b, blocks, stride=SUB), :])
    return jnp.concatenate(parts, axis=1).astype(BF)


def dispatch_kernel(t_ref, own_ref, b1_ref, b2_ref, g_ref, d_ref, h_ref, n_ref, o_ref, scratch):
    attn_out = own_ref[...] + b1_ref[...].astype(F32) + b2_ref[...].astype(F32)
    hidden = (t_ref[...].astype(F32) + attn_out).astype(BF)
    h_ref[...] = hidden
    normed = rms(hidden.astype(F32), g_ref[...]).astype(BF)
    n_ref[...] = normed
    wide = o_ref.shape[0]
    pack(o_ref, scratch, dot(d_ref[:wide, :], normed), dot(d_ref[wide:, :], normed))


def dispatch2_kernel(n_ref, d_ref, o_ref, scratch):
    normed = n_ref[...]
    wide = o_ref.shape[0]
    pack(o_ref, scratch, dot(d_ref[:wide, :], normed), dot(d_ref[wide:, :], normed))


def ffn_kernel(x_ref, g0, u0, d0, g1, u1, d1, o_ref, rows_ref, total, scratch):
    j = pl.program_id(0)
    width = g0.shape[0]
    wide = x_ref.shape[0]

    @pl.when(j == 0)
    def _():
        rows_ref[:wide, :] = x_ref[:, :width]
        rows_ref[wide:, :] = unpack_extra(x_ref, scratch, width)
        total[...] = jnp.zeros_like(total)

    def half(g_ref, u_ref, d_ref):
        x = rows_ref[...]
        gate = dot(x, g_ref[...])
        upper = dot(x, u_ref[...])
        act = (gate / (1.0 + jnp.exp(-gate)) * upper).astype(BF)
        total[...] += dot(act, d_ref[...])

    steps = pl.num_programs(0)

    @pl.when(j < steps // 2)
    def _():
        half(g0, u0, d0)

    @pl.when(j >= steps // 2)
    def _():
        half(g1, u1, d1)

    @pl.when(j == steps - 1)
    def _():
        pack(o_ref, scratch, total[:wide, :], total[wide:, :])


def ffn(x, w0, w1):
    wide, packed = x.shape
    width = w0[0].shape[0]
    hidden = w0[0].shape[1]
    block = 256
    steps = hidden // block
    rows = wide + wide // SUB
    first = lambda j: jnp.minimum(j, steps - 1)
    second = lambda j: jnp.maximum(j - steps, 0)
    col = lambda f: pl.BlockSpec((width, block), lambda j: (0, f(j)))
    row = lambda f: pl.BlockSpec((block, width), lambda j: (f(j), 0))
    return pl.pallas_call(
        ffn_kernel,
        grid=(2 * steps,),
        out_shape=shape((wide, packed), BF),
        in_specs=[
            pl.BlockSpec((wide, packed), lambda j: (0, 0)),
            col(first), col(first), row(first), col(second), col(second), row(second),
        ],
        out_specs=pl.BlockSpec((wide, packed), lambda j: (0, 0)),
        scratch_shapes=[
            pltpu.VMEM((rows, width), BF),
            pltpu.VMEM((rows, width), F32),
            pltpu.VMEM((width // SUB // 128, wide, 128), F32),
        ],
        name="ffn",
    )(x, *w0, *w1)


def weighted(r_ref, scratch, wm_ref, wx_ref, width):
    main = dot(wm_ref[...], r_ref[:, :width])
    extra = dot(wx_ref[...], unpack_extra(r_ref, scratch, width))
    both = main + extra
    rows = both.shape[0] // 2
    return both[:rows] + both[rows:]


def combine_kernel(r_ref, wm_ref, wx_ref, o_ref, scratch):
    o_ref[...] = weighted(r_ref, scratch, wm_ref, wx_ref, o_ref.shape[1])


def combine2_kernel(live_ref, r_ref, wm_ref, wx_ref, part_ref, h_ref, o_ref, scratch):
    moe = part_ref[...] + weighted(r_ref, scratch, wm_ref, wx_ref, o_ref.shape[1])
    out = h_ref[...].astype(F32) + moe
    row = lax.broadcasted_iota(jnp.int32, out.shape, 0)
    o_ref[...] = jnp.where(row < live_ref[0], out, 0.0).astype(BF)


def on_device(
    tokens, attn_gain, w_query, w_key, w_value, w_out, prefix_cache, group_of, lengths,
    moe_gain, w_gate, w_up, w_down, routes, route_weights,
):
    rows, width = tokens.shape
    zs = lax.axis_size("z")
    reqs = lax.axis_size("x") * lax.axis_size("y")
    experts = reqs * zs
    z = lax.axis_index("z")
    core = lax.axis_index("c")
    req = lax.axis_index("x") * lax.axis_size("y") + lax.axis_index("y")
    local = w_query.shape[1]
    up = [(i, (i + 1) % zs) for i in range(zs)]
    down = [(i, (i - 1) % zs) for i in range(zs)]
    swap = lambda v: lax.ppermute(v, "c", [(0, 1), (1, 0)])
    to_up = lambda v: lax.ppermute(v, "z", up)
    to_down = lambda v: lax.ppermute(v, "z", down)
    half = rows // 2

    normed = call(norm_kernel, shape((rows, width), BF), 2, name="norm")(tokens, attn_gain[None])
    from_low = to_up(normed)
    from_high = to_down(normed)
    own_b = swap(normed)
    far_lo = to_up(from_low[:half])
    far_hi = to_down(from_high[half:])
    low_b = swap(from_low)
    high_b = swap(from_high)
    far_lo_b = swap(far_lo)
    far_hi_b = swap(far_hi)

    group_spec = pltpu.PrefetchScalarGridSpec(
        num_scalar_prefetch=1,
        grid=(reqs,),
        in_specs=[pl.BlockSpec((1,) + prefix_cache.shape[1:], lambda r, g: (g[r], 0, 0, 0))],
        out_specs=pl.BlockSpec((prefix_cache.shape[1], 2 * local), lambda r, g: (r, 0)),
    )
    outgoing = pl.pallas_call(
        prefix_kernel,
        grid_spec=group_spec,
        out_shape=shape((reqs * prefix_cache.shape[1], 2 * local), BF),
        name="prefix",
    )(group_of, prefix_cache)
    prefix = lax.all_to_all(outgoing, ("x", "y"), split_axis=0, concat_axis=0, tiled=True)

    own_w = (w_gate[0], w_up[0], w_down[0])
    other_w = tuple(swap(w) for w in own_w)
    out_b = swap(w_out)

    wide = experts * SUB
    per = wide + experts
    table, weights_main, weights_extra = call(
        route_kernel,
        (
            shape((2 * per, rows), BF),
            shape((2 * rows, 2 * wide), BF),
            shape((2, 2 * rows, experts), BF),
        ),
        3,
        name="route",
    )(routes, routes.T, route_weights)

    chip = jnp.array([0, zs - 1, 1, 2], jnp.int32)
    chips = (z + chip) % zs
    place = (
        (chips[:, None] * 2 + jnp.stack([core, 1 - core])[None, :])[:, :, None] * rows
        + jnp.arange(rows, dtype=jnp.int32)
    ).reshape(-1)
    spots = (PREFIX + place).astype(F32)
    freqs = 10000.0 ** (-(jnp.arange(HD // 2, dtype=F32) * 2.0) / HD)
    angles = spots[:, None] * freqs[None, :]
    cosine = jnp.cos(angles)
    sine = jnp.sin(angles)
    cosine = jnp.concatenate([cosine, cosine], axis=1)
    sine = jnp.concatenate([-sine, sine], axis=1)
    length = lengths[req]
    bias = jnp.where(place < length, 0.0, -1e30)[None, :]

    slots = rows * 2 * zs
    pieces = (
        normed, own_b, from_low, low_b, from_high, high_b, far_lo, far_hi, far_lo_b, far_hi_b,
    )
    query, key, value = call(
        lambda *refs: qkv_kernel(len(pieces), *refs),
        tuple(shape((slots, local), BF) for _ in range(3)),
        len(pieces) + 5,
        name="qkv",
    )(*pieces, w_query, w_key, w_value, cosine, sine)

    chunk = 2 * rows
    whole = lambda a: pl.BlockSpec(a.shape, lambda i: (0, 0))
    scale = math.log2(math.e) / math.sqrt(HD)
    mine, other = pl.pallas_call(
        lambda *refs: attn_kernel(scale, *refs),
        grid=(zs,),
        out_shape=(shape((slots // 2, local), BF),) * 2,
        in_specs=[
            pl.BlockSpec((chunk, local), lambda i: (i, 0)),
            whole(key), whole(value), whole(prefix), whole(bias),
        ],
        out_specs=(pl.BlockSpec((rows, local), lambda i: (i, 0)),) * 2,
        name="attn",
    )(query, key, value, prefix, bias)

    other = swap(other)
    own, to_low, to_high, far1, far2 = call(
        proj_kernel,
        (
            shape((rows, width), F32), shape((rows, width), BF), shape((rows, width), BF),
            shape((half, width), BF), shape((half, width), BF),
        ),
        4,
        name="proj",
    )(mine, other, w_out, out_b)
    got1 = to_up(far1).astype(F32)
    got2 = to_down(far2).astype(F32)
    to_high = jnp.concatenate(
        [(to_high[:half].astype(F32) + got1).astype(BF), to_high[half:]], axis=0
    )
    to_low = jnp.concatenate(
        [to_low[:half], (to_low[half:].astype(F32) + got2).astype(BF)], axis=0
    )
    b1 = to_up(to_high)
    b2 = to_down(to_low)

    packed = width + width // SUB
    scratch = [pltpu.VMEM((width // SUB // 128, wide, 128), F32)]
    hidden, normed2, send0 = call(
        dispatch_kernel,
        (shape((rows, width), BF), shape((rows, width), BF), shape((wide, packed), BF)),
        6,
        scratch_shapes=scratch,
        name="dispatch0",
    )(tokens, own, b1, b2, moe_gain[None], table[:per])
    send1 = call(
        dispatch2_kernel, shape((wide, packed), BF), 2, scratch_shapes=scratch, name="dispatch1"
    )(normed2, table[per:])

    def exchange(v):
        return lax.all_to_all(
            v.reshape(experts, SUB, packed), ("x", "y", "z"), 0, 0, tiled=True
        ).reshape(wide, packed)

    back0 = exchange(ffn(exchange(send0), own_w, other_w))
    back1 = exchange(ffn(exchange(send1), own_w, other_w))

    part = call(
        combine_kernel, shape((rows, width), F32), 3, scratch_shapes=scratch, name="combine0"
    )(back0, weights_main[:, :wide], weights_extra[0])
    live = jnp.clip(length - (z * 2 + core) * rows, 0, rows).astype(jnp.int32)[None]
    return pl.pallas_call(
        combine2_kernel,
        out_shape=shape((rows, width), BF),
        in_specs=[pl.BlockSpec(memory_space=pltpu.SMEM)] + [vmem()] * 5,
        out_specs=vmem(),
        scratch_shapes=scratch,
        name="combine1",
    )(live, back1, weights_main[:, wide:], weights_extra[1], part, hidden)


def solution(mesh):
    side = math.isqrt(mesh.shape["req"])
    grid = Mesh(
        mesh.devices.reshape(side, side, mesh.shape["exp"] // 2, 2), ("x", "y", "z", "c")
    )
    req, exp = ("x", "y"), ("z", "c")
    every = req + exp
    return jax.shard_map(
        on_device,
        mesh=grid,
        in_specs=(
            P(every, None), P(), P(None, exp), P(None, exp), P(None, exp), P(exp, None),
            P(None, req, None, exp), P(), P(), P(),
            P(every, None, None), P(every, None, None), P(every, None, None),
            P(every, None), P(every, None),
        ),
        out_specs=P(every, None),
        check_vma=False,
    )
```

```python
import functools
import math

import jax
import jax.numpy as jnp
import numpy as np
from jax import lax
from jax.experimental import pallas as pl
from jax.experimental.pallas import tpu as pltpu
from jax.sharding import Mesh
from jax.sharding import PartitionSpec as P

HD = 128
PREFIX = 1024
BF = jnp.bfloat16
F32 = jnp.float32
SUB = 8


def vmem():
    return pl.BlockSpec(memory_space=pltpu.VMEM)


def call(kernel, out_shape, n_in, **kw):
    outs = jax.tree.map(lambda _: vmem(), out_shape)
    return pl.pallas_call(
        kernel, out_shape=out_shape, in_specs=[vmem()] * n_in, out_specs=outs, **kw
    )


def shape(dims, dtype):
    return jax.ShapeDtypeStruct(dims, dtype)


def dot(a, b):
    return jnp.dot(a, b, preferred_element_type=F32)


def rms(wide, gain):
    return wide * lax.rsqrt(jnp.mean(wide * wide, axis=-1, keepdims=True) + 1e-05) * gain


def norm_kernel(x_ref, g_ref, o_ref):
    o_ref[...] = rms(x_ref[...].astype(F32), g_ref[...]).astype(BF)


def route_kernel(r_ref, rt_ref, w_ref, dt0_ref, dt1_ref, wm0_ref, wx0_ref, wm1_ref, wx1_ref):
    rows, top = r_ref.shape
    experts = dt0_ref.shape[0] // (SUB + 1)
    wide = experts * SUB
    row_i = lax.broadcasted_iota(jnp.int32, (rows, rows), 0)
    col_i = lax.broadcasted_iota(jnp.int32, (rows, rows), 1)
    e_t = lax.broadcasted_iota(jnp.int32, (experts, rows), 0)
    named_t = jnp.zeros((experts, rows), F32)
    for k in range(top):
        named_t += jnp.where(rt_ref[k : k + 1, :] == e_t, 1.0, 0.0)
    rank_t = dot(named_t.astype(BF), jnp.where(row_i < col_i, 1.0, 0.0).astype(BF))
    rank_t = jnp.where(named_t > 0.5, rank_t, -1.0)
    j_t = lax.broadcasted_iota(jnp.int32, (wide, experts), 0)
    spread_t = jnp.where(
        j_t // SUB == lax.broadcasted_iota(jnp.int32, (wide, experts), 1), 1.0, 0.0
    ).astype(BF)
    big_t = dot(spread_t, rank_t.astype(BF))
    slot_t = (lax.broadcasted_iota(jnp.int32, (wide, rows), 0) % SUB).astype(F32)
    for c, dt_ref in enumerate((dt0_ref, dt1_ref)):
        first = float(c * (SUB + 1))
        dt_ref[:wide, :] = jnp.where(big_t == slot_t + first, 1.0, 0.0).astype(BF)
        dt_ref[wide:, :] = jnp.where(rank_t == first + SUB, 1.0, 0.0).astype(BF)
    e_n = lax.broadcasted_iota(jnp.int32, (rows, experts), 1)
    named = jnp.zeros((rows, experts), F32)
    weight = jnp.zeros((rows, experts), F32)
    for k in range(top):
        hit = r_ref[:, k : k + 1] == e_n
        named += jnp.where(hit, 1.0, 0.0)
        weight += jnp.where(hit, w_ref[:, k : k + 1], 0.0)
    rank = dot(jnp.where(col_i < row_i, 1.0, 0.0).astype(BF), named.astype(BF))
    rank = jnp.where(named > 0.5, rank, -1.0)
    high = weight.astype(BF)
    low = (weight - high.astype(F32)).astype(BF)
    j_n = lax.broadcasted_iota(jnp.int32, (experts, wide), 1)
    spread = jnp.where(
        j_n // SUB == lax.broadcasted_iota(jnp.int32, (experts, wide), 0), 1.0, 0.0
    ).astype(BF)
    big = dot(rank.astype(BF), spread)
    big_high = dot(high, spread)
    big_low = dot(low, spread)
    slot = (lax.broadcasted_iota(jnp.int32, (rows, wide), 1) % SUB).astype(F32)
    for c, (wm_ref, wx_ref) in enumerate(((wm0_ref, wx0_ref), (wm1_ref, wx1_ref))):
        first = float(c * (SUB + 1))
        hit = big == slot + first
        wm_ref[:rows, :] = jnp.where(hit, big_high, 0.0).astype(BF)
        wm_ref[rows:, :] = jnp.where(hit, big_low, 0.0).astype(BF)
        hit = rank == first + SUB
        wx_ref[:rows, :] = jnp.where(hit, high.astype(F32), 0.0).astype(BF)
        wx_ref[rows:, :] = jnp.where(hit, low.astype(F32), 0.0).astype(BF)


def prefix_kernel(group_ref, x_ref, o_ref, sem):
    rows, width = x_ref.shape[2:]
    copies = []
    for r in range(o_ref.shape[0] // rows):
        for j in range(2):
            copies.append(
                pltpu.make_async_copy(
                    x_ref.at[group_ref[r], j],
                    o_ref.at[r * rows : (r + 1) * rows, j * width : (j + 1) * width],
                    sem.at[r, j],
                )
            )
    for copy in copies:
        copy.start()
    for copy in copies:
        copy.wait()


def qkv_kernel(count, *refs):
    pieces = refs[:count]
    wq, wk, wv = refs[count : count + 2], refs[count + 2 : count + 4], refs[count + 4 : count + 6]
    cos_ref, sin_ref, q_ref, k_ref, v_ref, x_ref = refs[count + 6 :]
    at = 0
    for piece in pieces:
        x_ref[at : at + piece.shape[0], :] = piece[...]
        at += piece.shape[0]
    local = wq[0].shape[1]
    for side in range(2):
        for w_ref, o_ref in ((wk[side], k_ref), (wq[side], q_ref)):
            rows = o_ref.shape[0]
            mixed = dot(x_ref[:rows, :], w_ref[...])
            for h in range(local // HD):
                v = mixed[:, h * HD : (h + 1) * HD]
                turned = v * cos_ref[:rows, :] + pltpu.roll(v, HD // 2, 1) * sin_ref[:rows, :]
                col = side * local + h * HD
                o_ref[:, col : col + HD] = turned.astype(BF)
        v_ref[:, side * local : (side + 1) * local] = dot(x_ref[...], wv[side][...]).astype(BF)


def attend(scale, q_ref, keys, values, pre_refs, bias_ref, o_ref):
    local = pre_refs[0].shape[1] // 2
    nt = (((1,), (1,)), ((), ()))
    for h in range(q_ref.shape[1] // HD):
        side, col = divmod(h * HD, local)
        pre_ref = pre_refs[side]
        cols = slice(h * HD, (h + 1) * HD)
        q = q_ref[:, cols]
        scores = [
            lax.dot_general(q, pre_ref[:, col : col + HD], nt, preferred_element_type=F32)
        ]
        at = 0
        for k_ref in keys:
            n = k_ref.shape[0]
            s = lax.dot_general(q, k_ref[:, cols], nt, preferred_element_type=F32)
            scores.append(s + bias_ref[:, at : at + n])
            at += n
        top = jnp.max(scores[0], axis=-1, keepdims=True)
        for s in scores[1:]:
            top = jnp.maximum(top, jnp.max(s, axis=-1, keepdims=True))
        raised = [jnp.exp2((s - top) * scale) for s in scores]
        total = sum(jnp.sum(e, axis=-1, keepdims=True) for e in raised)
        out = dot(raised[0].astype(BF), pre_ref[:, local + col : local + col + HD])
        for e, v_ref in zip(raised[1:], values):
            out += dot(e.astype(BF), v_ref[:, cols])
        o_ref[:, cols] = (out / total).astype(BF)


def project(a_ref, wa_ref, wb_ref):
    local = wa_ref.shape[0]
    return dot(a_ref[:, :local], wa_ref[...]) + dot(a_ref[:, local:], wb_ref[...])


def attn_far_kernel(scale, q, k0, k1, k2, v0, v1, v2, pa, pb, bias, wa, wb, o1, o2, tmp):
    attend(scale, q, (k0, k1, k2), (v0, v1, v2), (pa, pb), bias, tmp)
    total = project(tmp, wa, wb).astype(BF)
    rows = o1.shape[0]
    o1[...] = total[:rows]
    o2[...] = total[rows:]


def attn_near_kernel(scale, q, k0, k1, k2, v0, v1, v2, pa, pb, bias, o):
    attend(scale, q, (k0, k1, k2), (v0, v1, v2), (pa, pb), bias, o)


def attn_own_kernel(scale, q, k0, k1, k2, v0, v1, v2, pa, pb, bias, wa, wb, o, tmp):
    attend(scale, q, (k0, k1, k2), (v0, v1, v2), (pa, pb), bias, tmp)
    o[...] = project(tmp, wa, wb)


def proj_near_kernel(a_ref, wa, wb, got1, got2, low_ref, high_ref):
    total = project(a_ref, wa, wb)
    rows = low_ref.shape[0]
    half = rows // 2
    low_ref[:half, :] = total[:half].astype(BF)
    low_ref[half:, :] = (total[half:rows] + got2[...].astype(F32)).astype(BF)
    high_ref[:half, :] = (total[rows : rows + half] + got1[...].astype(F32)).astype(BF)
    high_ref[half:, :] = total[rows + half :].astype(BF)


def pack(o_ref, scratch, main, extra):
    width = main.shape[1]
    part = width // SUB
    blocks = extra.shape[0]
    o_ref[:, :width] = main.astype(BF)
    for b in range(SUB):
        piece = extra[:, b * part : (b + 1) * part]
        for i in range(part // 128):
            scratch[i, pl.ds(b, blocks, stride=SUB), :] = piece[:, i * 128 : (i + 1) * 128]
    for i in range(part // 128):
        o_ref[:, width + i * 128 : width + (i + 1) * 128] = scratch[i].astype(BF)


def unpack_extra(x_ref, scratch, width):
    part = width // SUB
    blocks = x_ref.shape[0] // SUB
    for i in range(part // 128):
        scratch[i] = x_ref[:, width + i * 128 : width + (i + 1) * 128].astype(F32)
    parts = []
    for b in range(SUB):
        for i in range(part // 128):
            parts.append(scratch[i, pl.ds(b, blocks, stride=SUB), :])
    return jnp.concatenate(parts, axis=1).astype(BF)


def dispatch_kernel(t_ref, own_ref, b1_ref, b2_ref, g_ref, d_ref, h_ref, n_ref, o_ref, scratch):
    attn_out = own_ref[...] + b1_ref[...].astype(F32) + b2_ref[...].astype(F32)
    hidden = (t_ref[...].astype(F32) + attn_out).astype(BF)
    h_ref[...] = hidden
    normed = rms(hidden.astype(F32), g_ref[...]).astype(BF)
    n_ref[...] = normed
    wide = o_ref.shape[0]
    pack(o_ref, scratch, dot(d_ref[:wide, :], normed), dot(d_ref[wide:, :], normed))


def dispatch2_kernel(n_ref, d_ref, o_ref, scratch):
    normed = n_ref[...]
    wide = o_ref.shape[0]
    pack(o_ref, scratch, dot(d_ref[:wide, :], normed), dot(d_ref[wide:, :], normed))


def ffn_kernel(x_ref, g0, u0, d0, g1, u1, d1, o_ref, rows_ref, total, scratch):
    j = pl.program_id(0)
    width = g0.shape[0]
    wide = x_ref.shape[0]

    @pl.when(j == 0)
    def _():
        rows_ref[:wide, :] = x_ref[:, :width]
        rows_ref[wide:, :] = unpack_extra(x_ref, scratch, width)
        total[...] = jnp.zeros_like(total)

    def half(g_ref, u_ref, d_ref):
        x = rows_ref[...]
        gate = dot(x, g_ref[...])
        upper = dot(x, u_ref[...])
        act = (gate / (1.0 + jnp.exp(-gate)) * upper).astype(BF)
        total[...] += dot(act, d_ref[...])

    steps = pl.num_programs(0)

    @pl.when(j < steps // 2)
    def _():
        half(g0, u0, d0)

    @pl.when(j >= steps // 2)
    def _():
        half(g1, u1, d1)

    @pl.when(j == steps - 1)
    def _():
        pack(o_ref, scratch, total[:wide, :], total[wide:, :])


def ffn(x, w0, w1):
    wide, packed = x.shape
    width = w0[0].shape[0]
    hidden = w0[0].shape[1]
    block = 256
    steps = hidden // block
    rows = wide + wide // SUB
    first = lambda j: jnp.minimum(j, steps - 1)
    second = lambda j: jnp.maximum(j - steps, 0)
    col = lambda f: pl.BlockSpec((width, block), lambda j: (0, f(j)))
    row = lambda f: pl.BlockSpec((block, width), lambda j: (f(j), 0))
    return pl.pallas_call(
        ffn_kernel,
        grid=(2 * steps,),
        out_shape=shape((wide, packed), BF),
        in_specs=[
            pl.BlockSpec((wide, packed), lambda j: (0, 0)),
            col(first), col(first), row(first), col(second), col(second), row(second),
        ],
        out_specs=pl.BlockSpec((wide, packed), lambda j: (0, 0)),
        scratch_shapes=[
            pltpu.VMEM((rows, width), BF),
            pltpu.VMEM((rows, width), F32),
            pltpu.VMEM((width // SUB // 128, wide, 128), F32),
        ],
        name="ffn",
    )(x, *w0, *w1)


def weighted(r_ref, scratch, wm_ref, wx_ref, width):
    main = dot(wm_ref[...], r_ref[:, :width])
    extra = dot(wx_ref[...], unpack_extra(r_ref, scratch, width))
    both = main + extra
    rows = both.shape[0] // 2
    return both[:rows] + both[rows:]


def combine_kernel(r_ref, wm_ref, wx_ref, o_ref, scratch):
    o_ref[...] = weighted(r_ref, scratch, wm_ref, wx_ref, o_ref.shape[1])


def combine2_kernel(live_ref, r_ref, wm_ref, wx_ref, part_ref, h_ref, o_ref, scratch):
    moe = part_ref[...] + weighted(r_ref, scratch, wm_ref, wx_ref, o_ref.shape[1])
    out = h_ref[...].astype(F32) + moe
    row = lax.broadcasted_iota(jnp.int32, out.shape, 0)
    o_ref[...] = jnp.where(row < live_ref[0], out, 0.0).astype(BF)


def on_device(
    tokens, attn_gain, w_query, w_key, w_value, w_out, prefix_cache, group_of, lengths,
    moe_gain, w_gate, w_up, w_down, routes, route_weights,
):
    rows, width = tokens.shape
    zs = lax.axis_size("z")
    reqs = lax.axis_size("x") * lax.axis_size("y")
    experts = reqs * zs
    z = lax.axis_index("z")
    core = lax.axis_index("c")
    req = lax.axis_index("x") * lax.axis_size("y") + lax.axis_index("y")
    local = w_query.shape[1]
    up = [(i, (i + 1) % zs) for i in range(zs)]
    down = [(i, (i - 1) % zs) for i in range(zs)]
    swap = lambda v: lax.ppermute(v, "c", [(0, 1), (1, 0)])
    to_up = lambda v: lax.ppermute(v, "z", up)
    to_down = lambda v: lax.ppermute(v, "z", down)
    half = rows // 2

    normed = call(norm_kernel, shape((rows, width), BF), 2, name="norm")(tokens, attn_gain[None])
    normed, prefix_cache = lax.optimization_barrier((normed, prefix_cache))
    from_low = to_up(normed)
    from_high = to_down(normed)
    own_b = swap(normed)
    far_lo = to_up(from_low[:half])
    far_hi = to_down(from_high[half:])
    low_b = swap(from_low)
    high_b = swap(from_high)

    out_b = swap(w_out)
    wq = (w_query, swap(w_query))
    wk = (w_key, swap(w_key))
    wv = (w_value, swap(w_value))

    spread = prefix_cache.shape[1]
    outgoing = pl.pallas_call(
        prefix_kernel,
        out_shape=shape((reqs * spread, 2 * local), BF),
        in_specs=[pl.BlockSpec(memory_space=pltpu.SMEM), pl.BlockSpec(memory_space=pltpu.HBM)],
        out_specs=pl.BlockSpec(memory_space=pltpu.HBM),
        scratch_shapes=[pltpu.SemaphoreType.DMA((reqs, 2))],
        name="prefix",
    )(group_of, jnp.transpose(prefix_cache, (0, 2, 1, 3)))
    pre_a = lax.all_to_all(outgoing, ("x", "y"), split_axis=0, concat_axis=0, tiled=True)
    pre_b = swap(pre_a)

    own_w = (w_gate[0], w_up[0], w_down[0])
    other_w = tuple(swap(w) for w in own_w)

    wide = experts * SUB
    per = wide + experts
    *tables, wm0, wx0, wm1, wx1 = call(
        route_kernel,
        [shape((per, rows), BF)] * 2
        + [shape((2 * rows, wide), BF), shape((2 * rows, experts), BF)] * 2,
        3,
        name="route",
    )(routes, routes.T, route_weights)

    mine, yours = core * rows, (1 - core) * rows
    z_low, z_high, z_far = (z + zs - 1) % zs, (z + 1) % zs, (z + 2) % zs
    starts = jnp.stack(
        [
            z * 2 * rows + mine, z * 2 * rows + yours,
            z_low * 2 * rows + mine, z_high * 2 * rows + mine,
            z_low * 2 * rows + yours, z_high * 2 * rows + yours,
            z_far * 2 * rows + mine, z_far * 2 * rows + yours,
        ]
    )
    place = (starts[:, None] + jnp.arange(rows, dtype=jnp.int32)).reshape(-1)
    spots = (PREFIX + place).astype(F32)
    freqs = 10000.0 ** (-(jnp.arange(HD // 2, dtype=F32) * 2.0) / HD)
    angles = spots[:, None] * freqs[None, :]
    cosine = jnp.cos(angles)
    sine = jnp.sin(angles)
    cosine = jnp.concatenate([cosine, cosine], axis=1)
    sine = jnp.concatenate([-sine, sine], axis=1)
    length = lengths[req]
    bias = jnp.where(place < length, 0.0, -1e30)[None, :]

    def projections(pieces, first, count, name):
        return call(
            lambda *refs: qkv_kernel(len(pieces), *refs),
            (
                shape((count // 2, 2 * local), BF),
                shape((count, 2 * local), BF),
                shape((count, 2 * local), BF),
            ),
            len(pieces) + 8,
            scratch_shapes=[pltpu.VMEM((count, width), BF)],
            name=name,
        )(*pieces, *wq, *wk, *wv, cosine[first : first + count], sine[first : first + count])

    q0, k0, v0 = projections((normed, own_b), 0, 2 * rows, "qkv_own")
    low_b, high_b, k0 = lax.optimization_barrier((low_b, high_b, k0))
    q1, k1, v1 = projections((from_low, from_high, low_b, high_b), 2 * rows, 4 * rows, "qkv_near")
    far_lo, far_hi, k1 = lax.optimization_barrier((far_lo, far_hi, k1))
    far_lo_b = swap(far_lo)
    far_hi_b = swap(far_hi)
    q2, k2, v2 = projections((far_lo, far_hi, far_lo_b, far_hi_b), 6 * rows, 2 * rows, "qkv_far")
    cache = (k0, k1, k2, v0, v1, v2, pre_a, pre_b, bias)
    scale = math.log2(math.e) / math.sqrt(HD)
    tmp = [pltpu.VMEM((rows, 2 * local), BF)]

    far1, far2 = call(
        functools.partial(attn_far_kernel, scale),
        [shape((half, width), BF)] * 2,
        12,
        scratch_shapes=tmp,
        name="attn_far",
    )(q2, *cache, w_out, out_b)
    got1 = to_up(far1)
    got2 = to_down(far2)
    near = call(
        functools.partial(attn_near_kernel, scale), shape((2 * rows, 2 * local), BF), 10,
        name="attn_near",
    )(q1, *cache)
    to_low, to_high = call(
        proj_near_kernel, [shape((rows, width), BF)] * 2, 5, name="proj_near"
    )(near, w_out, out_b, got1, got2)
    to_low, to_high, q0 = lax.optimization_barrier((to_low, to_high, q0))
    b1 = to_up(to_high)
    b2 = to_down(to_low)
    own = call(
        functools.partial(attn_own_kernel, scale),
        shape((rows, width), F32),
        12,
        scratch_shapes=tmp,
        name="attn_own",
    )(q0, *cache, w_out, out_b)
    own, other_w = lax.optimization_barrier((own, other_w))

    packed = width + width // SUB
    scratch = [pltpu.VMEM((width // SUB // 128, wide, 128), F32)]
    hidden, normed2, send0 = call(
        dispatch_kernel,
        (shape((rows, width), BF), shape((rows, width), BF), shape((wide, packed), BF)),
        6,
        scratch_shapes=scratch,
        name="dispatch0",
    )(tokens, own, b1, b2, moe_gain[None], tables[0])
    send1 = call(
        dispatch2_kernel, shape((wide, packed), BF), 2, scratch_shapes=scratch, name="dispatch1"
    )(normed2, tables[1])

    def exchange(v):
        return lax.all_to_all(
            v.reshape(experts, SUB, packed), ("x", "y", "z"), 0, 0, tiled=True
        ).reshape(wide, packed)

    back0 = exchange(ffn(exchange(send0), own_w, other_w))
    back1 = exchange(ffn(exchange(send1), own_w, other_w))

    part = call(
        combine_kernel, shape((rows, width), F32), 3, scratch_shapes=scratch, name="combine0"
    )(back0, wm0, wx0)
    live = jnp.clip(length - (z * 2 + core) * rows, 0, rows).astype(jnp.int32)[None]
    return pl.pallas_call(
        combine2_kernel,
        out_shape=shape((rows, width), BF),
        in_specs=[pl.BlockSpec(memory_space=pltpu.SMEM)] + [vmem()] * 5,
        out_specs=vmem(),
        scratch_shapes=scratch,
        name="combine1",
    )(live, back1, wm1, wx1, part, hidden)


def solution(mesh):
    side = math.isqrt(mesh.shape["req"])
    grid = Mesh(
        mesh.devices.reshape(side, side, mesh.shape["exp"] // 2, 2), ("x", "y", "z", "c")
    )
    req, exp = ("x", "y"), ("z", "c")
    every = req + exp
    return jax.shard_map(
        on_device,
        mesh=grid,
        in_specs=(
            P(every, None), P(), P(None, exp), P(None, exp), P(None, exp), P(exp, None),
            P(None, req, None, exp), P(), P(), P(),
            P(every, None, None), P(every, None, None), P(every, None, None),
            P(every, None), P(every, None),
        ),
        out_specs=P(every, None),
        check_vma=False,
    )
```

```python
import functools
import math

import jax
import jax.numpy as jnp
from jax import lax
from jax.experimental import pallas as pl
from jax.experimental.pallas import tpu as pltpu
from jax.sharding import Mesh
from jax.sharding import PartitionSpec as P


HD = 128
PREFIX = 1024
BF = jnp.bfloat16
F32 = jnp.float32
SUB = 8


def vmem():
    return pl.BlockSpec(memory_space=pltpu.VMEM)


def limit(mib):
    return pltpu.CompilerParams(vmem_limit_bytes=mib << 20)


def call(kernel, out_shape, n_in, mib=16, **kw):
    outs = jax.tree.map(lambda _: vmem(), out_shape)
    return pl.pallas_call(
        kernel, out_shape=out_shape, in_specs=[vmem()] * n_in, out_specs=outs,
        compiler_params=limit(mib), **kw
    )


def shape(dims, dtype):
    return jax.ShapeDtypeStruct(dims, dtype)


def dot(a, b):
    return jnp.dot(a, b, preferred_element_type=F32)


def rms(wide, gain):
    return wide * lax.rsqrt(jnp.mean(wide * wide, axis=-1, keepdims=True) + 1e-05) * gain


def norm_kernel(x_ref, g_ref, o_ref, first_ref, last_ref):
    normed = rms(x_ref[...].astype(F32), g_ref[...]).astype(BF)
    o_ref[...] = normed
    half = first_ref.shape[0]
    first_ref[...] = normed[:half]
    last_ref[...] = normed[half:]


def slots_of(index):
    block = index // SUB
    return block // 2, (block % 2) * (SUB + 1) + index % SUB


def route_kernel(r_ref, rt_ref, w_ref, dt_ref, wm_ref, wx_ref):
    rows, top = r_ref.shape
    blocks = wx_ref.shape[1]
    experts = blocks // 2
    wide = blocks * SUB
    iota = lambda dims, axis: lax.broadcasted_iota(jnp.int32, dims, axis)
    one = lambda hit: jnp.where(hit, 1.0, 0.0)
    row_i = iota((rows, rows), 0)
    col_i = iota((rows, rows), 1)
    e_t = iota((experts, rows), 0)
    named_t = jnp.zeros((experts, rows), F32)
    for k in range(top):
        named_t += one(rt_ref[k : k + 1, :] == e_t)
    rank_t = dot(named_t.astype(BF), one(row_i < col_i).astype(BF))
    rank_t = jnp.where(named_t > 0.5, rank_t, -1.0).astype(BF)
    expert, _ = slots_of(iota((wide, experts), 0))
    spread = one(expert == iota((wide, experts), 1)).astype(BF)
    _, slot = slots_of(iota((wide, rows), 0))
    dt_ref[:wide, :] = one(dot(spread, rank_t) == slot.astype(F32)).astype(BF)
    block = iota((blocks, experts), 0)
    spread = one(block // 2 == iota((blocks, experts), 1)).astype(BF)
    slot = (iota((blocks, rows), 0) % 2) * (SUB + 1) + SUB
    dt_ref[wide:, :] = one(dot(spread, rank_t) == slot.astype(F32)).astype(BF)
    e_n = iota((rows, experts), 1)
    named = jnp.zeros((rows, experts), F32)
    weight = jnp.zeros((rows, experts), F32)
    for k in range(top):
        hit = r_ref[:, k : k + 1] == e_n
        named += one(hit)
        weight += jnp.where(hit, w_ref[:, k : k + 1], 0.0)
    rank = dot(one(col_i < row_i).astype(BF), named.astype(BF))
    rank = jnp.where(named > 0.5, rank, -1.0).astype(BF)
    high = weight.astype(BF)
    low = (weight - high.astype(F32)).astype(BF)
    expert, _ = slots_of(iota((experts, wide), 1))
    spread = one(expert == iota((experts, wide), 0)).astype(BF)
    _, slot = slots_of(iota((rows, wide), 1))
    hit = dot(rank, spread) == slot.astype(F32)
    wm_ref[:rows, :] = jnp.where(hit, dot(high, spread), 0.0).astype(BF)
    wm_ref[rows:, :] = jnp.where(hit, dot(low, spread), 0.0).astype(BF)
    block = iota((experts, blocks), 1)
    spread = one(block // 2 == iota((experts, blocks), 0)).astype(BF)
    slot = (iota((rows, blocks), 1) % 2) * (SUB + 1) + SUB
    hit = dot(rank, spread) == slot.astype(F32)
    wx_ref[:rows, :] = jnp.where(hit, dot(high, spread), 0.0).astype(BF)
    wx_ref[rows:, :] = jnp.where(hit, dot(low, spread), 0.0).astype(BF)


def prefix_kernel(group_ref, x_ref, o_ref):
    rows, width = x_ref.shape[2:]
    for r in range(o_ref.shape[0] // rows):
        for j in range(2):
            o_ref[r * rows : (r + 1) * rows, j * width : (j + 1) * width] = x_ref[group_ref[r], j]


def qkv_kernel(count, *refs):
    pieces = refs[:count]
    wq, wk, wv = refs[count : count + 2], refs[count + 2 : count + 4], refs[count + 4 : count + 6]
    cos_ref, sin_ref, q_ref, k_ref, v_ref, x_ref = refs[count + 6 :]
    at = 0
    for piece in pieces:
        x_ref[at : at + piece.shape[0], :] = piece[...]
        at += piece.shape[0]
    local = wq[0].shape[1]
    for side in range(2):
        for w_ref, o_ref in ((wk[side], k_ref), (wq[side], q_ref)):
            rows = o_ref.shape[0]
            mixed = dot(x_ref[:rows, :], w_ref[...])
            for h in range(local // HD):
                v = mixed[:, h * HD : (h + 1) * HD]
                turned = v * cos_ref[:rows, :] + pltpu.roll(v, HD // 2, 1) * sin_ref[:rows, :]
                col = side * local + h * HD
                o_ref[:, col : col + HD] = turned.astype(BF)
        v_ref[:, side * local : (side + 1) * local] = dot(x_ref[...], wv[side][...]).astype(BF)


def attend(scale, q_ref, keys, values, pre_refs, bias_ref, o_ref):
    local = pre_refs[0].shape[1] // 2
    nt = (((1,), (1,)), ((), ()))
    for h in range(q_ref.shape[1] // HD):
        side, col = divmod(h * HD, local)
        pre_ref = pre_refs[side]
        cols = slice(h * HD, (h + 1) * HD)
        q = q_ref[:, cols]
        scores = [
            lax.dot_general(q, pre_ref[:, col : col + HD], nt, preferred_element_type=F32)
        ]
        at = 0
        for k_ref in keys:
            n = k_ref.shape[0]
            s = lax.dot_general(q, k_ref[:, cols], nt, preferred_element_type=F32)
            scores.append(s + bias_ref[:, at : at + n])
            at += n
        top = jnp.max(scores[0], axis=-1, keepdims=True)
        for s in scores[1:]:
            top = jnp.maximum(top, jnp.max(s, axis=-1, keepdims=True))
        raised = [jnp.exp2((s - top) * scale) for s in scores]
        total = sum(jnp.sum(e, axis=-1, keepdims=True) for e in raised)
        out = dot(raised[0].astype(BF), pre_ref[:, local + col : local + col + HD])
        for e, v_ref in zip(raised[1:], values):
            out += dot(e.astype(BF), v_ref[:, cols])
        o_ref[:, cols] = (out / total).astype(BF)


def project(a_ref, wa_ref, wb_ref):
    local = wa_ref.shape[0]
    return dot(a_ref[:, :local], wa_ref[...]) + dot(a_ref[:, local:], wb_ref[...])


def attn_far_kernel(scale, q, k0, k1, k2, v0, v1, v2, pa, pb, bias, wa, wb, o1, o2, tmp):
    attend(scale, q, (k0, k1, k2), (v0, v1, v2), (pa, pb), bias, tmp)
    total = project(tmp, wa, wb).astype(BF)
    rows = o1.shape[0]
    o1[...] = total[:rows]
    o2[...] = total[rows:]


def attn_near_kernel(scale, q, k0, k1, k2, v0, v1, v2, pa, pb, bias, o):
    attend(scale, q, (k0, k1, k2), (v0, v1, v2), (pa, pb), bias, o)


def attn_own_kernel(scale, q, k0, k1, k2, v0, v1, v2, pa, pb, bias, wa, wb, o, tmp):
    attend(scale, q, (k0, k1, k2), (v0, v1, v2), (pa, pb), bias, tmp)
    o[...] = project(tmp, wa, wb)


def proj_near_kernel(a_ref, wa, wb, got1, got2, low_ref, high_ref):
    total = project(a_ref, wa, wb)
    rows = low_ref.shape[0]
    half = rows // 2
    low_ref[:half, :] = total[:half].astype(BF)
    low_ref[half:, :] = (total[half:rows] + got2[...].astype(F32)).astype(BF)
    high_ref[:half, :] = (total[rows : rows + half] + got1[...].astype(F32)).astype(BF)
    high_ref[half:, :] = total[rows + half :].astype(BF)


def dispatch_kernel(t_ref, own_ref, b1_ref, b2_ref, g_ref, d_ref, h_ref, o_ref, normed, extra):
    b = pl.program_id(0)
    part = o_ref.shape[1]
    wide = o_ref.shape[0]
    blocks = wide // SUB

    @pl.when(b == 0)
    def _():
        attn_out = own_ref[...] + b1_ref[...].astype(F32) + b2_ref[...].astype(F32)
        hidden = (t_ref[...].astype(F32) + attn_out).astype(BF)
        h_ref[...] = hidden
        rows = rms(hidden.astype(F32), g_ref[...]).astype(BF)
        for i in range(SUB):
            normed[i] = rows[:, i * part : (i + 1) * part]

    @pl.when(b < SUB)
    def _():
        x = normed[b]
        o_ref[...] = dot(d_ref[:wide, :], x).astype(BF)
        more = dot(d_ref[wide:, :], x)
        for i in range(part // 128):
            extra[i, pl.ds(b, blocks, stride=SUB), :] = more[:, i * 128 : (i + 1) * 128]

    @pl.when(b == SUB)
    def _():
        for i in range(part // 128):
            o_ref[:, i * 128 : (i + 1) * 128] = extra[i].astype(BF)


def dispatch(tokens, own, b1, b2, gain, table):
    rows, width = tokens.shape
    part = width // SUB
    blocks = table.shape[0] // (SUB + 1)
    wide = blocks * SUB
    whole = lambda a: pl.BlockSpec(a.shape, lambda b: (0, 0))
    args = (tokens, own, b1, b2, gain, table)
    return pl.pallas_call(
        dispatch_kernel,
        grid=(SUB + 1,),
        out_shape=(shape((rows, width), BF), shape((wide, width + part), BF)),
        in_specs=[whole(a) for a in args],
        out_specs=(whole(tokens), pl.BlockSpec((wide, part), lambda b: (0, b))),
        scratch_shapes=[
            pltpu.VMEM((SUB, rows, part), BF), pltpu.VMEM((part // 128, wide, 128), F32),
        ],
        compiler_params=limit(20),
        name="dispatch",
    )(*args)


def ffn_kernel(x_ref, *refs):
    sources, (o_ref, wg, wu, wd, rows_ref, extra, sem) = refs[:6], refs[6:]
    j = pl.program_id(0)
    width = rows_ref.shape[1]
    part = width // SUB
    wide = x_ref.shape[0]
    blocks = wide // SUB
    copies = [
        pltpu.make_async_copy(source, target.at[h], sem.at[h, i])
        for h in range(2)
        for i, (source, target) in enumerate(zip(sources[3 * h : 3 * h + 3], (wg, wu, wd)))
    ]

    @pl.when(j == 0)
    def _():
        for copy in copies:
            copy.start()

    rows_ref[:wide, :] = x_ref[:, :width]
    for i in range(part // 128):
        extra[i] = x_ref[:, width + i * 128 : width + (i + 1) * 128].astype(F32)
    for b in range(SUB):
        for i in range(part // 128):
            col = b * part + i * 128
            rows_ref[wide:, col : col + 128] = extra[i, pl.ds(b, blocks, stride=SUB), :].astype(BF)
    total = None
    for h in range(2):

        @pl.when(j == 0)
        def _():
            copies[3 * h].wait()
            copies[3 * h + 1].wait()

        gate = dot(rows_ref[...], wg[h])
        upper = dot(rows_ref[...], wu[h])
        act = (gate / (1.0 + jnp.exp(-gate)) * upper).astype(BF)

        @pl.when(j == 0)
        def _():
            copies[3 * h + 2].wait()

        out = dot(act, wd[h])
        total = out if total is None else total + out
    o_ref[:, :width] = total[:wide].astype(BF)
    for b in range(SUB):
        for i in range(part // 128):
            col = b * part + i * 128
            extra[i, pl.ds(b, blocks, stride=SUB), :] = total[wide:, col : col + 128]
    for i in range(part // 128):
        o_ref[:, width + i * 128 : width + (i + 1) * 128] = extra[i].astype(BF)


def ffn(x, w0, w1):
    wide, packed = x.shape
    width, hidden = w0[0].shape
    step = 256
    rows = step + step // SUB
    block = pl.BlockSpec((step, packed), lambda j: (j, 0))
    return pl.pallas_call(
        ffn_kernel,
        grid=(wide // step,),
        out_shape=shape((wide, packed), BF),
        in_specs=[block] + [pl.BlockSpec(memory_space=pltpu.HBM)] * 6,
        out_specs=block,
        scratch_shapes=[
            pltpu.VMEM((2, width, hidden), BF),
            pltpu.VMEM((2, width, hidden), BF),
            pltpu.VMEM((2, hidden, width), BF),
            pltpu.VMEM((rows, width), BF),
            pltpu.VMEM((width // SUB // 128, step, 128), F32),
            pltpu.SemaphoreType.DMA((2, 3)),
        ],
        compiler_params=limit(40),
        name="ffn",
    )(x, *w0, *w1)


def combine_kernel(live_ref, r_ref, x_ref, wm_ref, wx_ref, h_ref, o_ref, extra):
    b = pl.program_id(0)
    rows, part = o_ref.shape
    blocks = r_ref.shape[0] // SUB

    @pl.when(b == 0)
    def _():
        for i in range(part // 128):
            extra[i] = x_ref[:, i * 128 : (i + 1) * 128].astype(F32)

    more = jnp.concatenate(
        [extra[i, pl.ds(b, blocks, stride=SUB), :] for i in range(part // 128)], axis=1
    ).astype(BF)
    both = dot(wm_ref[...], r_ref[...]) + dot(wx_ref[...], more)
    out = h_ref[...].astype(F32) + both[:rows] + both[rows:]
    row = lax.broadcasted_iota(jnp.int32, out.shape, 0)
    o_ref[...] = jnp.where(row < live_ref[0], out, 0.0).astype(BF)


def combine(live, back, wm, wx, hidden):
    rows, width = hidden.shape
    part = width // SUB
    wide = back.shape[0]
    whole = lambda a: pl.BlockSpec(a.shape, lambda b: (0, 0))
    cols = lambda n: pl.BlockSpec((n, part), lambda b: (0, b))
    return pl.pallas_call(
        combine_kernel,
        grid=(SUB,),
        out_shape=shape((rows, width), BF),
        in_specs=[
            pl.BlockSpec(memory_space=pltpu.SMEM), cols(wide),
            pl.BlockSpec((wide, part), lambda b: (0, SUB)), whole(wm), whole(wx), cols(rows),
        ],
        out_specs=cols(rows),
        scratch_shapes=[pltpu.VMEM((part // 128, wide, 128), F32)],
        compiler_params=limit(20),
        name="combine",
    )(live, back, back, wm, wx, hidden)


def layer(
    tokens, attn_gain, w_query, w_key, w_value, w_out, prefix_cache, group_of, lengths,
    moe_gain, w_gate, w_up, w_down, routes, route_weights,
):
    rows, width = tokens.shape
    zs = lax.axis_size("z")
    reqs = lax.axis_size("x") * lax.axis_size("y")
    experts = reqs * zs
    z = lax.axis_index("z")
    core = lax.axis_index("c")
    req = lax.axis_index("x") * lax.axis_size("y") + lax.axis_index("y")
    local = w_query.shape[1]
    up = [(i, (i + 1) % zs) for i in range(zs)]
    down = [(i, (i - 1) % zs) for i in range(zs)]
    swap = lambda v: lax.ppermute(v, "c", [(0, 1), (1, 0)])
    to_up = lambda v: lax.ppermute(v, "z", up)
    to_down = lambda v: lax.ppermute(v, "z", down)
    half = rows // 2

    part = shape((half, width), BF)
    normed, first, last = call(norm_kernel, (shape((rows, width), BF), part, part), 2, name="norm")(
        tokens, attn_gain[None]
    )
    low0 = to_up(first)
    high1 = to_down(last)
    low1 = to_up(last)
    high0 = to_down(first)
    own_b = swap(normed)
    far0 = to_up(low0)
    far1 = to_down(high1)
    near_a = (low0, low1, high0, high1)
    near_b = tuple(swap(v) for v in near_a)

    out_b = swap(w_out)
    wq = (w_query, swap(w_query))
    wk = (w_key, swap(w_key))
    wv = (w_value, swap(w_value))

    spread = prefix_cache.shape[1]
    outgoing = pl.pallas_call(
        prefix_kernel,
        out_shape=shape((reqs * spread, 2 * local), BF),
        in_specs=[pl.BlockSpec(memory_space=pltpu.SMEM), vmem()],
        out_specs=vmem(),
        compiler_params=limit(16),
        name="prefix",
    )(group_of, jnp.transpose(prefix_cache, (0, 2, 1, 3)))
    pre_a = lax.all_to_all(outgoing, ("x", "y"), split_axis=0, concat_axis=0, tiled=True)
    pre_b = swap(pre_a)

    own_w = (w_gate[0], w_up[0], w_down[0])
    other_w = tuple(swap(w) for w in own_w)

    blocks = 2 * experts
    wide = blocks * SUB
    table, wm, wx = call(
        route_kernel,
        [
            shape((wide + blocks, rows), BF), shape((2 * rows, wide), BF),
            shape((2 * rows, blocks), BF),
        ],
        3,
        name="route",
    )(routes, routes.T, route_weights)

    mine, yours = core * rows, (1 - core) * rows
    z_low, z_high, z_far = (z + zs - 1) % zs, (z + 1) % zs, (z + 2) % zs
    starts = jnp.stack(
        [
            z * 2 * rows + mine, z * 2 * rows + yours,
            z_low * 2 * rows + mine, z_high * 2 * rows + mine,
            z_low * 2 * rows + yours, z_high * 2 * rows + yours,
            z_far * 2 * rows + mine, z_far * 2 * rows + yours,
        ]
    )
    place = (starts[:, None] + jnp.arange(rows, dtype=jnp.int32)).reshape(-1)
    spots = (PREFIX + place).astype(F32)
    freqs = 10000.0 ** (-(jnp.arange(HD // 2, dtype=F32) * 2.0) / HD)
    angles = spots[:, None] * freqs[None, :]
    cosine = jnp.cos(angles)
    sine = jnp.sin(angles)
    cosine = jnp.concatenate([cosine, cosine], axis=1)
    sine = jnp.concatenate([-sine, sine], axis=1)
    length = lengths[req]
    bias = jnp.where(place < length, 0.0, -1e30)[None, :]

    def projections(pieces, first, count, name):
        return call(
            lambda *refs: qkv_kernel(len(pieces), *refs),
            (
                shape((count // 2, 2 * local), BF),
                shape((count, 2 * local), BF),
                shape((count, 2 * local), BF),
            ),
            len(pieces) + 8,
            scratch_shapes=[pltpu.VMEM((count, width), BF)],
            name=name,
        )(*pieces, *wq, *wk, *wv, cosine[first : first + count], sine[first : first + count])

    q0, k0, v0 = projections((normed, own_b), 0, 2 * rows, "qkv_own")
    *near_b, k0 = lax.optimization_barrier((*near_b, k0))
    q1, k1, v1 = projections((*near_a, *near_b), 2 * rows, 4 * rows, "qkv_near")
    far0, far1, k1 = lax.optimization_barrier((far0, far1, k1))
    q2, k2, v2 = projections((far0, far1, swap(far0), swap(far1)), 6 * rows, 2 * rows, "qkv_far")
    cache = (k0, k1, k2, v0, v1, v2, pre_a, pre_b, bias)
    scale = math.log2(math.e) / math.sqrt(HD)
    tmp = [pltpu.VMEM((rows, 2 * local), BF)]

    far1, far2 = call(
        functools.partial(attn_far_kernel, scale),
        [shape((half, width), BF)] * 2,
        12,
        scratch_shapes=tmp,
        name="attn_far",
    )(q2, *cache, w_out, out_b)
    got1 = to_up(far1)
    got2 = to_down(far2)
    near = call(
        functools.partial(attn_near_kernel, scale), shape((2 * rows, 2 * local), BF), 10,
        name="attn_near",
    )(q1, *cache)
    to_low, to_high = call(
        proj_near_kernel, [shape((rows, width), BF)] * 2, 5, name="proj_near"
    )(near, w_out, out_b, got1, got2)
    to_low, to_high, q0 = lax.optimization_barrier((to_low, to_high, q0))
    b1 = to_up(to_high)
    b2 = to_down(to_low)
    own = call(
        functools.partial(attn_own_kernel, scale),
        shape((rows, width), F32),
        12,
        scratch_shapes=tmp,
        name="attn_own",
    )(q0, *cache, w_out, out_b)
    own, other_w = lax.optimization_barrier((own, other_w))

    hidden, send = dispatch(tokens, own, b1, b2, moe_gain[None], table)

    def exchange(v):
        return lax.all_to_all(
            v.reshape(experts, 2 * SUB, v.shape[1]), ("x", "y", "z"), 0, 0, tiled=True
        ).reshape(v.shape)

    back = exchange(ffn(exchange(send), own_w, other_w))
    live = jnp.clip(length - (z * 2 + core) * rows, 0, rows).astype(jnp.int32)[None]
    return combine(live, back, wm, wx, hidden)


def solution(mesh):
    side = math.isqrt(mesh.shape["req"])
    grid = Mesh(
        mesh.devices.reshape(side, side, mesh.shape["exp"] // 2, 2), ("x", "y", "z", "c")
    )
    req, exp = ("x", "y"), ("z", "c")
    every = req + exp
    return jax.shard_map(
        layer,
        mesh=grid,
        in_specs=(
            P(every, None), P(), P(None, exp), P(None, exp), P(None, exp), P(exp, None),
            P(None, req, None, exp), P(), P(), P(),
            P(every, None, None), P(every, None, None), P(every, None, None),
            P(every, None), P(every, None),
        ),
        out_specs=P(every, None),
        check_vma=False,
    )
```

```python
import functools
import math

import jax
import jax.numpy as jnp
from jax import lax
from jax.experimental import pallas as pl
from jax.experimental.pallas import tpu as pltpu
from jax.sharding import Mesh
from jax.sharding import PartitionSpec as P


HD = 128
PREFIX = 1024
BF = jnp.bfloat16
F32 = jnp.float32
SUB = 8


def vmem():
    return pl.BlockSpec(memory_space=pltpu.VMEM)


def limit(mib):
    return pltpu.CompilerParams(vmem_limit_bytes=mib << 20)


def call(kernel, out_shape, n_in, mib=16, **kw):
    outs = jax.tree.map(lambda _: vmem(), out_shape)
    return pl.pallas_call(
        kernel, out_shape=out_shape, in_specs=[vmem()] * n_in, out_specs=outs,
        compiler_params=limit(mib), **kw
    )


def near(a):
    return pltpu.with_memory_space_constraint(a, pltpu.VMEM)


def away(a):
    return pltpu.with_memory_space_constraint(a, pltpu.HBM)


def shape(dims, dtype):
    return jax.ShapeDtypeStruct(dims, dtype)


def dot(a, b):
    return jnp.dot(a, b, preferred_element_type=F32)


def rms(wide, gain):
    return wide * lax.rsqrt(jnp.mean(wide * wide, axis=-1, keepdims=True) + 1e-05) * gain


def norm_kernel(x_ref, g_ref, o_ref, first_ref, last_ref):
    normed = rms(x_ref[...].astype(F32), g_ref[...]).astype(BF)
    o_ref[...] = normed
    half = first_ref.shape[0]
    first_ref[...] = normed[:half]
    last_ref[...] = normed[half:]


def slots_of(index):
    block = index // SUB
    return block // 2, (block % 2) * (SUB + 1) + index % SUB


def route_kernel(r_ref, rt_ref, w_ref, dt_ref, wm_ref, wx_ref):
    rows, top = r_ref.shape
    blocks = wx_ref.shape[1]
    experts = blocks // 2
    wide = blocks * SUB
    iota = lambda dims, axis: lax.broadcasted_iota(jnp.int32, dims, axis)
    one = lambda hit: jnp.where(hit, 1.0, 0.0)
    row_i = iota((rows, rows), 0)
    col_i = iota((rows, rows), 1)
    e_t = iota((experts, rows), 0)
    named_t = jnp.zeros((experts, rows), F32)
    for k in range(top):
        named_t += one(rt_ref[k : k + 1, :] == e_t)
    rank_t = dot(named_t.astype(BF), one(row_i < col_i).astype(BF))
    rank_t = jnp.where(named_t > 0.5, rank_t, -1.0).astype(BF)
    expert, _ = slots_of(iota((wide, experts), 0))
    spread = one(expert == iota((wide, experts), 1)).astype(BF)
    _, slot = slots_of(iota((wide, rows), 0))
    dt_ref[:wide, :] = one(dot(spread, rank_t) == slot.astype(F32)).astype(BF)
    block = iota((blocks, experts), 0)
    spread = one(block // 2 == iota((blocks, experts), 1)).astype(BF)
    slot = (iota((blocks, rows), 0) % 2) * (SUB + 1) + SUB
    dt_ref[wide:, :] = one(dot(spread, rank_t) == slot.astype(F32)).astype(BF)
    e_n = iota((rows, experts), 1)
    named = jnp.zeros((rows, experts), F32)
    weight = jnp.zeros((rows, experts), F32)
    for k in range(top):
        hit = r_ref[:, k : k + 1] == e_n
        named += one(hit)
        weight += jnp.where(hit, w_ref[:, k : k + 1], 0.0)
    rank = dot(one(col_i < row_i).astype(BF), named.astype(BF))
    rank = jnp.where(named > 0.5, rank, -1.0).astype(BF)
    high = weight.astype(BF)
    low = (weight - high.astype(F32)).astype(BF)
    expert, _ = slots_of(iota((experts, wide), 1))
    spread = one(expert == iota((experts, wide), 0)).astype(BF)
    _, slot = slots_of(iota((rows, wide), 1))
    hit = dot(rank, spread) == slot.astype(F32)
    wm_ref[:rows, :] = jnp.where(hit, dot(high, spread), 0.0).astype(BF)
    wm_ref[rows:, :] = jnp.where(hit, dot(low, spread), 0.0).astype(BF)
    block = iota((experts, blocks), 1)
    spread = one(block // 2 == iota((experts, blocks), 0)).astype(BF)
    slot = (iota((rows, blocks), 1) % 2) * (SUB + 1) + SUB
    hit = dot(rank, spread) == slot.astype(F32)
    wx_ref[:rows, :] = jnp.where(hit, dot(high, spread), 0.0).astype(BF)
    wx_ref[rows:, :] = jnp.where(hit, dot(low, spread), 0.0).astype(BF)


def prefix_kernel(group_ref, x_ref, o_ref):
    rows, width = x_ref.shape[2:]
    for r in range(o_ref.shape[0] // rows):
        for j in range(2):
            o_ref[r * rows : (r + 1) * rows, j * width : (j + 1) * width] = x_ref[group_ref[r], j]


def qkv_kernel(count, *refs):
    pieces, weights, refs = refs[:count], refs[count : count + 6], refs[count + 6 :]
    cos_ref, sin_ref, q_ref, k_ref, v_ref, x_ref, w_ref, x_sem, w_sem = refs
    at = 0
    copies = []
    for i, piece in enumerate(pieces):
        n = piece.shape[0]
        copies.append(pltpu.make_async_copy(piece, x_ref.at[at : at + n], x_sem.at[i]))
        at += n
    loads = [pltpu.make_async_copy(w, w_ref.at[i], w_sem.at[i]) for i, w in enumerate(weights)]
    loads[0].start()
    for copy in copies:
        copy.start()
    for load in loads[1:]:
        load.start()
    for copy in copies:
        copy.wait()
    local = w_ref.shape[2]
    for i, load in enumerate(loads):
        load.wait()
        o_ref = (k_ref, q_ref, v_ref)[i // 2]
        rows = o_ref.shape[0]
        mixed = dot(x_ref[:rows, :], w_ref[i])
        col = i % 2 * local
        if o_ref is v_ref:
            o_ref[:, col : col + local] = mixed.astype(BF)
            continue
        for h in range(local // HD):
            v = mixed[:, h * HD : (h + 1) * HD]
            turned = v * cos_ref[:rows, :] + pltpu.roll(v, HD // 2, 1) * sin_ref[:rows, :]
            o_ref[:, col + h * HD : col + (h + 1) * HD] = turned.astype(BF)


def attend(scale, q_ref, k_ref, v_ref, pre_refs, bias_ref, o_ref, first):
    local = pre_refs[0].shape[1] // 2
    rows = o_ref.shape[0]
    nt = (((1,), (1,)), ((), ()))
    for h in range(q_ref.shape[1] // HD):
        side, col = divmod(h * HD, local)
        pre_ref = pre_refs[side]
        cols = slice(h * HD, (h + 1) * HD)
        q = q_ref[first : first + rows, cols]
        s1 = lax.dot_general(q, pre_ref[:, col : col + HD], nt, preferred_element_type=F32)
        s2 = lax.dot_general(q, k_ref[:, cols], nt, preferred_element_type=F32) + bias_ref[...]
        top = jnp.maximum(
            jnp.max(s1, axis=-1, keepdims=True), jnp.max(s2, axis=-1, keepdims=True)
        )
        e1 = jnp.exp2((s1 - top) * scale)
        e2 = jnp.exp2((s2 - top) * scale)
        total = jnp.sum(e1, axis=-1, keepdims=True) + jnp.sum(e2, axis=-1, keepdims=True)
        out = dot(e1.astype(BF), pre_ref[:, local + col : local + col + HD])
        out += dot(e2.astype(BF), v_ref[:, cols])
        o_ref[:, cols] = (out / total).astype(BF)


def project(a_ref, wa_ref, wb_ref):
    local = wa_ref.shape[0]
    return dot(a_ref[:, :local], wa_ref[...]) + dot(a_ref[:, local:], wb_ref[...])


def attn_far_kernel(scale, first, q, k, v, pa, pb, bias, wa, wb, o1, o2, tmp):
    attend(scale, q, k, v, (pa, pb), bias, tmp, first)
    total = project(tmp, wa, wb).astype(BF)
    rows = o1.shape[0]
    o1[...] = total[:rows]
    o2[...] = total[rows:]


def attn_near_kernel(scale, first, q, k, v, pa, pb, bias, o):
    attend(scale, q, k, v, (pa, pb), bias, o, first)


def attn_own_kernel(scale, first, q, k, v, pa, pb, bias, wa, wb, o, tmp):
    attend(scale, q, k, v, (pa, pb), bias, tmp, first)
    o[...] = project(tmp, wa, wb)


def proj_near_kernel(a_ref, wa, wb, got1, got2, low_ref, high_ref):
    total = project(a_ref, wa, wb)
    rows = low_ref.shape[0]
    half = rows // 2
    low_ref[:half, :] = total[:half].astype(BF)
    low_ref[half:, :] = (total[half:rows] + got2[...].astype(F32)).astype(BF)
    high_ref[:half, :] = (total[rows : rows + half] + got1[...].astype(F32)).astype(BF)
    high_ref[half:, :] = total[rows + half :].astype(BF)


def dispatch_kernel(t_ref, own_ref, b1_ref, b2_ref, g_ref, d_ref, h_ref, o_ref, normed, extra):
    b = pl.program_id(0)
    part = o_ref.shape[1]
    wide = o_ref.shape[0]
    blocks = wide // SUB

    @pl.when(b == 0)
    def _():
        attn_out = own_ref[...] + b1_ref[...].astype(F32) + b2_ref[...].astype(F32)
        hidden = (t_ref[...].astype(F32) + attn_out).astype(BF)
        h_ref[...] = hidden
        rows = rms(hidden.astype(F32), g_ref[...]).astype(BF)
        for i in range(SUB):
            normed[i] = rows[:, i * part : (i + 1) * part]

    @pl.when(b < SUB)
    def _():
        x = normed[b]
        o_ref[...] = dot(d_ref[:wide, :], x).astype(BF)
        more = dot(d_ref[wide:, :], x)
        for i in range(part // 128):
            extra[i, pl.ds(b, blocks, stride=SUB), :] = more[:, i * 128 : (i + 1) * 128]

    @pl.when(b == SUB)
    def _():
        for i in range(part // 128):
            o_ref[:, i * 128 : (i + 1) * 128] = extra[i].astype(BF)


def dispatch(tokens, own, b1, b2, gain, table):
    rows, width = tokens.shape
    part = width // SUB
    blocks = table.shape[0] // (SUB + 1)
    wide = blocks * SUB
    whole = lambda a: pl.BlockSpec(a.shape, lambda b: (0, 0))
    args = (tokens, own, b1, b2, gain, table)
    return pl.pallas_call(
        dispatch_kernel,
        grid=(SUB + 1,),
        out_shape=(pltpu.HBM((rows, width), BF), pltpu.HBM((wide, width + part), BF)),
        in_specs=[whole(a) for a in args],
        out_specs=(whole(tokens), pl.BlockSpec((wide, part), lambda b: (0, b))),
        scratch_shapes=[
            pltpu.VMEM((SUB, rows, part), BF), pltpu.VMEM((part // 128, wide, 128), F32),
        ],
        compiler_params=limit(20),
        name="dispatch",
    )(*args)


def ffn_kernel(x_ref, *refs):
    sources, (o_ref, wg, wu, wd, rows_ref, extra, sem) = refs[:6], refs[6:]
    j = pl.program_id(0)
    width = rows_ref.shape[1]
    part = width // SUB
    wide = x_ref.shape[0]
    blocks = wide // SUB
    copies = [
        pltpu.make_async_copy(source, target.at[h], sem.at[h, i])
        for h in range(2)
        for i, (source, target) in enumerate(zip(sources[3 * h : 3 * h + 3], (wg, wu, wd)))
    ]

    @pl.when(j == 0)
    def _():
        for copy in copies:
            copy.start()

    rows_ref[:wide, :] = x_ref[:, :width]
    for i in range(part // 128):
        extra[i] = x_ref[:, width + i * 128 : width + (i + 1) * 128].astype(F32)
    for b in range(SUB):
        for i in range(part // 128):
            col = b * part + i * 128
            rows_ref[wide:, col : col + 128] = extra[i, pl.ds(b, blocks, stride=SUB), :].astype(BF)
    total = None
    for h in range(2):

        @pl.when(j == 0)
        def _():
            copies[3 * h].wait()
            copies[3 * h + 1].wait()

        gate = dot(rows_ref[...], wg[h])
        upper = dot(rows_ref[...], wu[h])
        act = (gate / (1.0 + jnp.exp(-gate)) * upper).astype(BF)

        @pl.when(j == 0)
        def _():
            copies[3 * h + 2].wait()

        out = dot(act, wd[h])
        total = out if total is None else total + out
    o_ref[:, :width] = total[:wide].astype(BF)
    for b in range(SUB):
        for i in range(part // 128):
            col = b * part + i * 128
            extra[i, pl.ds(b, blocks, stride=SUB), :] = total[wide:, col : col + 128]
    for i in range(part // 128):
        o_ref[:, width + i * 128 : width + (i + 1) * 128] = extra[i].astype(BF)


def ffn(x, w0, w1):
    wide, packed = x.shape
    width, hidden = w0[0].shape
    step = 256
    rows = step + step // SUB
    block = pl.BlockSpec((step, packed), lambda j: (j, 0))
    return pl.pallas_call(
        ffn_kernel,
        grid=(wide // step,),
        out_shape=shape((wide, packed), BF),
        in_specs=[block] + [pl.BlockSpec(memory_space=pltpu.HBM)] * 6,
        out_specs=block,
        scratch_shapes=[
            pltpu.VMEM((2, width, hidden), BF),
            pltpu.VMEM((2, width, hidden), BF),
            pltpu.VMEM((2, hidden, width), BF),
            pltpu.VMEM((rows, width), BF),
            pltpu.VMEM((width // SUB // 128, step, 128), F32),
            pltpu.SemaphoreType.DMA((2, 3)),
        ],
        compiler_params=limit(40),
        name="ffn",
    )(x, *w0, *w1)


def combine_kernel(live_ref, r_ref, x_ref, wm_ref, wx_ref, h_ref, o_ref, extra):
    b = pl.program_id(0)
    rows, part = o_ref.shape
    blocks = r_ref.shape[0] // SUB

    @pl.when(b == 0)
    def _():
        for i in range(part // 128):
            extra[i] = x_ref[:, i * 128 : (i + 1) * 128].astype(F32)

    more = jnp.concatenate(
        [extra[i, pl.ds(b, blocks, stride=SUB), :] for i in range(part // 128)], axis=1
    ).astype(BF)
    both = dot(wm_ref[...], r_ref[...]) + dot(wx_ref[...], more)
    out = h_ref[...].astype(F32) + both[:rows] + both[rows:]
    row = lax.broadcasted_iota(jnp.int32, out.shape, 0)
    o_ref[...] = jnp.where(row < live_ref[0], out, 0.0).astype(BF)


def combine(live, back, wm, wx, hidden):
    rows, width = hidden.shape
    part = width // SUB
    wide = back.shape[0]
    whole = lambda a: pl.BlockSpec(a.shape, lambda b: (0, 0))
    cols = lambda n: pl.BlockSpec((n, part), lambda b: (0, b))
    return pl.pallas_call(
        combine_kernel,
        grid=(SUB,),
        out_shape=shape((rows, width), BF),
        in_specs=[
            pl.BlockSpec(memory_space=pltpu.SMEM), cols(wide),
            pl.BlockSpec((wide, part), lambda b: (0, SUB)), whole(wm), whole(wx), cols(rows),
        ],
        out_specs=cols(rows),
        scratch_shapes=[pltpu.VMEM((part // 128, wide, 128), F32)],
        compiler_params=limit(20),
        name="combine",
    )(live, back, back, wm, wx, hidden)


def layer(
    tokens, attn_gain, w_query, w_key, w_value, w_out, prefix_cache, group_of, lengths,
    moe_gain, w_gate, w_up, w_down, routes, route_weights,
):
    rows, width = tokens.shape
    zs = lax.axis_size("z")
    reqs = lax.axis_size("x") * lax.axis_size("y")
    experts = reqs * zs
    z = lax.axis_index("z")
    core = lax.axis_index("c")
    req = lax.axis_index("x") * lax.axis_size("y") + lax.axis_index("y")
    local = w_query.shape[1]
    up = [(i, (i + 1) % zs) for i in range(zs)]
    down = [(i, (i - 1) % zs) for i in range(zs)]
    swap = lambda v: lax.ppermute(v, "c", [(0, 1), (1, 0)])
    to_up = lambda v: lax.ppermute(v, "z", up)
    to_down = lambda v: lax.ppermute(v, "z", down)
    half = rows // 2

    part = pltpu.HBM((half, width), BF)
    normed, first, last = call(
        norm_kernel, (pltpu.HBM((rows, width), BF), part, part), 2, name="norm"
    )(away(tokens), away(attn_gain[None]))
    low0 = to_up(first)
    high1 = to_down(last)
    low1 = to_up(last)
    high0 = to_down(first)
    own_b = swap(normed)
    far0 = to_up(low0)
    far1 = to_down(high1)
    near_a = (low0, low1, high0, high1)
    near_b = tuple(swap(v) for v in near_a)
    far_b = swap(far0), swap(far1)

    wk = (w_key, swap(w_key))
    wq = (w_query, swap(w_query))
    wv = (w_value, swap(w_value))
    out_b = swap(w_out)

    spread = prefix_cache.shape[1]
    outgoing = pl.pallas_call(
        prefix_kernel,
        out_shape=pltpu.HBM((reqs * spread, 2 * local), BF),
        in_specs=[pl.BlockSpec(memory_space=pltpu.SMEM), vmem()],
        out_specs=vmem(),
        compiler_params=limit(16),
        name="prefix",
    )(group_of, jnp.transpose(prefix_cache, (0, 2, 1, 3)))
    pre_a = lax.all_to_all(outgoing, ("x", "y"), split_axis=0, concat_axis=0, tiled=True)
    pre_b = swap(pre_a)

    own_w = (w_gate[0], w_up[0], w_down[0])
    other_w = tuple(swap(w) for w in own_w)

    mine, yours = core * rows, (1 - core) * rows
    z_low, z_high, z_far = (z + zs - 1) % zs, (z + 1) % zs, (z + 2) % zs
    starts = jnp.stack(
        [chip * 2 * rows + who for who in (mine, yours) for chip in (z, z_low, z_high, z_far)]
    )
    place = (starts[:, None] + jnp.arange(rows, dtype=jnp.int32)).reshape(-1)
    spots = (PREFIX + place).astype(F32)
    freqs = 10000.0 ** (-(jnp.arange(HD // 2, dtype=F32) * 2.0) / HD)
    angles = spots[:, None] * freqs[None, :]
    cosine = jnp.cos(angles)
    sine = jnp.sin(angles)
    cosine = jnp.concatenate([cosine, cosine], axis=1)
    sine = jnp.concatenate([-sine, sine], axis=1)
    length = lengths[req]
    bias = jnp.where(place < length, 0.0, -1e30)[None, :]

    live = jnp.clip(length - (z * 2 + core) * rows, 0, rows).astype(jnp.int32)[None]
    routes, cosine, sine, bias, live = lax.optimization_barrier(
        (routes, cosine, sine, bias, live)
    )

    blocks = 2 * experts
    wide = blocks * SUB
    table, wm, wx = call(
        route_kernel,
        [
            pltpu.HBM((wide + blocks, rows), BF), pltpu.HBM((2 * rows, wide), BF),
            pltpu.HBM((2 * rows, blocks), BF),
        ],
        3,
        name="route",
    )(routes, routes.T, route_weights)

    far_b, table = lax.optimization_barrier((far_b, table))

    slots = 2 * zs * rows
    pieces = (normed, *near_a, far0, far1, own_b, *near_b, *far_b)
    q, k, v = pl.pallas_call(
        lambda *refs: qkv_kernel(len(pieces), *refs),
        out_shape=(
            pltpu.VMEM((slots // 2, 2 * local), BF),
            pltpu.VMEM((slots, 2 * local), BF),
            pltpu.VMEM((slots, 2 * local), BF),
        ),
        in_specs=[pl.BlockSpec(memory_space=pl.ANY)] * (len(pieces) + 6) + [vmem()] * 2,
        out_specs=(vmem(),) * 3,
        scratch_shapes=[
            pltpu.VMEM((slots, width), BF),
            pltpu.VMEM((6, width, local), BF),
            pltpu.SemaphoreType.DMA((len(pieces),)),
            pltpu.SemaphoreType.DMA((6,)),
        ],
        compiler_params=limit(24),
        name="qkv",
    )(*map(away, (*pieces, *wk, *wq, *wv, cosine, sine)))
    cache = (near(q), near(k), near(v), pre_a, pre_b, bias)
    scale = math.log2(math.e) / math.sqrt(HD)
    tmp = [pltpu.VMEM((rows, 2 * local), BF)]

    sum1, sum2 = call(
        functools.partial(attn_far_kernel, scale, 3 * rows),
        [shape((half, width), BF)] * 2,
        8,
        scratch_shapes=tmp,
        name="attn_far",
    )(*cache, w_out, out_b)
    got1 = to_up(sum1)
    got2 = to_down(sum2)
    around = call(
        functools.partial(attn_near_kernel, scale, rows),
        shape((2 * rows, 2 * local), BF),
        6,
        name="attn_near",
    )(*cache)
    to_low, to_high = call(
        proj_near_kernel, [shape((rows, width), BF)] * 2, 5, name="proj_near"
    )(around, w_out, out_b, got1, got2)
    b1 = to_up(to_high)
    b2 = to_down(to_low)
    own = call(
        functools.partial(attn_own_kernel, scale, 0),
        shape((rows, width), F32),
        8,
        scratch_shapes=tmp,
        name="attn_own",
    )(*cache, w_out, out_b)
    own, other_w = lax.optimization_barrier((own, other_w))

    hidden, send = dispatch(tokens, own, b1, b2, moe_gain[None], table)

    def exchange(v):
        return lax.all_to_all(
            v.reshape(experts, 2 * SUB, v.shape[1]), ("x", "y", "z"), 0, 0, tiled=True
        ).reshape(v.shape)

    back = exchange(ffn(exchange(send), own_w, other_w))
    return combine(live, back, wm, wx, hidden)


def solution(mesh):
    side = math.isqrt(mesh.shape["req"])
    grid = Mesh(
        mesh.devices.reshape(side, side, mesh.shape["exp"] // 2, 2), ("x", "y", "z", "c")
    )
    req, exp = ("x", "y"), ("z", "c")
    every = req + exp
    return jax.shard_map(
        layer,
        mesh=grid,
        in_specs=(
            P(every, None), P(), P(None, exp), P(None, exp), P(None, exp), P(exp, None),
            P(None, req, None, exp), P(), P(), P(),
            P(every, None, None), P(every, None, None), P(every, None, None),
            P(every, None), P(every, None),
        ),
        out_specs=P(every, None),
        check_vma=False,
    )
```

```python
import functools
import math

import jax
import jax.numpy as jnp
from jax import lax
from jax.experimental import pallas as pl
from jax.experimental.pallas import tpu as pltpu
from jax.sharding import Mesh
from jax.sharding import PartitionSpec as P


HD = 128
PREFIX = 1024
BF = jnp.bfloat16
F32 = jnp.float32
SUB = 8


def vmem():
    return pl.BlockSpec(memory_space=pltpu.VMEM)


def limit(mib):
    return pltpu.CompilerParams(vmem_limit_bytes=mib << 20)


def call(kernel, out_shape, n_in, mib=16, **kw):
    outs = jax.tree.map(lambda _: vmem(), out_shape)
    return pl.pallas_call(
        kernel, out_shape=out_shape, in_specs=[vmem()] * n_in, out_specs=outs,
        compiler_params=limit(mib), **kw
    )


def near(a):
    return pltpu.with_memory_space_constraint(a, pltpu.VMEM)


def away(a):
    return pltpu.with_memory_space_constraint(a, pltpu.HBM)


def shape(dims, dtype):
    return jax.ShapeDtypeStruct(dims, dtype)


def dot(a, b):
    return jnp.dot(a, b, preferred_element_type=F32)


def rms(wide, gain):
    return wide * lax.rsqrt(jnp.mean(wide * wide, axis=-1, keepdims=True) + 1e-05) * gain


def norm_kernel(x_ref, g_ref, o_ref, first_ref, last_ref):
    normed = rms(x_ref[...].astype(F32), g_ref[...]).astype(BF)
    o_ref[...] = normed
    half = first_ref.shape[0]
    first_ref[...] = normed[:half]
    last_ref[...] = normed[half:]


def slots_of(index):
    block = index // SUB
    return block // 2, (block % 2) * (SUB + 1) + index % SUB


def route_kernel(r_ref, rt_ref, w_ref, dt_ref, wm_ref, wx_ref):
    rows, top = r_ref.shape
    blocks = wx_ref.shape[1]
    experts = blocks // 2
    wide = blocks * SUB
    iota = lambda dims, axis: lax.broadcasted_iota(jnp.int32, dims, axis)
    one = lambda hit: jnp.where(hit, 1.0, 0.0)
    row_i = iota((rows, rows), 0)
    col_i = iota((rows, rows), 1)
    e_t = iota((experts, rows), 0)
    named_t = jnp.zeros((experts, rows), F32)
    for k in range(top):
        named_t += one(rt_ref[k : k + 1, :] == e_t)
    rank_t = dot(named_t.astype(BF), one(row_i < col_i).astype(BF))
    rank_t = jnp.where(named_t > 0.5, rank_t, -1.0).astype(BF)
    expert, _ = slots_of(iota((wide, experts), 0))
    spread = one(expert == iota((wide, experts), 1)).astype(BF)
    _, slot = slots_of(iota((wide, rows), 0))
    dt_ref[:wide, :] = one(dot(spread, rank_t) == slot.astype(F32)).astype(BF)
    block = iota((blocks, experts), 0)
    spread = one(block // 2 == iota((blocks, experts), 1)).astype(BF)
    slot = (iota((blocks, rows), 0) % 2) * (SUB + 1) + SUB
    dt_ref[wide:, :] = one(dot(spread, rank_t) == slot.astype(F32)).astype(BF)
    e_n = iota((rows, experts), 1)
    named = jnp.zeros((rows, experts), F32)
    weight = jnp.zeros((rows, experts), F32)
    for k in range(top):
        hit = r_ref[:, k : k + 1] == e_n
        named += one(hit)
        weight += jnp.where(hit, w_ref[:, k : k + 1], 0.0)
    rank = dot(one(col_i < row_i).astype(BF), named.astype(BF))
    rank = jnp.where(named > 0.5, rank, -1.0).astype(BF)
    high = weight.astype(BF)
    low = (weight - high.astype(F32)).astype(BF)
    expert, _ = slots_of(iota((experts, wide), 1))
    spread = one(expert == iota((experts, wide), 0)).astype(BF)
    _, slot = slots_of(iota((rows, wide), 1))
    hit = dot(rank, spread) == slot.astype(F32)
    wm_ref[:rows, :] = jnp.where(hit, dot(high, spread), 0.0).astype(BF)
    wm_ref[rows:, :] = jnp.where(hit, dot(low, spread), 0.0).astype(BF)
    block = iota((experts, blocks), 1)
    spread = one(block // 2 == iota((experts, blocks), 0)).astype(BF)
    slot = (iota((rows, blocks), 1) % 2) * (SUB + 1) + SUB
    hit = dot(rank, spread) == slot.astype(F32)
    wx_ref[:rows, :] = jnp.where(hit, dot(high, spread), 0.0).astype(BF)
    wx_ref[rows:, :] = jnp.where(hit, dot(low, spread), 0.0).astype(BF)


def prefix_kernel(group_ref, x_ref, o_ref):
    rows, width = x_ref.shape[2:]
    for r in range(o_ref.shape[0] // rows):
        for j in range(2):
            o_ref[r * rows : (r + 1) * rows, j * width : (j + 1) * width] = x_ref[group_ref[r], j]


def qkv_kernel(count, *refs):
    pieces, weights, refs = refs[:count], refs[count : count + 6], refs[count + 6 :]
    cos_ref, sin_ref, q_ref, k_ref, v_ref, x_ref, w_ref, x_sem, w_sem = refs
    at = 0
    copies = []
    for i, piece in enumerate(pieces):
        n = piece.shape[0]
        copies.append(pltpu.make_async_copy(piece, x_ref.at[at : at + n], x_sem.at[i]))
        at += n
    local = w_ref.shape[2] // 2
    loads = [
        pltpu.make_async_copy(
            w, w_ref.at[i // 2, :, i % 2 * local : (i % 2 + 1) * local], w_sem.at[i]
        )
        for i, w in enumerate(weights)
    ]
    for load in loads[:2]:
        load.start()
    for copy in copies:
        copy.start()
    for load in loads[2:]:
        load.start()
    for copy in copies:
        copy.wait()
    for i, o_ref in enumerate((k_ref, q_ref, v_ref)):
        loads[2 * i].wait()
        loads[2 * i + 1].wait()
        rows = o_ref.shape[0]
        mixed = dot(x_ref[:rows, :], w_ref[i])
        if o_ref is v_ref:
            o_ref[...] = mixed.astype(BF)
            continue
        for h in range(2 * local // HD):
            v = mixed[:, h * HD : (h + 1) * HD]
            turned = v * cos_ref[:rows, :] + pltpu.roll(v, HD // 2, 1) * sin_ref[:rows, :]
            o_ref[:, h * HD : (h + 1) * HD] = turned.astype(BF)


def attend(scale, q_ref, k_ref, v_ref, pre_refs, bias_ref, o_ref, first):
    local = pre_refs[0].shape[1] // 2
    rows = o_ref.shape[0]
    nt = (((1,), (1,)), ((), ()))
    for h in range(q_ref.shape[1] // HD):
        side, col = divmod(h * HD, local)
        pre_ref = pre_refs[side]
        cols = slice(h * HD, (h + 1) * HD)
        q = q_ref[first : first + rows, cols]
        s1 = lax.dot_general(q, pre_ref[:, col : col + HD], nt, preferred_element_type=F32)
        s2 = lax.dot_general(q, k_ref[:, cols], nt, preferred_element_type=F32) + bias_ref[...]
        top = jnp.maximum(
            jnp.max(s1, axis=-1, keepdims=True), jnp.max(s2, axis=-1, keepdims=True)
        )
        e1 = jnp.exp2((s1 - top) * scale)
        e2 = jnp.exp2((s2 - top) * scale)
        total = jnp.sum(e1, axis=-1, keepdims=True) + jnp.sum(e2, axis=-1, keepdims=True)
        out = dot(e1.astype(BF), pre_ref[:, local + col : local + col + HD])
        out += dot(e2.astype(BF), v_ref[:, cols])
        o_ref[:, cols] = (out / total).astype(BF)


def project(a_ref, wa_ref, wb_ref):
    local = wa_ref.shape[0]
    return dot(a_ref[:, :local], wa_ref[...]) + dot(a_ref[:, local:], wb_ref[...])


def attn_far_kernel(scale, first, q, k, v, pa, pb, bias, wa, wb, o1, o2, tmp):
    attend(scale, q, k, v, (pa, pb), bias, tmp, first)
    total = project(tmp, wa, wb).astype(BF)
    rows = o1.shape[0]
    o1[...] = total[:rows]
    o2[...] = total[rows:]


def attn_near_kernel(
    scale, first, q, k, v, pa, pb, bias, wa, wb, low_free, low_need, high_need, high_free, tmp
):
    attend(scale, q, k, v, (pa, pb), bias, tmp, first)
    total = project(tmp, wa, wb)
    n = low_free.shape[0]
    for i, o_ref in enumerate((low_free, low_need, high_need, high_free)):
        o_ref[...] = total[i * n : (i + 1) * n].astype(o_ref.dtype)


def attn_own_kernel(scale, first, q, k, v, pa, pb, bias, wa, wb, o, tmp):
    attend(scale, q, k, v, (pa, pb), bias, tmp, first)
    o[...] = project(tmp, wa, wb)


def add_kernel(a_ref, a_got, b_ref, b_got, a_out, b_out):
    a_out[...] = (a_ref[...] + a_got[...].astype(F32)).astype(BF)
    b_out[...] = (b_ref[...] + b_got[...].astype(F32)).astype(BF)


def dispatch_kernel(
    t_ref, own_ref, a1, a2, b1, b2, g_ref, d_ref, h_ref, o_ref, normed, extra
):
    step = pl.program_id(0)
    part = normed.shape[2]
    group = o_ref.shape[1] // part
    wide = o_ref.shape[0]
    blocks = wide // SUB

    @pl.when(step == 0)
    def _():
        half = a1.shape[0]
        for at, x, y in ((0, a1, a2), (half, b1, b2)):
            here = slice(at, at + half)
            attn_out = own_ref[here, :] + x[...].astype(F32) + y[...].astype(F32)
            hidden = (t_ref[here, :].astype(F32) + attn_out).astype(BF)
            h_ref[here, :] = hidden
            rows = rms(hidden.astype(F32), g_ref[...]).astype(BF)
            for i in range(SUB):
                normed[i, here, :] = rows[:, i * part : (i + 1) * part]

    for i in range(group):
        b = step * group + i

        def columns(b=b, i=i):
            x = normed[b]
            o_ref[:, i * part : (i + 1) * part] = dot(d_ref[:wide, :], x).astype(BF)
            more = dot(d_ref[wide:, :], x)
            for n in range(part // 128):
                extra[n, pl.ds(b, blocks, stride=SUB), :] = more[:, n * 128 : (n + 1) * 128]

        if i < group - 1:
            columns()
            continue
        pl.when(b < SUB)(columns)

        @pl.when(b == SUB)
        def _():
            for n in range(part // 128):
                o_ref[:, i * part + n * 128 : i * part + (n + 1) * 128] = extra[n].astype(BF)


def dispatch(tokens, *rest):
    args = (tokens, *rest)
    table = rest[-1]
    rows, width = tokens.shape
    part = width // SUB
    group = 3
    wide = table.shape[0] // (SUB + 1) * SUB
    whole = lambda a: pl.BlockSpec(a.shape, lambda b: (0, 0))
    return pl.pallas_call(
        dispatch_kernel,
        grid=((SUB + 1) // group,),
        out_shape=(pltpu.HBM((rows, width), BF), pltpu.HBM((wide, width + part), BF)),
        in_specs=[whole(a) for a in args],
        out_specs=(whole(tokens), pl.BlockSpec((wide, group * part), lambda b: (0, b))),
        scratch_shapes=[
            pltpu.VMEM((SUB, rows, part), BF), pltpu.VMEM((part // 128, wide, 128), F32),
        ],
        compiler_params=limit(24),
        name="dispatch",
    )(*args)


def ffn_kernel(x_ref, *refs):
    sources, (o_ref, wgu, wd, rows_ref, act, extra, sem) = refs[:6], refs[6:]
    j = pl.program_id(0)
    width = rows_ref.shape[1]
    part = width // SUB
    wide = x_ref.shape[0]
    blocks = wide // SUB
    hidden = act.shape[1] // 2
    copies = []
    for h in range(2):
        targets = (
            wgu.at[h, :, :hidden], wgu.at[h, :, hidden:], wd.at[h * hidden : (h + 1) * hidden]
        )
        for i, target in enumerate(targets):
            copies.append(pltpu.make_async_copy(sources[3 * h + i], target, sem.at[h, i]))

    @pl.when(j == 0)
    def _():
        for i in (0, 1, 3, 4, 2, 5):
            copies[i].start()

    rows_ref[:wide, :] = x_ref[:, :width]
    for i in range(part // 128):
        extra[i] = x_ref[:, width + i * 128 : width + (i + 1) * 128].astype(F32)
    for b in range(SUB):
        for i in range(part // 128):
            col = b * part + i * 128
            rows_ref[wide:, col : col + 128] = extra[i, pl.ds(b, blocks, stride=SUB), :].astype(BF)
    for h in range(2):

        @pl.when(j == 0)
        def _():
            copies[3 * h].wait()
            copies[3 * h + 1].wait()

        both = dot(rows_ref[...], wgu[h])
        gate = both[:, :hidden]
        silu = 0.5 * gate * (1.0 + jnp.tanh(0.5 * gate))
        act[:, h * hidden : (h + 1) * hidden] = (silu * both[:, hidden:]).astype(BF)

    @pl.when(j == 0)
    def _():
        copies[2].wait()
        copies[5].wait()

    total = dot(act[...], wd[...])
    o_ref[:, :width] = total[:wide].astype(BF)
    for b in range(SUB):
        for i in range(part // 128):
            col = b * part + i * 128
            extra[i, pl.ds(b, blocks, stride=SUB), :] = total[wide:, col : col + 128]
    for i in range(part // 128):
        o_ref[:, width + i * 128 : width + (i + 1) * 128] = extra[i].astype(BF)


def ffn(x, w0, w1):
    wide, packed = x.shape
    width, hidden = w0[0].shape
    step = 256
    rows = step + step // SUB
    block = pl.BlockSpec((step, packed), lambda j: (j, 0))
    return pl.pallas_call(
        ffn_kernel,
        grid=(wide // step,),
        out_shape=shape((wide, packed), BF),
        in_specs=[block] + [pl.BlockSpec(memory_space=pltpu.HBM)] * 6,
        out_specs=block,
        scratch_shapes=[
            pltpu.VMEM((2, width, 2 * hidden), BF),
            pltpu.VMEM((2 * hidden, width), BF),
            pltpu.VMEM((rows, width), BF),
            pltpu.VMEM((rows, 2 * hidden), BF),
            pltpu.VMEM((width // SUB // 128, step, 128), F32),
            pltpu.SemaphoreType.DMA((2, 3)),
        ],
        compiler_params=limit(40),
        name="ffn",
    )(x, *w0, *w1)


def combine_kernel(live_ref, r_ref, x_ref, wm_ref, wx_ref, h_ref, o_ref, extra):
    b = pl.program_id(0)
    rows, part = o_ref.shape
    blocks = r_ref.shape[0] // SUB

    @pl.when(b == 0)
    def _():
        for i in range(x_ref.shape[1] // 128):
            extra[i] = x_ref[:, i * 128 : (i + 1) * 128].astype(F32)

    each = x_ref.shape[1]
    more = [
        extra[i, pl.ds(b * (part // each) + n, blocks, stride=SUB), :]
        for n in range(part // each)
        for i in range(each // 128)
    ]
    more = jnp.concatenate(more, axis=1).astype(BF)
    both = dot(wm_ref[...], r_ref[...]) + dot(wx_ref[...], more)
    out = h_ref[...].astype(F32) + both[:rows] + both[rows:]
    row = lax.broadcasted_iota(jnp.int32, out.shape, 0)
    o_ref[...] = jnp.where(row < live_ref[0], out, 0.0).astype(BF)


def combine(live, back, wm, wx, hidden):
    rows, width = hidden.shape
    part = 2 * width // SUB
    wide = back.shape[0]
    whole = lambda a: pl.BlockSpec(a.shape, lambda b: (0, 0))
    cols = lambda n: pl.BlockSpec((n, part), lambda b: (0, b))
    return pl.pallas_call(
        combine_kernel,
        grid=(SUB // 2,),
        out_shape=shape((rows, width), BF),
        in_specs=[
            pl.BlockSpec(memory_space=pltpu.SMEM), cols(wide),
            pl.BlockSpec((wide, part // 2), lambda b: (0, SUB)), whole(wm), whole(wx), cols(rows),
        ],
        out_specs=cols(rows),
        scratch_shapes=[pltpu.VMEM((part // 256, wide, 128), F32)],
        compiler_params=limit(20),
        name="combine",
    )(live, back, back, wm, wx, hidden)


def layer(
    tokens, attn_gain, w_query, w_key, w_value, w_out, prefix_cache, group_of, lengths,
    moe_gain, w_gate, w_up, w_down, routes, route_weights,
):
    rows, width = tokens.shape
    zs = lax.axis_size("z")
    reqs = lax.axis_size("x") * lax.axis_size("y")
    experts = reqs * zs
    z = lax.axis_index("z")
    core = lax.axis_index("c")
    req = lax.axis_index("x") * lax.axis_size("y") + lax.axis_index("y")
    local = w_query.shape[1]
    up = [(i, (i + 1) % zs) for i in range(zs)]
    down = [(i, (i - 1) % zs) for i in range(zs)]
    swap = lambda v: lax.ppermute(v, "c", [(0, 1), (1, 0)])
    to_up = lambda v: lax.ppermute(v, "z", up)
    to_down = lambda v: lax.ppermute(v, "z", down)
    half = rows // 2

    part = pltpu.HBM((half, width), BF)
    normed, first, last = call(
        norm_kernel, (pltpu.HBM((rows, width), BF), part, part), 2, name="norm"
    )(away(tokens), away(attn_gain[None]))
    low0 = to_up(first)
    high1 = to_down(last)
    low1 = to_up(last)
    high0 = to_down(first)
    own_b = swap(normed)
    far0 = to_up(low0)
    far1 = to_down(high1)
    near_a = (low0, low1, high0, high1)
    near_b = tuple(swap(v) for v in near_a)
    far_b = swap(far0), swap(far1)

    wk = (w_key, swap(w_key))
    wq = (w_query, swap(w_query))
    wv = (w_value, swap(w_value))
    out_b = swap(w_out)

    spread = prefix_cache.shape[1]
    outgoing = pl.pallas_call(
        prefix_kernel,
        out_shape=pltpu.HBM((reqs * spread, 2 * local), BF),
        in_specs=[pl.BlockSpec(memory_space=pltpu.SMEM), vmem()],
        out_specs=vmem(),
        compiler_params=limit(16),
        name="prefix",
    )(group_of, jnp.transpose(prefix_cache, (0, 2, 1, 3)))
    pre_a = lax.all_to_all(outgoing, ("x", "y"), split_axis=0, concat_axis=0, tiled=True)
    pre_b = swap(pre_a)

    own_w = (w_gate[0], w_up[0], w_down[0])
    other_w = tuple(swap(w) for w in own_w)

    mine, yours = core * rows, (1 - core) * rows
    z_low, z_high, z_far = (z + zs - 1) % zs, (z + 1) % zs, (z + 2) % zs
    starts = jnp.stack(
        [chip * 2 * rows + who for who in (mine, yours) for chip in (z, z_low, z_high, z_far)]
    )
    place = (starts[:, None] + jnp.arange(rows, dtype=jnp.int32)).reshape(-1)
    spots = (PREFIX + place).astype(F32)
    freqs = 10000.0 ** (-(jnp.arange(HD // 2, dtype=F32) * 2.0) / HD)
    angles = spots[:, None] * freqs[None, :]
    cosine = jnp.cos(angles)
    sine = jnp.sin(angles)
    cosine = jnp.concatenate([cosine, cosine], axis=1)
    sine = jnp.concatenate([-sine, sine], axis=1)
    length = lengths[req]
    bias = jnp.where(place < length, 0.0, -1e30)[None, :]

    live = jnp.clip(length - (z * 2 + core) * rows, 0, rows).astype(jnp.int32)[None]
    routes, cosine, sine, bias, live = lax.optimization_barrier(
        (routes, cosine, sine, bias, live)
    )

    blocks = 2 * experts
    wide = blocks * SUB
    table, wm, wx = call(
        route_kernel,
        [
            pltpu.HBM((wide + blocks, rows), BF), pltpu.HBM((2 * rows, wide), BF),
            pltpu.HBM((2 * rows, blocks), BF),
        ],
        3,
        name="route",
    )(routes, routes.T, route_weights)

    far_b, table = lax.optimization_barrier((far_b, table))

    slots = 2 * zs * rows
    pieces = (normed, *near_a, far0, far1, own_b, *near_b, *far_b)
    q, k, v = pl.pallas_call(
        lambda *refs: qkv_kernel(len(pieces), *refs),
        out_shape=(
            pltpu.VMEM((slots // 2, 2 * local), BF),
            pltpu.VMEM((slots, 2 * local), BF),
            pltpu.VMEM((slots, 2 * local), BF),
        ),
        in_specs=[pl.BlockSpec(memory_space=pl.ANY)] * (len(pieces) + 6) + [vmem()] * 2,
        out_specs=(vmem(),) * 3,
        scratch_shapes=[
            pltpu.VMEM((slots, width), BF),
            pltpu.VMEM((3, width, 2 * local), BF),
            pltpu.SemaphoreType.DMA((len(pieces),)),
            pltpu.SemaphoreType.DMA((6,)),
        ],
        compiler_params=limit(24),
        name="qkv",
    )(*map(away, (*pieces, *wk, *wq, *wv, cosine, sine)))
    cache = (near(q), near(k), near(v), pre_a, pre_b, bias)
    scale = math.log2(math.e) / math.sqrt(HD)
    tmp = [pltpu.VMEM((rows, 2 * local), BF)]

    sum1, sum2 = call(
        functools.partial(attn_far_kernel, scale, 3 * rows),
        [shape((half, width), BF)] * 2,
        8,
        scratch_shapes=tmp,
        name="attn_far",
    )(*cache, w_out, out_b)
    got1 = to_up(sum1)
    got2 = to_down(sum2)
    part = shape((half, width), BF)
    wide_part = shape((half, width), F32)
    low_free, low_need, high_need, high_free = call(
        functools.partial(attn_near_kernel, scale, rows),
        [part, wide_part, wide_part, part],
        8,
        scratch_shapes=[pltpu.VMEM((2 * rows, 2 * local), BF)],
        name="attn_near",
    )(*cache, w_out, out_b)
    low_free = to_down(low_free)
    high_free = to_up(high_free)
    low_need, high_need = call(add_kernel, [part] * 2, 4, name="add")(
        low_need, got2, high_need, got1
    )
    low_need = to_down(low_need)
    high_need = to_up(high_need)
    own = call(
        functools.partial(attn_own_kernel, scale, 0),
        shape((rows, width), F32),
        8,
        scratch_shapes=tmp,
        name="attn_own",
    )(*cache, w_out, out_b)
    own, other_w = lax.optimization_barrier((own, other_w))

    hidden, send = dispatch(
        tokens, own, high_need, low_free, high_free, low_need, moe_gain[None], table
    )

    def exchange(v):
        return lax.all_to_all(
            v.reshape(experts, 2 * SUB, v.shape[1]), ("x", "y", "z"), 0, 0, tiled=True
        ).reshape(v.shape)

    back = exchange(ffn(exchange(send), own_w, other_w))
    return combine(live, back, wm, wx, hidden)


def solution(mesh):
    side = math.isqrt(mesh.shape["req"])
    grid = Mesh(
        mesh.devices.reshape(side, side, mesh.shape["exp"] // 2, 2), ("x", "y", "z", "c")
    )
    req, exp = ("x", "y"), ("z", "c")
    every = req + exp

    return jax.shard_map(
        layer,
        mesh=grid,
        in_specs=(
            P(every, None), P(), P(None, exp), P(None, exp), P(None, exp), P(exp, None),
            P(None, req, None, exp), P(), P(), P(),
            P(every, None, None), P(every, None, None), P(every, None, None),
            P(every, None), P(every, None),
        ),
        out_specs=P(every, None),
        check_vma=False,
    )
```

```python
import functools
import math

import jax
import jax.numpy as jnp
from jax import lax
from jax.experimental import pallas as pl
from jax.experimental.pallas import tpu as pltpu
from jax.sharding import Mesh
from jax.sharding import PartitionSpec as P


HD = 128
PREFIX = 1024
BF = jnp.bfloat16
F32 = jnp.float32
SUB = 8


def vmem():
    return pl.BlockSpec(memory_space=pltpu.VMEM)


def limit(mib):
    return pltpu.CompilerParams(vmem_limit_bytes=mib << 20)


def call(kernel, out_shape, n_in, mib=16, **kw):
    outs = jax.tree.map(lambda _: vmem(), out_shape)
    return pl.pallas_call(
        kernel, out_shape=out_shape, in_specs=[vmem()] * n_in, out_specs=outs,
        compiler_params=limit(mib), **kw
    )


def near(a):
    return pltpu.with_memory_space_constraint(a, pltpu.VMEM)


def away(a):
    return pltpu.with_memory_space_constraint(a, pltpu.HBM)


def shape(dims, dtype):
    return jax.ShapeDtypeStruct(dims, dtype)


def dot(a, b):
    return jnp.dot(a, b, preferred_element_type=F32)


def rms(wide, gain):
    return wide * lax.rsqrt(jnp.mean(wide * wide, axis=-1, keepdims=True) + 1e-05) * gain


def norm_kernel(x_ref, g_ref, o_ref, first_ref, last_ref):
    normed = rms(x_ref[...].astype(F32), g_ref[...]).astype(BF)
    o_ref[...] = normed
    half = first_ref.shape[0]
    first_ref[...] = normed[:half]
    last_ref[...] = normed[half:]


def facts_kernel(a_ref, b_ref, o_ref):
    for i in range(a_ref.shape[0]):
        o_ref[i] = a_ref[i]
    for i in range(b_ref.shape[0]):
        o_ref[a_ref.shape[0] + i] = b_ref[i]


def slots_of(index):
    block = index // SUB
    return block // 2, (block % 2) * (SUB + 1) + index % SUB


def route_kernel(rt_ref, wt_ref, dt_ref, wm_ref, wx_ref):
    top, rows = rt_ref.shape
    blocks = wx_ref.shape[1]
    experts = blocks // 2
    wide = blocks * SUB
    iota = lambda dims, axis: lax.broadcasted_iota(jnp.int32, dims, axis)
    one = lambda hit: jnp.where(hit, 1.0, 0.0)
    row_i = iota((rows, rows), 0)
    col_i = iota((rows, rows), 1)
    e_t = iota((experts, rows), 0)
    named_t = jnp.zeros((experts, rows), F32)
    weight_t = jnp.zeros((experts, rows), F32)
    for k in range(top):
        hit = rt_ref[k : k + 1, :] == e_t
        named_t += one(hit)
        weight_t += jnp.where(hit, wt_ref[k : k + 1, :], 0.0)
    rank_t = dot(named_t.astype(BF), one(row_i < col_i).astype(BF))
    rank_t = jnp.where(named_t > 0.5, rank_t, -1.0).astype(BF)
    expert, _ = slots_of(iota((wide, experts), 0))
    spread = one(expert == iota((wide, experts), 1)).astype(BF)
    _, slot = slots_of(iota((wide, rows), 0))
    dt_ref[:wide, :] = one(dot(spread, rank_t) == slot.astype(F32)).astype(BF)
    block = iota((blocks, experts), 0)
    spread = one(block // 2 == iota((blocks, experts), 1)).astype(BF)
    slot = (iota((blocks, rows), 0) % 2) * (SUB + 1) + SUB
    dt_ref[wide:, :] = one(dot(spread, rank_t) == slot.astype(F32)).astype(BF)
    named = jnp.transpose(named_t)
    weight = jnp.transpose(weight_t)
    rank = dot(one(col_i < row_i).astype(BF), named.astype(BF))
    rank = jnp.where(named > 0.5, rank, -1.0).astype(BF)
    high = weight.astype(BF)
    low = (weight - high.astype(F32)).astype(BF)
    expert, _ = slots_of(iota((experts, wide), 1))
    spread = one(expert == iota((experts, wide), 0)).astype(BF)
    _, slot = slots_of(iota((rows, wide), 1))
    hit = dot(rank, spread) == slot.astype(F32)
    wm_ref[:rows, :] = jnp.where(hit, dot(high, spread), 0.0).astype(BF)
    wm_ref[rows:, :] = jnp.where(hit, dot(low, spread), 0.0).astype(BF)
    block = iota((experts, blocks), 1)
    spread = one(block // 2 == iota((experts, blocks), 0)).astype(BF)
    slot = (iota((rows, blocks), 1) % 2) * (SUB + 1) + SUB
    hit = dot(rank, spread) == slot.astype(F32)
    wx_ref[:rows, :] = jnp.where(hit, dot(high, spread), 0.0).astype(BF)
    wx_ref[rows:, :] = jnp.where(hit, dot(low, spread), 0.0).astype(BF)


def prefix_kernel(group_ref, x_ref, o_ref):
    rows, width = x_ref.shape[2:]
    for r in range(o_ref.shape[0] // rows):
        for j in range(2):
            o_ref[r * rows : (r + 1) * rows, j * width : (j + 1) * width] = x_ref[group_ref[r], j]


def qkv_kernel(count, *refs):
    pieces, weights, refs = refs[:count], refs[count : count + 6], refs[count + 6 :]
    cos_ref, sin_ref, q_ref, k_ref, v_ref, x_ref, w_ref, x_sem, w_sem = refs
    at = 0
    copies = []
    for i, piece in enumerate(pieces):
        n = piece.shape[0]
        copies.append(pltpu.make_async_copy(piece, x_ref.at[at : at + n], x_sem.at[i]))
        at += n
    local = w_ref.shape[2] // 2
    loads = [
        pltpu.make_async_copy(
            w, w_ref.at[i // 2, :, i % 2 * local : (i % 2 + 1) * local], w_sem.at[i]
        )
        for i, w in enumerate(weights)
    ]
    for load in loads[:2]:
        load.start()
    for copy in copies:
        copy.start()
    for load in loads[2:]:
        load.start()
    half = q_ref.shape[0]
    at, left = 0, list(copies)
    for rows in (slice(0, half), slice(half, 2 * half)):
        while at < rows.stop:
            left.pop(0).wait()
            at += pieces[len(pieces) - len(left) - 1].shape[0]
        for i, o_ref in enumerate((k_ref, q_ref, v_ref)):
            if rows.start == 0:
                loads[2 * i].wait()
                loads[2 * i + 1].wait()
            elif o_ref is q_ref:
                continue
            mixed = dot(x_ref[rows, :], w_ref[i])
            if o_ref is v_ref:
                o_ref[rows, :] = mixed.astype(BF)
                continue
            for h in range(2 * local // HD):
                v = mixed[:, h * HD : (h + 1) * HD]
                turned = v * cos_ref[rows, :] + pltpu.roll(v, HD // 2, 1) * sin_ref[rows, :]
                o_ref[rows, h * HD : (h + 1) * HD] = turned.astype(BF)


def attend(scale, q_ref, k_ref, v_ref, pre_refs, bias_ref, o_ref, first):
    local = pre_refs[0].shape[1] // 2
    rows = o_ref.shape[0]
    nt = (((1,), (1,)), ((), ()))
    for h in range(q_ref.shape[1] // HD):
        side, col = divmod(h * HD, local)
        pre_ref = pre_refs[side]
        cols = slice(h * HD, (h + 1) * HD)
        q = q_ref[first : first + rows, cols]
        s1 = lax.dot_general(q, pre_ref[:, col : col + HD], nt, preferred_element_type=F32)
        s2 = lax.dot_general(q, k_ref[:, cols], nt, preferred_element_type=F32) + bias_ref[...]
        top = jnp.maximum(
            jnp.max(s1, axis=-1, keepdims=True), jnp.max(s2, axis=-1, keepdims=True)
        )
        e1 = jnp.exp2((s1 - top) * scale)
        e2 = jnp.exp2((s2 - top) * scale)
        total = jnp.sum(e1, axis=-1, keepdims=True) + jnp.sum(e2, axis=-1, keepdims=True)
        out = dot(e1.astype(BF), pre_ref[:, local + col : local + col + HD])
        out += dot(e2.astype(BF), v_ref[:, cols])
        o_ref[:, cols] = (out / total).astype(BF)


def project(a_ref, wa_ref, wb_ref):
    local = wa_ref.shape[0]
    return dot(a_ref[:, :local], wa_ref[...]) + dot(a_ref[:, local:], wb_ref[...])


def attn_far_kernel(scale, first, q, k, v, pa, pb, bias, wa, wb, o1, o2, tmp):
    attend(scale, q, k, v, (pa, pb), bias, tmp, first)
    total = project(tmp, wa, wb).astype(BF)
    rows = o1.shape[0]
    o1[...] = total[:rows]
    o2[...] = total[rows:]


def attn_near_kernel(
    scale, first, q, k, v, pa, pb, bias, wa, wb, low_free, low_need, high_need, high_free, tmp
):
    attend(scale, q, k, v, (pa, pb), bias, tmp, first)
    total = project(tmp, wa, wb)
    n = low_free.shape[0]
    for i, o_ref in enumerate((low_free, low_need, high_need, high_free)):
        o_ref[...] = total[i * n : (i + 1) * n].astype(o_ref.dtype)


def attn_own_kernel(scale, first, q, k, v, pa, pb, bias, wa, wb, o, tmp):
    attend(scale, q, k, v, (pa, pb), bias, tmp, first)
    o[...] = project(tmp, wa, wb)


def add_kernel(a_ref, a_got, b_ref, b_got, a_out, b_out):
    a_out[...] = (a_ref[...] + a_got[...].astype(F32)).astype(BF)
    b_out[...] = (b_ref[...] + b_got[...].astype(F32)).astype(BF)


def dispatch_kernel(
    t_ref, own_ref, a1, a2, b1, b2, g_ref, d_ref, h_ref, o_ref, normed, extra
):
    step = pl.program_id(0)
    part = normed.shape[2]
    group = o_ref.shape[1] // part
    wide = o_ref.shape[0]
    blocks = wide // SUB

    @pl.when(step == 0)
    def _():
        half = a1.shape[0]
        for at, x, y in ((0, a1, a2), (half, b1, b2)):
            here = slice(at, at + half)
            attn_out = own_ref[here, :] + x[...].astype(F32) + y[...].astype(F32)
            hidden = (t_ref[here, :].astype(F32) + attn_out).astype(BF)
            h_ref[here, :] = hidden
            rows = rms(hidden.astype(F32), g_ref[...]).astype(BF)
            for i in range(SUB):
                normed[i, here, :] = rows[:, i * part : (i + 1) * part]

    for i in range(group):
        b = step * group + i

        def columns(b=b, i=i):
            x = normed[b]
            o_ref[:, i * part : (i + 1) * part] = dot(d_ref[:wide, :], x).astype(BF)
            more = dot(d_ref[wide:, :], x)
            for n in range(part // 128):
                extra[n, pl.ds(b, blocks, stride=SUB), :] = more[:, n * 128 : (n + 1) * 128]

        if i < group - 1:
            columns()
            continue
        pl.when(b < SUB)(columns)

        @pl.when(b == SUB)
        def _():
            for n in range(part // 128):
                o_ref[:, i * part + n * 128 : i * part + (n + 1) * 128] = extra[n].astype(BF)


def dispatch(tokens, *rest):
    args = (tokens, *rest)
    table = rest[-1]
    rows, width = tokens.shape
    part = width // SUB
    group = 3
    wide = table.shape[0] // (SUB + 1) * SUB
    whole = lambda a: pl.BlockSpec(a.shape, lambda b: (0, 0))
    return pl.pallas_call(
        dispatch_kernel,
        grid=((SUB + 1) // group,),
        out_shape=(pltpu.HBM((rows, width), BF), pltpu.HBM((wide, width + part), BF)),
        in_specs=[whole(a) for a in args],
        out_specs=(whole(tokens), pl.BlockSpec((wide, group * part), lambda b: (0, b))),
        scratch_shapes=[
            pltpu.VMEM((SUB, rows, part), BF), pltpu.VMEM((part // 128, wide, 128), F32),
        ],
        compiler_params=limit(24),
        name="dispatch",
    )(*args)


def ffn_kernel(group, order_ref, x_hbm, *refs):
    sources = refs[:6]
    o_hbm, x_ref, o_ref, wgu, wd, rows_ref, act, extra, w_sem, x_sem, o_sem = refs[6:]
    j = pl.program_id(0)
    senders, each = x_hbm.shape[:2]
    width = rows_ref.shape[1]
    part = width // SUB
    wide = group * each
    blocks = wide // SUB
    hidden = act.shape[1] // 2
    steps = (order_ref[senders] + group - 1) // group
    copies = []
    for h in range(2):
        targets = (
            wgu.at[h, :, :hidden], wgu.at[h, :, hidden:], wd.at[h * hidden : (h + 1) * hidden]
        )
        for i, target in enumerate(targets):
            copies.append(pltpu.make_async_copy(sources[3 * h + i], target, w_sem.at[h, i]))

    def moves(step, inward):
        slot = step % 2
        out = []
        for s in range(group):
            sender = order_ref[step * group + s]
            here = pl.ds(s * each, each)
            if inward:
                ends = x_hbm.at[sender], x_ref.at[slot, here]
            else:
                ends = o_ref.at[slot, here], o_hbm.at[sender]
            out.append(pltpu.make_async_copy(*ends, (x_sem if inward else o_sem).at[slot, s]))
        return out

    def start(step, inward):
        for move in moves(step, inward):
            move.start()

    def wait(step, inward):
        for move in moves(step, inward):
            move.wait()

    @pl.when(j == 0)
    def _():
        copies[0].start()
        copies[1].start()
        start(0, True)
        for i in (3, 4, 2, 5):
            copies[i].start()

    @pl.when(j + 1 < steps)
    def _():
        start(j + 1, True)

    @pl.when(j < steps)
    def _():
        slot = j % 2
        wait(j, True)
        rows_ref[:wide, :] = x_ref[slot, :, :width]
        for i in range(part // 128):
            extra[i] = x_ref[slot, :, width + i * 128 : width + (i + 1) * 128].astype(F32)
        for b in range(SUB):
            for i in range(part // 128):
                col = b * part + i * 128
                rows_ref[wide:, col : col + 128] = extra[i, pl.ds(b, blocks, stride=SUB), :].astype(
                    BF
                )
        for h in range(2):

            @pl.when(j == 0)
            def _():
                copies[3 * h].wait()
                copies[3 * h + 1].wait()

            both = dot(rows_ref[...], wgu[h])
            gate = both[:, :hidden]
            silu = 0.5 * gate * (1.0 + jnp.tanh(0.5 * gate))
            act[:, h * hidden : (h + 1) * hidden] = (silu * both[:, hidden:]).astype(BF)

        @pl.when(j == 0)
        def _():
            copies[2].wait()
            copies[5].wait()

        @pl.when(j >= 2)
        def _():
            wait(j - 2, False)

        total = dot(act[...], wd[...])
        o_ref[slot, :, :width] = total[:wide].astype(BF)
        for b in range(SUB):
            for i in range(part // 128):
                col = b * part + i * 128
                extra[i, pl.ds(b, blocks, stride=SUB), :] = total[wide:, col : col + 128]
        for i in range(part // 128):
            o_ref[slot, :, width + i * 128 : width + (i + 1) * 128] = extra[i].astype(BF)
        start(j, False)

    @pl.when(j == pl.num_programs(0) - 1)
    def _():
        @pl.when(steps >= 2)
        def _():
            wait(steps - 2, False)

        @pl.when(steps >= 1)
        def _():
            wait(steps - 1, False)


def ffn(order, x, w0, w1):
    senders, each, packed = x.shape
    width, hidden = w0[0].shape
    group = 16
    wide = group * each
    rows = wide + wide // SUB
    any_space = pl.BlockSpec(memory_space=pl.ANY)
    return pl.pallas_call(
        functools.partial(ffn_kernel, group),
        grid=(senders // group,),
        out_shape=pltpu.HBM(x.shape, BF),
        in_specs=[pl.BlockSpec(memory_space=pltpu.SMEM)] + [any_space] * 7,
        out_specs=any_space,
        scratch_shapes=[
            pltpu.VMEM((2, wide, packed), BF),
            pltpu.VMEM((2, wide, packed), BF),
            pltpu.VMEM((2, width, 2 * hidden), BF),
            pltpu.VMEM((2 * hidden, width), BF),
            pltpu.VMEM((rows, width), BF),
            pltpu.VMEM((rows, 2 * hidden), BF),
            pltpu.VMEM((width // SUB // 128, wide, 128), F32),
            pltpu.SemaphoreType.DMA((2, 3)),
            pltpu.SemaphoreType.DMA((2, group)),
            pltpu.SemaphoreType.DMA((2, group)),
        ],
        compiler_params=limit(40),
        name="ffn",
    )(order, *map(away, (x, *w0, *w1)))


def combine_kernel(live_ref, r_ref, x_ref, wm_ref, wx_ref, h_ref, o_ref, extra):
    b = pl.program_id(0)
    rows, part = o_ref.shape
    blocks = r_ref.shape[0] // SUB

    @pl.when(b == 0)
    def _():
        for i in range(x_ref.shape[1] // 128):
            extra[i] = x_ref[:, i * 128 : (i + 1) * 128].astype(F32)

    each = x_ref.shape[1]
    more = [
        extra[i, pl.ds(b * (part // each) + n, blocks, stride=SUB), :]
        for n in range(part // each)
        for i in range(each // 128)
    ]
    more = jnp.concatenate(more, axis=1).astype(BF)
    both = dot(wm_ref[...], r_ref[...]) + dot(wx_ref[...], more)
    out = h_ref[...].astype(F32) + both[:rows] + both[rows:]
    row = lax.broadcasted_iota(jnp.int32, out.shape, 0)
    o_ref[...] = jnp.where(row < live_ref[0], out, 0.0).astype(BF)


def combine(live, back, wm, wx, hidden):
    rows, width = hidden.shape
    part = 2 * width // SUB
    wide = back.shape[0]
    whole = lambda a: pl.BlockSpec(a.shape, lambda b: (0, 0))
    cols = lambda n: pl.BlockSpec((n, part), lambda b: (0, b))
    return pl.pallas_call(
        combine_kernel,
        grid=(SUB // 2,),
        out_shape=shape((rows, width), BF),
        in_specs=[
            pl.BlockSpec(memory_space=pltpu.SMEM), cols(wide),
            pl.BlockSpec((wide, part // 2), lambda b: (0, SUB)), whole(wm), whole(wx), cols(rows),
        ],
        out_specs=cols(rows),
        scratch_shapes=[pltpu.VMEM((part // 256, wide, 128), F32)],
        compiler_params=limit(20),
        name="combine",
    )(live, back, back, wm, wx, hidden)


def layer(
    tokens, attn_gain, w_query, w_key, w_value, w_out, prefix_cache, group_of, lengths,
    moe_gain, w_gate, w_up, w_down, routes, route_weights,
):
    rows, width = tokens.shape
    zs = lax.axis_size("z")
    reqs = lax.axis_size("x") * lax.axis_size("y")
    experts = reqs * zs
    z = lax.axis_index("z")
    core = lax.axis_index("c")
    req = lax.axis_index("x") * lax.axis_size("y") + lax.axis_index("y")
    local = w_query.shape[1]
    up = [(i, (i + 1) % zs) for i in range(zs)]
    down = [(i, (i - 1) % zs) for i in range(zs)]
    swap = lambda v: lax.ppermute(v, "c", [(0, 1), (1, 0)])
    to_up = lambda v: lax.ppermute(v, "z", up)
    to_down = lambda v: lax.ppermute(v, "z", down)
    half = rows // 2

    part = pltpu.HBM((half, width), BF)
    normed, first, last = call(
        norm_kernel, (pltpu.HBM((rows, width), BF), part, part), 2, name="norm"
    )(away(tokens), away(attn_gain[None]))
    low0 = to_up(first)
    high1 = to_down(last)
    low1 = to_up(last)
    high0 = to_down(first)
    own_b = swap(normed)
    far0 = to_up(low0)
    far1 = to_down(high1)
    smem = pl.BlockSpec(memory_space=pltpu.SMEM)
    facts = pl.pallas_call(
        facts_kernel,
        out_shape=shape((reqs + 2,), jnp.int32),
        in_specs=[smem] * 2,
        out_specs=smem,
        compiler_params=limit(2),
        name="facts",
    )(lengths, jnp.stack([z, core]))
    lengths, z, core = facts[:reqs], facts[reqs], facts[reqs + 1]
    near_a = (low0, low1, high0, high1)
    near_b = tuple(swap(v) for v in near_a)

    wk = (w_key, swap(w_key))
    wq = (w_query, swap(w_query))
    wv = (w_value, swap(w_value))
    out_b = swap(w_out)

    spread = prefix_cache.shape[1]
    outgoing = pl.pallas_call(
        prefix_kernel,
        out_shape=pltpu.HBM((reqs * spread, 2 * local), BF),
        in_specs=[pl.BlockSpec(memory_space=pltpu.SMEM), vmem()],
        out_specs=vmem(),
        compiler_params=limit(16),
        name="prefix",
    )(group_of, jnp.transpose(prefix_cache, (0, 2, 1, 3)))
    pre_a = lax.all_to_all(outgoing, ("x", "y"), split_axis=0, concat_axis=0, tiled=True)
    pre_b = swap(pre_a)

    own_w = (w_gate[0], w_up[0], w_down[0])
    other_w = tuple(swap(w) for w in own_w)

    mine, yours = core * rows, (1 - core) * rows
    z_low, z_high, z_far = (z + zs - 1) % zs, (z + 1) % zs, (z + 2) % zs
    starts = jnp.stack(
        [chip * 2 * rows + who for who in (mine, yours) for chip in (z, z_low, z_high, z_far)]
    )
    place = (starts[:, None] + jnp.arange(rows, dtype=jnp.int32)).reshape(-1)
    spots = (PREFIX + place).astype(F32)
    freqs = 10000.0 ** (-(jnp.arange(HD // 2, dtype=F32) * 2.0) / HD)
    angles = spots[:, None] * freqs[None, :]
    cosine = jnp.cos(angles)
    sine = jnp.sin(angles)
    cosine = jnp.concatenate([cosine, cosine], axis=1)
    sine = jnp.concatenate([-sine, sine], axis=1)
    length = lengths[req]
    bias = jnp.where(place < length, 0.0, -1e30)[None, :]

    live = jnp.clip(length - (z * 2 + core) * rows, 0, rows).astype(jnp.int32)[None]
    sender = jnp.arange(experts, dtype=jnp.int32)
    each = jnp.broadcast_to(lengths[:, None], (reqs, zs)).reshape(-1)
    full = each > (sender % zs * 2 + core) * rows
    before = sender[None, :] < sender[:, None]
    count = jnp.sum(full.astype(jnp.int32))
    rank = jnp.where(
        full,
        jnp.sum((before & full[None, :]).astype(jnp.int32), axis=1),
        count + jnp.sum((before & ~full[None, :]).astype(jnp.int32), axis=1),
    )
    order = jnp.sum(jnp.where(rank[None, :] == sender[:, None], sender[None, :], 0), axis=1)
    order = jnp.concatenate([order, count[None]])
    far0, far1, cosine, sine, bias, live, order = lax.optimization_barrier(
        (far0, far1, cosine, sine, bias, live, order)
    )
    far_b = swap(far0), swap(far1)


    slots = 2 * zs * rows
    pieces = (normed, *near_a, far0, far1, own_b, *near_b, *far_b)
    q, k, v = pl.pallas_call(
        lambda *refs: qkv_kernel(len(pieces), *refs),
        out_shape=(
            pltpu.VMEM((slots // 2, 2 * local), BF),
            pltpu.VMEM((slots, 2 * local), BF),
            pltpu.VMEM((slots, 2 * local), BF),
        ),
        in_specs=[pl.BlockSpec(memory_space=pl.ANY)] * (len(pieces) + 6) + [vmem()] * 2,
        out_specs=(vmem(),) * 3,
        scratch_shapes=[
            pltpu.VMEM((slots, width), BF),
            pltpu.VMEM((3, width, 2 * local), BF),
            pltpu.SemaphoreType.DMA((len(pieces),)),
            pltpu.SemaphoreType.DMA((6,)),
        ],
        compiler_params=limit(24),
        name="qkv",
    )(*map(away, (*pieces, *wk, *wq, *wv, cosine, sine)))
    cache = (near(q), near(k), near(v), pre_a, pre_b, bias)
    scale = math.log2(math.e) / math.sqrt(HD)
    tmp = [pltpu.VMEM((rows, 2 * local), BF)]

    sum1, sum2 = call(
        functools.partial(attn_far_kernel, scale, 3 * rows),
        [shape((half, width), BF)] * 2,
        8,
        scratch_shapes=tmp,
        name="attn_far",
    )(*cache, w_out, out_b)
    got1 = to_up(sum1)
    got2 = to_down(sum2)
    part = shape((half, width), BF)
    wide_part = shape((half, width), F32)
    low_free, low_need, high_need, high_free = call(
        functools.partial(attn_near_kernel, scale, rows),
        [part, wide_part, wide_part, part],
        8,
        scratch_shapes=[pltpu.VMEM((2 * rows, 2 * local), BF)],
        name="attn_near",
    )(*cache, w_out, out_b)
    low_free = to_down(low_free)
    high_free = to_up(high_free)
    low_need, high_need = call(add_kernel, [part] * 2, 4, name="add")(
        low_need, got2, high_need, got1
    )
    low_need = to_down(low_need)
    high_need = to_up(high_need)
    own = call(
        functools.partial(attn_own_kernel, scale, 0),
        shape((rows, width), F32),
        8,
        scratch_shapes=tmp,
        name="attn_own",
    )(*cache, w_out, out_b)
    own, other_w = lax.optimization_barrier((own, other_w))

    blocks = 2 * experts
    wide = blocks * SUB
    table, wm, wx = call(
        route_kernel,
        [
            pltpu.HBM((wide + blocks, rows), BF), pltpu.HBM((2 * rows, wide), BF),
            pltpu.HBM((2 * rows, blocks), BF),
        ],
        2,
        name="route",
    )(away(routes.T), away(route_weights.T))

    hidden, send = dispatch(
        tokens, own, high_need, low_free, high_free, low_need, moe_gain[None], away(table)
    )

    def exchange(v):
        return lax.all_to_all(v, ("x", "y", "z"), 0, 0, tiled=True)

    got = exchange(send.reshape(experts, 2 * SUB, send.shape[1]))
    back = exchange(ffn(order, got, own_w, other_w)).reshape(send.shape)
    return combine(live, back, wm, wx, hidden)


def solution(mesh):
    side = math.isqrt(mesh.shape["req"])
    grid = Mesh(
        mesh.devices.reshape(side, side, mesh.shape["exp"] // 2, 2), ("x", "y", "z", "c")
    )
    req, exp = ("x", "y"), ("z", "c")
    every = req + exp

    return jax.shard_map(
        layer,
        mesh=grid,
        in_specs=(
            P(every, None), P(), P(None, exp), P(None, exp), P(None, exp), P(exp, None),
            P(None, req, None, exp), P(), P(), P(),
            P(every, None, None), P(every, None, None), P(every, None, None),
            P(every, None), P(every, None),
        ),
        out_specs=P(every, None),
        check_vma=False,
    )
```

```python
import functools
import math

import jax
import jax.numpy as jnp
import numpy as np
from jax import lax
from jax.experimental import pallas as pl
from jax.experimental.pallas import tpu as pltpu
from jax.sharding import Mesh
from jax.sharding import PartitionSpec as P


HD = 128
PREFIX = 1024
BF = jnp.bfloat16
F32 = jnp.float32
SUB = 8


def vmem():
    return pl.BlockSpec(memory_space=pltpu.VMEM)


def limit(mib):
    return pltpu.CompilerParams(vmem_limit_bytes=mib << 20)


def smem():
    return pl.BlockSpec(memory_space=pltpu.SMEM)


def call(kernel, out_shape, n_in, mib=16, lengths=0, **kw):
    outs = jax.tree.map(lambda _: vmem(), out_shape)
    return pl.pallas_call(
        kernel, out_shape=out_shape, in_specs=[vmem()] * n_in + [smem()] * lengths,
        out_specs=outs, compiler_params=limit(mib), **kw
    )


def near(a):
    return pltpu.with_memory_space_constraint(a, pltpu.VMEM)


def away(a):
    return pltpu.with_memory_space_constraint(a, pltpu.HBM)


def shape(dims, dtype):
    return jax.ShapeDtypeStruct(dims, dtype)


def dot(a, b):
    return jnp.dot(a, b, preferred_element_type=F32)


def rms(wide, gain):
    return wide * lax.rsqrt(jnp.mean(wide * wide, axis=-1, keepdims=True) + 1e-05) * gain


def norm_kernel(x_ref, g_ref, o_ref, first_ref, last_ref):
    normed = rms(x_ref[...].astype(F32), g_ref[...]).astype(BF)
    o_ref[...] = normed
    half = first_ref.shape[0]
    first_ref[...] = normed[:half]
    last_ref[...] = normed[half:]


def seat():
    req = lax.axis_index("x") * lax.axis_size("y") + lax.axis_index("y")
    return req, lax.axis_index("z"), lax.axis_index("c")


def held_blocks():
    _, z, core = seat()
    zs = lax.axis_size("z")
    chips = [lax.rem(z + d, zs) for d in (0, zs - 1, 1, 2)]
    return [chip * 2 + who for who in (core, 1 - core) for chip in chips]


def tables(rows, blocks):
    freqs = 10000.0 ** (-(np.arange(HD // 2) * 2.0) / HD)
    freqs = np.concatenate([freqs, freqs])
    first = (PREFIX + rows * np.arange(blocks))[:, None] * freqs
    within = np.arange(rows)[:, None] * freqs
    return [f(a).astype(np.float32) for a in (first, within) for f in (np.cos, np.sin)]


def slots_of(index):
    block = index // SUB
    return block // 2, (block % 2) * (SUB + 1) + index % SUB


def route_kernel(zs, len_ref, rt_ref, wt_ref, dt_ref, wm_ref, wx_ref, order_ref):
    top, rows = rt_ref.shape
    _, _, core = seat()
    senders = order_ref.shape[0] - 1

    def pick(wanted):
        def step(s, n):
            full = len_ref[s // zs] > (s % zs * 2 + core) * rows
            take = full == wanted

            @pl.when(take)
            def _():
                order_ref[n] = s

            return n + take.astype(jnp.int32)

        return step

    count = lax.fori_loop(0, senders, pick(True), jnp.int32(0))
    order_ref[senders] = count
    lax.fori_loop(0, senders, pick(False), count)
    blocks = wx_ref.shape[1]
    experts = blocks // 2
    wide = blocks * SUB
    iota = lambda dims, axis: lax.broadcasted_iota(jnp.int32, dims, axis)
    one = lambda hit: jnp.where(hit, 1.0, 0.0)
    row_i = iota((rows, rows), 0)
    col_i = iota((rows, rows), 1)
    e_t = iota((experts, rows), 0)
    named_t = jnp.zeros((experts, rows), F32)
    weight_t = jnp.zeros((experts, rows), F32)
    for k in range(top):
        hit = rt_ref[k : k + 1, :] == e_t
        named_t += one(hit)
        weight_t += jnp.where(hit, wt_ref[k : k + 1, :], 0.0)
    rank_t = dot(named_t.astype(BF), one(row_i < col_i).astype(BF))
    rank_t = jnp.where(named_t > 0.5, rank_t, -1.0).astype(BF)
    expert, _ = slots_of(iota((wide, experts), 0))
    spread = one(expert == iota((wide, experts), 1)).astype(BF)
    _, slot = slots_of(iota((wide, rows), 0))
    dt_ref[:wide, :] = one(dot(spread, rank_t) == slot.astype(F32)).astype(BF)
    block = iota((blocks, experts), 0)
    spread = one(block // 2 == iota((blocks, experts), 1)).astype(BF)
    slot = (iota((blocks, rows), 0) % 2) * (SUB + 1) + SUB
    dt_ref[wide:, :] = one(dot(spread, rank_t) == slot.astype(F32)).astype(BF)
    named = jnp.transpose(named_t)
    weight = jnp.transpose(weight_t)
    rank = dot(one(col_i < row_i).astype(BF), named.astype(BF))
    rank = jnp.where(named > 0.5, rank, -1.0).astype(BF)
    high = weight.astype(BF)
    low = (weight - high.astype(F32)).astype(BF)
    expert, _ = slots_of(iota((experts, wide), 1))
    spread = one(expert == iota((experts, wide), 0)).astype(BF)
    _, slot = slots_of(iota((rows, wide), 1))
    hit = dot(rank, spread) == slot.astype(F32)
    wm_ref[:rows, :] = jnp.where(hit, dot(high, spread), 0.0).astype(BF)
    wm_ref[rows:, :] = jnp.where(hit, dot(low, spread), 0.0).astype(BF)
    block = iota((experts, blocks), 1)
    spread = one(block // 2 == iota((experts, blocks), 0)).astype(BF)
    slot = (iota((rows, blocks), 1) % 2) * (SUB + 1) + SUB
    hit = dot(rank, spread) == slot.astype(F32)
    wx_ref[:rows, :] = jnp.where(hit, dot(high, spread), 0.0).astype(BF)
    wx_ref[rows:, :] = jnp.where(hit, dot(low, spread), 0.0).astype(BF)


def prefix_kernel(group_ref, x_ref, o_ref):
    rows, width = x_ref.shape[2:]
    for r in range(o_ref.shape[0] // rows):
        for j in range(2):
            o_ref[r * rows : (r + 1) * rows, j * width : (j + 1) * width] = x_ref[group_ref[r], j]


def qkv_kernel(count, *refs):
    pieces, weights, refs = refs[:count], refs[count : count + 6], refs[count + 6 :]
    c0_ref, s0_ref, c1_ref, s1_ref, q_ref, k_ref, v_ref, x_ref, w_ref = refs[:9]
    cos_ref, sin_ref, x_sem, w_sem = refs[9:]
    at = 0
    copies = []
    for i, piece in enumerate(pieces):
        n = piece.shape[0]
        copies.append(pltpu.make_async_copy(piece, x_ref.at[at : at + n], x_sem.at[i]))
        at += n
    local = w_ref.shape[2] // 2
    loads = [
        pltpu.make_async_copy(
            w, w_ref.at[i // 2, :, i % 2 * local : (i % 2 + 1) * local], w_sem.at[i]
        )
        for i, w in enumerate(weights)
    ]
    for load in loads[:2]:
        load.start()
    for copy in copies:
        copy.start()
    for load in loads[2:]:
        load.start()
    n = c1_ref.shape[0]
    side = jnp.where(lax.broadcasted_iota(jnp.int32, (n, HD), 1) < HD // 2, -1.0, 1.0)
    for i, block in enumerate(held_blocks()):
        c0, s0 = c0_ref[pl.ds(block, 1), :], s0_ref[pl.ds(block, 1), :]
        here = slice(i * n, (i + 1) * n)
        cos_ref[here, :] = c0 * c1_ref[...] - s0 * s1_ref[...]
        sin_ref[here, :] = side * (s0 * c1_ref[...] + c0 * s1_ref[...])
    half = q_ref.shape[0]
    at, left = 0, list(copies)
    for rows in (slice(0, half), slice(half, 2 * half)):
        while at < rows.stop:
            left.pop(0).wait()
            at += pieces[len(pieces) - len(left) - 1].shape[0]
        for i, o_ref in enumerate((k_ref, q_ref, v_ref)):
            if rows.start == 0:
                loads[2 * i].wait()
                loads[2 * i + 1].wait()
            elif o_ref is q_ref:
                continue
            mixed = dot(x_ref[rows, :], w_ref[i])
            if o_ref is v_ref:
                o_ref[rows, :] = mixed.astype(BF)
                continue
            for h in range(2 * local // HD):
                v = mixed[:, h * HD : (h + 1) * HD]
                turned = v * cos_ref[rows, :] + pltpu.roll(v, HD // 2, 1) * sin_ref[rows, :]
                o_ref[rows, h * HD : (h + 1) * HD] = turned.astype(BF)


def attend(scale, q_ref, k_ref, v_ref, pre_refs, len_ref, o_ref, first):
    req, _, _ = seat()
    blocks = held_blocks()
    n = k_ref.shape[0] // len(blocks)
    lane = lax.broadcasted_iota(jnp.int32, (1, n), 1)
    bias = jnp.concatenate(
        [jnp.where(block * n + lane < len_ref[req], 0.0, -1e30) for block in blocks], axis=1
    )
    local = pre_refs[0].shape[1] // 2
    rows = o_ref.shape[0]
    nt = (((1,), (1,)), ((), ()))
    for h in range(q_ref.shape[1] // HD):
        side, col = divmod(h * HD, local)
        pre_ref = pre_refs[side]
        cols = slice(h * HD, (h + 1) * HD)
        q = q_ref[first : first + rows, cols]
        s1 = lax.dot_general(q, pre_ref[:, col : col + HD], nt, preferred_element_type=F32)
        s2 = lax.dot_general(q, k_ref[:, cols], nt, preferred_element_type=F32) + bias
        top = jnp.maximum(
            jnp.max(s1, axis=-1, keepdims=True), jnp.max(s2, axis=-1, keepdims=True)
        )
        e1 = jnp.exp2((s1 - top) * scale)
        e2 = jnp.exp2((s2 - top) * scale)
        total = jnp.sum(e1, axis=-1, keepdims=True) + jnp.sum(e2, axis=-1, keepdims=True)
        out = dot(e1.astype(BF), pre_ref[:, local + col : local + col + HD])
        out += dot(e2.astype(BF), v_ref[:, cols])
        o_ref[:, cols] = (out / total).astype(BF)


def project(a_ref, wa_ref, wb_ref):
    local = wa_ref.shape[0]
    return dot(a_ref[:, :local], wa_ref[...]) + dot(a_ref[:, local:], wb_ref[...])


def attn_far_kernel(scale, first, q, k, v, pa, pb, wa, wb, lens, o1, o2, tmp):
    attend(scale, q, k, v, (pa, pb), lens, tmp, first)
    total = project(tmp, wa, wb).astype(BF)
    rows = o1.shape[0]
    o1[...] = total[:rows]
    o2[...] = total[rows:]


def attn_near_kernel(
    scale, first, q, k, v, pa, pb, wa, wb, lens, low_free, low_need, high_need, high_free, tmp
):
    attend(scale, q, k, v, (pa, pb), lens, tmp, first)
    total = project(tmp, wa, wb)
    n = low_free.shape[0]
    for i, o_ref in enumerate((low_free, low_need, high_need, high_free)):
        o_ref[...] = total[i * n : (i + 1) * n].astype(o_ref.dtype)


def attn_own_kernel(scale, first, q, k, v, pa, pb, wa, wb, lens, o, tmp):
    attend(scale, q, k, v, (pa, pb), lens, tmp, first)
    o[...] = project(tmp, wa, wb)


def add_kernel(a_ref, a_got, b_ref, b_got, a_out, b_out):
    a_out[...] = (a_ref[...] + a_got[...].astype(F32)).astype(BF)
    b_out[...] = (b_ref[...] + b_got[...].astype(F32)).astype(BF)


def dispatch_kernel(
    t_ref, own_ref, a1, a2, b1, b2, g_ref, d_ref, h_ref, o_ref, normed, extra
):
    step = pl.program_id(0)
    part = normed.shape[2]
    group = o_ref.shape[1] // part
    wide = o_ref.shape[0]
    blocks = wide // SUB

    @pl.when(step == 0)
    def _():
        half = a1.shape[0]
        for at, x, y in ((0, a1, a2), (half, b1, b2)):
            here = slice(at, at + half)
            attn_out = own_ref[here, :] + x[...].astype(F32) + y[...].astype(F32)
            hidden = (t_ref[here, :].astype(F32) + attn_out).astype(BF)
            h_ref[here, :] = hidden
            rows = rms(hidden.astype(F32), g_ref[...]).astype(BF)
            for i in range(SUB):
                normed[i, here, :] = rows[:, i * part : (i + 1) * part]

    for i in range(group):
        b = step * group + i

        def columns(b=b, i=i):
            x = normed[b]
            o_ref[:, i * part : (i + 1) * part] = dot(d_ref[:wide, :], x).astype(BF)
            more = dot(d_ref[wide:, :], x)
            for n in range(part // 128):
                extra[n, pl.ds(b, blocks, stride=SUB), :] = more[:, n * 128 : (n + 1) * 128]

        if i < group - 1:
            columns()
            continue
        pl.when(b < SUB)(columns)

        @pl.when(b == SUB)
        def _():
            for n in range(part // 128):
                o_ref[:, i * part + n * 128 : i * part + (n + 1) * 128] = extra[n].astype(BF)


def dispatch(tokens, *rest):
    args = (tokens, *rest)
    table = rest[-1]
    rows, width = tokens.shape
    part = width // SUB
    group = 3
    wide = table.shape[0] // (SUB + 1) * SUB
    whole = lambda a: pl.BlockSpec(a.shape, lambda b: (0, 0))
    return pl.pallas_call(
        dispatch_kernel,
        grid=((SUB + 1) // group,),
        out_shape=(pltpu.HBM((rows, width), BF), pltpu.HBM((wide, width + part), BF)),
        in_specs=[whole(a) for a in args],
        out_specs=(whole(tokens), pl.BlockSpec((wide, group * part), lambda b: (0, b))),
        scratch_shapes=[
            pltpu.VMEM((SUB, rows, part), BF), pltpu.VMEM((part // 128, wide, 128), F32),
        ],
        compiler_params=limit(24),
        name="dispatch",
    )(*args)


def ffn_kernel(group, order_ref, x_hbm, *refs):
    weights = refs[:3], refs[3:6]
    o_hbm, x_ref, o_ref, rows_ref, act, extra, x_sem, o_sem = refs[6:]
    senders, each = x_hbm.shape[:2]
    width = rows_ref.shape[1]
    part = width // SUB
    wide = group * each
    blocks = wide // SUB
    hidden = act.shape[1] // 2
    steps = (order_ref[senders] + group - 1) // group

    def moves(step, inward):
        slot = step % 2
        out = []
        for s in range(group):
            sender = order_ref[step * group + s]
            here = pl.ds(s * each, each)
            if inward:
                ends = x_hbm.at[sender], x_ref.at[slot, here]
            else:
                ends = o_ref.at[slot, here], o_hbm.at[sender]
            out.append(pltpu.make_async_copy(*ends, (x_sem if inward else o_sem).at[slot, s]))
        return out

    def start(step, inward):
        for move in moves(step, inward):
            move.start()

    def wait(step, inward):
        for move in moves(step, inward):
            move.wait()

    @pl.when(steps > 0)
    def _():
        start(0, True)

    def body(j, carry):
        slot = j % 2

        @pl.when(j + 1 < steps)
        def _():
            start(j + 1, True)

        wait(j, True)
        rows_ref[:wide, :] = x_ref[slot, :, :width]
        for i in range(part // 128):
            extra[i] = x_ref[slot, :, width + i * 128 : width + (i + 1) * 128].astype(F32)
        for b in range(SUB):
            for i in range(part // 128):
                col = b * part + i * 128
                rows_ref[wide:, col : col + 128] = extra[i, pl.ds(b, blocks, stride=SUB), :].astype(
                    BF
                )
        for h, (g_ref, u_ref, _) in enumerate(weights):
            gate = dot(rows_ref[...], g_ref[...])
            silu = 0.5 * gate * (1.0 + jnp.tanh(0.5 * gate))
            upper = dot(rows_ref[...], u_ref[...])
            act[:, h * hidden : (h + 1) * hidden] = (silu * upper).astype(BF)

        @pl.when(j >= 2)
        def _():
            wait(j - 2, False)

        total = dot(act[:, :hidden], weights[0][2][...])
        total += dot(act[:, hidden:], weights[1][2][...])
        o_ref[slot, :, :width] = total[:wide].astype(BF)
        for b in range(SUB):
            for i in range(part // 128):
                col = b * part + i * 128
                extra[i, pl.ds(b, blocks, stride=SUB), :] = total[wide:, col : col + 128]
        for i in range(part // 128):
            o_ref[slot, :, width + i * 128 : width + (i + 1) * 128] = extra[i].astype(BF)
        start(j, False)
        return carry

    lax.fori_loop(0, steps, body, 0)

    @pl.when(steps >= 2)
    def _():
        wait(steps - 2, False)

    @pl.when(steps >= 1)
    def _():
        wait(steps - 1, False)


def ffn(order, x, w0, w1):
    _, each, packed = x.shape
    width, hidden = w0[0].shape
    group = 16
    wide = group * each
    rows = wide + wide // SUB
    any_space = pl.BlockSpec(memory_space=pl.ANY)
    return pl.pallas_call(
        functools.partial(ffn_kernel, group),
        out_shape=pltpu.HBM(x.shape, BF),
        in_specs=[smem(), any_space] + [vmem()] * 6,
        out_specs=any_space,
        scratch_shapes=[
            pltpu.VMEM((2, wide, packed), BF),
            pltpu.VMEM((2, wide, packed), BF),
            pltpu.VMEM((rows, width), BF),
            pltpu.VMEM((rows, 2 * hidden), BF),
            pltpu.VMEM((width // SUB // 128, wide, 128), F32),
            pltpu.SemaphoreType.DMA((2, group)),
            pltpu.SemaphoreType.DMA((2, group)),
        ],
        compiler_params=limit(24),
        name="ffn",
    )(order, away(x), *map(near, (*w0, *w1)))


def combine_kernel(len_ref, r_ref, x_ref, wm_ref, wx_ref, h_ref, o_ref, extra):
    b = pl.program_id(0)
    rows, part = o_ref.shape
    blocks = r_ref.shape[0] // SUB

    @pl.when(b == 0)
    def _():
        for i in range(x_ref.shape[1] // 128):
            extra[i] = x_ref[:, i * 128 : (i + 1) * 128].astype(F32)

    each = x_ref.shape[1]
    more = [
        extra[i, pl.ds(b * (part // each) + n, blocks, stride=SUB), :]
        for n in range(part // each)
        for i in range(each // 128)
    ]
    more = jnp.concatenate(more, axis=1).astype(BF)
    both = dot(wm_ref[...], r_ref[...]) + dot(wx_ref[...], more)
    out = h_ref[...].astype(F32) + both[:rows] + both[rows:]
    row = lax.broadcasted_iota(jnp.int32, out.shape, 0)
    req, z, core = seat()
    live = len_ref[req] - (z * 2 + core) * rows
    o_ref[...] = jnp.where(row < live, out, 0.0).astype(BF)


def combine(lengths, back, wm, wx, hidden):
    rows, width = hidden.shape
    part = 2 * width // SUB
    wide = back.shape[0]
    whole = lambda a: pl.BlockSpec(a.shape, lambda b: (0, 0))
    cols = lambda n: pl.BlockSpec((n, part), lambda b: (0, b))
    return pl.pallas_call(
        combine_kernel,
        grid=(SUB // 2,),
        out_shape=shape((rows, width), BF),
        in_specs=[
            pl.BlockSpec(memory_space=pltpu.SMEM), cols(wide),
            pl.BlockSpec((wide, part // 2), lambda b: (0, SUB)), whole(wm), whole(wx), cols(rows),
        ],
        out_specs=cols(rows),
        scratch_shapes=[pltpu.VMEM((part // 256, wide, 128), F32)],
        compiler_params=limit(20),
        name="combine",
    )(lengths, back, back, wm, wx, hidden)


def layer(
    tokens, attn_gain, w_query, w_key, w_value, w_out, prefix_cache, group_of, lengths,
    moe_gain, w_gate, w_up, w_down, routes, route_weights,
):
    rows, width = tokens.shape
    zs = lax.axis_size("z")
    reqs = lax.axis_size("x") * lax.axis_size("y")
    experts = reqs * zs
    local = w_query.shape[1]
    up = [(i, (i + 1) % zs) for i in range(zs)]
    down = [(i, (i - 1) % zs) for i in range(zs)]
    swap = lambda v: lax.ppermute(v, "c", [(0, 1), (1, 0)])
    to_up = lambda v: lax.ppermute(v, "z", up)
    to_down = lambda v: lax.ppermute(v, "z", down)
    half = rows // 2

    part = pltpu.HBM((half, width), BF)
    normed, first, last = call(
        norm_kernel, (pltpu.HBM((rows, width), BF), part, part), 2, name="norm"
    )(away(tokens), away(attn_gain[None]))
    low0 = to_up(first)
    high1 = to_down(last)
    low1 = to_up(last)
    high0 = to_down(first)
    own_b = swap(normed)
    far0 = to_up(low0)
    far1 = to_down(high1)
    near_a = (low0, low1, high0, high1)
    near_b = tuple(swap(v) for v in near_a)

    wk = (w_key, swap(w_key))
    wq = (w_query, swap(w_query))
    wv = (w_value, swap(w_value))
    out_b = swap(w_out)

    spread = prefix_cache.shape[1]
    outgoing = pl.pallas_call(
        prefix_kernel,
        out_shape=pltpu.HBM((reqs * spread, 2 * local), BF),
        in_specs=[pl.BlockSpec(memory_space=pltpu.SMEM), vmem()],
        out_specs=vmem(),
        compiler_params=limit(16),
        name="prefix",
    )(group_of, jnp.transpose(prefix_cache, (0, 2, 1, 3)))
    pre_a = lax.all_to_all(outgoing, ("x", "y"), split_axis=0, concat_axis=0, tiled=True)
    pre_b = swap(pre_a)

    own_w = (w_gate[0], w_up[0], w_down[0])
    other_w = tuple(swap(w) for w in own_w)

    far_b = swap(far0), swap(far1)


    slots = 2 * zs * rows
    pieces = (normed, *near_a, far0, far1, own_b, *near_b, *far_b)
    q, k, v = pl.pallas_call(
        lambda *refs: qkv_kernel(len(pieces), *refs),
        out_shape=(
            pltpu.VMEM((slots // 2, 2 * local), BF),
            pltpu.VMEM((slots, 2 * local), BF),
            pltpu.VMEM((slots, 2 * local), BF),
        ),
        in_specs=[pl.BlockSpec(memory_space=pl.ANY)] * (len(pieces) + 6) + [vmem()] * 4,
        out_specs=(vmem(),) * 3,
        scratch_shapes=[
            pltpu.VMEM((slots, width), BF),
            pltpu.VMEM((3, width, 2 * local), BF),
            pltpu.VMEM((slots, HD), F32),
            pltpu.VMEM((slots, HD), F32),
            pltpu.SemaphoreType.DMA((len(pieces),)),
            pltpu.SemaphoreType.DMA((6,)),
        ],
        compiler_params=limit(24),
        name="qkv",
    )(*map(away, (*pieces, *wk, *wq, *wv, *map(jnp.asarray, tables(rows, 2 * zs)))))
    cache = (near(q), near(k), near(v), pre_a, pre_b, w_out, out_b, lengths)
    scale = math.log2(math.e) / math.sqrt(HD)
    tmp = [pltpu.VMEM((rows, 2 * local), BF)]

    sum1, sum2 = call(
        functools.partial(attn_far_kernel, scale, 3 * rows),
        [shape((half, width), BF)] * 2,
        7,
        lengths=1,
        scratch_shapes=tmp,
        name="attn_far",
    )(*cache)
    got1 = to_up(sum1)
    got2 = to_down(sum2)
    part = shape((half, width), BF)
    wide_part = shape((half, width), F32)
    low_free, low_need, high_need, high_free = call(
        functools.partial(attn_near_kernel, scale, rows),
        [part, wide_part, wide_part, part],
        7,
        lengths=1,
        scratch_shapes=[pltpu.VMEM((2 * rows, 2 * local), BF)],
        name="attn_near",
    )(*cache)
    low_free = to_down(low_free)
    high_free = to_up(high_free)
    low_need, high_need = call(add_kernel, [part] * 2, 4, name="add")(
        low_need, got2, high_need, got1
    )
    low_need = to_down(low_need)
    high_need = to_up(high_need)
    own = call(
        functools.partial(attn_own_kernel, scale, 0),
        shape((rows, width), F32),
        7,
        lengths=1,
        scratch_shapes=tmp,
        name="attn_own",
    )(*cache)
    own, other_w = lax.optimization_barrier((own, other_w))

    blocks = 2 * experts
    wide = blocks * SUB
    table, wm, wx, order = pl.pallas_call(
        functools.partial(route_kernel, zs),
        out_shape=[
            pltpu.HBM((wide + blocks, rows), BF), pltpu.HBM((2 * rows, wide), BF),
            pltpu.HBM((2 * rows, blocks), BF), shape((experts + 1,), jnp.int32),
        ],
        in_specs=[smem(), vmem(), vmem()],
        out_specs=[vmem(), vmem(), vmem(), smem()],
        compiler_params=limit(16),
        name="route",
    )(lengths, away(routes.T), away(route_weights.T))
    hidden, send = dispatch(
        tokens, own, high_need, low_free, high_free, low_need, moe_gain[None], away(table)
    )

    def exchange(v):
        return lax.all_to_all(v, ("x", "y", "z"), 0, 0, tiled=True)

    got = exchange(send.reshape(experts, 2 * SUB, send.shape[1]))
    back = exchange(ffn(order, got, own_w, other_w)).reshape(send.shape)
    return combine(lengths, back, wm, wx, hidden)


def solution(mesh):
    side = math.isqrt(mesh.shape["req"])
    grid = Mesh(
        mesh.devices.reshape(side, side, mesh.shape["exp"] // 2, 2), ("x", "y", "z", "c")
    )
    req, exp = ("x", "y"), ("z", "c")
    every = req + exp

    return jax.shard_map(
        layer,
        mesh=grid,
        in_specs=(
            P(every, None), P(), P(None, exp), P(None, exp), P(None, exp), P(exp, None),
            P(None, req, None, exp), P(), P(), P(),
            P(every, None, None), P(every, None, None), P(every, None, None),
            P(every, None), P(every, None),
        ),
        out_specs=P(every, None),
        check_vma=False,
    )
```

```python
import functools
import math

import jax
import jax.numpy as jnp
import numpy as np
from jax import lax
from jax.experimental import pallas as pl
from jax.experimental.pallas import tpu as pltpu
from jax.sharding import Mesh
from jax.sharding import PartitionSpec as P


HD = 128
PREFIX = 1024
BF = jnp.bfloat16
F32 = jnp.float32
SUB = 8


def vmem():
    return pl.BlockSpec(memory_space=pltpu.VMEM)


def limit(mib):
    return pltpu.CompilerParams(vmem_limit_bytes=mib << 20)


def smem():
    return pl.BlockSpec(memory_space=pltpu.SMEM)


def call(kernel, out_shape, n_in, mib=16, lengths=0, **kw):
    outs = jax.tree.map(lambda _: vmem(), out_shape)
    return pl.pallas_call(
        kernel, out_shape=out_shape, in_specs=[vmem()] * n_in + [smem()] * lengths,
        out_specs=outs, compiler_params=limit(mib), **kw
    )


def near(a):
    return pltpu.with_memory_space_constraint(a, pltpu.VMEM)


def away(a):
    return pltpu.with_memory_space_constraint(a, pltpu.HBM)


def shape(dims, dtype):
    return jax.ShapeDtypeStruct(dims, dtype)


def dot(a, b):
    return jnp.dot(a, b, preferred_element_type=F32)


def rms(wide, gain):
    return wide * lax.rsqrt(jnp.mean(wide * wide, axis=-1, keepdims=True) + 1e-05) * gain


def norm_kernel(x_ref, g_ref, o_ref, first_ref, last_ref):
    normed = rms(x_ref[...].astype(F32), g_ref[...]).astype(BF)
    o_ref[...] = normed
    half = first_ref.shape[0]
    first_ref[...] = normed[:half]
    last_ref[...] = normed[half:]


def seat():
    req = lax.axis_index("x") * lax.axis_size("y") + lax.axis_index("y")
    return req, lax.axis_index("z"), lax.axis_index("c")


def held_blocks():
    _, z, core = seat()
    zs = lax.axis_size("z")
    chips = [lax.rem(z + d, zs) for d in (0, zs - 1, 1, 2)]
    return [chip * 2 + who for who in (core, 1 - core) for chip in chips]


def tables(rows, blocks):
    freqs = 10000.0 ** (-(np.arange(HD // 2) * 2.0) / HD)
    freqs = np.concatenate([freqs, freqs])
    first = (PREFIX + rows * np.arange(blocks))[:, None] * freqs
    within = np.arange(rows)[:, None] * freqs
    return [f(a).astype(np.float32) for a in (first, within) for f in (np.cos, np.sin)]


def slots_of(index):
    block = index // SUB
    return block // 2, (block % 2) * (SUB + 1) + index % SUB


def route_kernel(zs, len_ref, rt_ref, wt_ref, dt_ref, wm_ref, wx_ref, order_ref):
    top, rows = rt_ref.shape
    _, _, core = seat()
    senders = order_ref.shape[0] - 1

    def pick(wanted):
        def step(s, n):
            full = len_ref[s // zs] > (s % zs * 2 + core) * rows
            take = full == wanted

            @pl.when(take)
            def _():
                order_ref[n] = s

            return n + take.astype(jnp.int32)

        return step

    count = lax.fori_loop(0, senders, pick(True), jnp.int32(0))
    order_ref[senders] = count
    lax.fori_loop(0, senders, pick(False), count)
    blocks = wx_ref.shape[1]
    experts = blocks // 2
    wide = blocks * SUB
    iota = lambda dims, axis: lax.broadcasted_iota(jnp.int32, dims, axis)
    one = lambda hit: jnp.where(hit, 1.0, 0.0)
    row_i = iota((rows, rows), 0)
    col_i = iota((rows, rows), 1)
    e_t = iota((experts, rows), 0)
    named_t = jnp.zeros((experts, rows), F32)
    weight_t = jnp.zeros((experts, rows), F32)
    for k in range(top):
        hit = rt_ref[k : k + 1, :] == e_t
        named_t += one(hit)
        weight_t += jnp.where(hit, wt_ref[k : k + 1, :], 0.0)
    rank_t = dot(named_t.astype(BF), one(row_i < col_i).astype(BF))
    rank_t = jnp.where(named_t > 0.5, rank_t, -1.0).astype(BF)
    expert, _ = slots_of(iota((wide, experts), 0))
    spread = one(expert == iota((wide, experts), 1)).astype(BF)
    _, slot = slots_of(iota((wide, rows), 0))
    dt_ref[:wide, :] = one(dot(spread, rank_t) == slot.astype(F32)).astype(BF)
    block = iota((blocks, experts), 0)
    spread = one(block // 2 == iota((blocks, experts), 1)).astype(BF)
    slot = (iota((blocks, rows), 0) % 2) * (SUB + 1) + SUB
    dt_ref[wide:, :] = one(dot(spread, rank_t) == slot.astype(F32)).astype(BF)
    named = jnp.transpose(named_t)
    weight = jnp.transpose(weight_t)
    rank = dot(one(col_i < row_i).astype(BF), named.astype(BF))
    rank = jnp.where(named > 0.5, rank, -1.0).astype(BF)
    high = weight.astype(BF)
    low = (weight - high.astype(F32)).astype(BF)
    expert, _ = slots_of(iota((experts, wide), 1))
    spread = one(expert == iota((experts, wide), 0)).astype(BF)
    _, slot = slots_of(iota((rows, wide), 1))
    hit = dot(rank, spread) == slot.astype(F32)
    wm_ref[:rows, :] = jnp.where(hit, dot(high, spread), 0.0).astype(BF)
    wm_ref[rows:, :] = jnp.where(hit, dot(low, spread), 0.0).astype(BF)
    block = iota((experts, blocks), 1)
    spread = one(block // 2 == iota((experts, blocks), 0)).astype(BF)
    slot = (iota((rows, blocks), 1) % 2) * (SUB + 1) + SUB
    hit = dot(rank, spread) == slot.astype(F32)
    wx_ref[:rows, :] = jnp.where(hit, dot(high, spread), 0.0).astype(BF)
    wx_ref[rows:, :] = jnp.where(hit, dot(low, spread), 0.0).astype(BF)


def prefix_kernel(group_ref, x_ref, o_ref):
    rows, width = x_ref.shape[2:]
    for r in range(o_ref.shape[0] // rows):
        for j in range(2):
            o_ref[r * rows : (r + 1) * rows, j * width : (j + 1) * width] = x_ref[group_ref[r], j]


def qkv_kernel(count, *refs):
    pieces, weights, refs = refs[:count], refs[count : count + 6], refs[count + 6 :]
    c0_ref, s0_ref, c1_ref, s1_ref, q_ref, k_ref, v_ref, x_ref, w_ref = refs[:9]
    cos_ref, sin_ref, x_sem, w_sem = refs[9:]
    at = 0
    copies = []
    for i, piece in enumerate(pieces):
        n = piece.shape[0]
        copies.append(pltpu.make_async_copy(piece, x_ref.at[at : at + n], x_sem.at[i]))
        at += n
    local = w_ref.shape[2] // 2
    loads = [
        pltpu.make_async_copy(
            w, w_ref.at[i // 2, :, i % 2 * local : (i % 2 + 1) * local], w_sem.at[i]
        )
        for i, w in enumerate(weights)
    ]
    for load in loads[:2]:
        load.start()
    for copy in copies:
        copy.start()
    for load in loads[2:]:
        load.start()
    n = c1_ref.shape[0]
    side = jnp.where(lax.broadcasted_iota(jnp.int32, (n, HD), 1) < HD // 2, -1.0, 1.0)
    for i, block in enumerate(held_blocks()):
        c0, s0 = c0_ref[pl.ds(block, 1), :], s0_ref[pl.ds(block, 1), :]
        here = slice(i * n, (i + 1) * n)
        cos_ref[here, :] = c0 * c1_ref[...] - s0 * s1_ref[...]
        sin_ref[here, :] = side * (s0 * c1_ref[...] + c0 * s1_ref[...])
    half = q_ref.shape[0]
    at, left = 0, list(copies)
    for rows in (slice(0, half), slice(half, 2 * half)):
        while at < rows.stop:
            left.pop(0).wait()
            at += pieces[len(pieces) - len(left) - 1].shape[0]
        for i, o_ref in enumerate((k_ref, q_ref, v_ref)):
            if rows.start == 0:
                loads[2 * i].wait()
                loads[2 * i + 1].wait()
            elif o_ref is q_ref:
                continue
            mixed = dot(x_ref[rows, :], w_ref[i])
            if o_ref is v_ref:
                o_ref[rows, :] = mixed.astype(BF)
                continue
            for h in range(2 * local // HD):
                v = mixed[:, h * HD : (h + 1) * HD]
                turned = v * cos_ref[rows, :] + pltpu.roll(v, HD // 2, 1) * sin_ref[rows, :]
                o_ref[rows, h * HD : (h + 1) * HD] = turned.astype(BF)


def attend(scale, q_ref, k_ref, v_ref, pre_refs, len_ref, o_ref, bias_ref, first):
    req, _, _ = seat()
    blocks = held_blocks()
    n = k_ref.shape[0] // len(blocks)
    lane = lax.broadcasted_iota(jnp.int32, (1, n), 1)
    for i, block in enumerate(blocks):
        bias_ref[:, i * n : (i + 1) * n] = jnp.where(block * n + lane < len_ref[req], 0.0, -1e30)
    local = pre_refs[0].shape[1] // 2
    rows = o_ref.shape[0]
    nt = (((1,), (1,)), ((), ()))
    for h in range(q_ref.shape[1] // HD):
        side, col = divmod(h * HD, local)
        pre_ref = pre_refs[side]
        cols = slice(h * HD, (h + 1) * HD)
        q = q_ref[first : first + rows, cols]
        s1 = lax.dot_general(q, pre_ref[:, col : col + HD], nt, preferred_element_type=F32)
        s2 = lax.dot_general(q, k_ref[:, cols], nt, preferred_element_type=F32) + bias_ref[...]
        top = jnp.maximum(
            jnp.max(s1, axis=-1, keepdims=True), jnp.max(s2, axis=-1, keepdims=True)
        )
        e1 = jnp.exp2((s1 - top) * scale)
        e2 = jnp.exp2((s2 - top) * scale)
        total = jnp.sum(e1, axis=-1, keepdims=True) + jnp.sum(e2, axis=-1, keepdims=True)
        out = dot(e1.astype(BF), pre_ref[:, local + col : local + col + HD])
        out += dot(e2.astype(BF), v_ref[:, cols])
        o_ref[:, cols] = (out / total).astype(BF)


def project(a_ref, wa_ref, wb_ref):
    local = wa_ref.shape[0]
    return dot(a_ref[:, :local], wa_ref[...]) + dot(a_ref[:, local:], wb_ref[...])


def attn_far_kernel(scale, first, q, k, v, pa, pb, wa, wb, lens, o1, o2, tmp, bias):
    attend(scale, q, k, v, (pa, pb), lens, tmp, bias, first)
    total = project(tmp, wa, wb).astype(BF)
    rows = o1.shape[0]
    o1[...] = total[:rows]
    o2[...] = total[rows:]


def attn_near_kernel(
    scale, first, q, k, v, pa, pb, wa, wb, lens, low_free, low_need, high_need, high_free,
    tmp, bias,
):
    attend(scale, q, k, v, (pa, pb), lens, tmp, bias, first)
    total = project(tmp, wa, wb)
    n = low_free.shape[0]
    for i, o_ref in enumerate((low_free, low_need, high_need, high_free)):
        o_ref[...] = total[i * n : (i + 1) * n].astype(o_ref.dtype)


def attn_own_kernel(scale, first, q, k, v, pa, pb, wa, wb, lens, o, tmp, bias):
    attend(scale, q, k, v, (pa, pb), lens, tmp, bias, first)
    o[...] = project(tmp, wa, wb)


def add_kernel(a_ref, a_got, b_ref, b_got, a_out, b_out):
    a_out[...] = (a_ref[...] + a_got[...].astype(F32)).astype(BF)
    b_out[...] = (b_ref[...] + b_got[...].astype(F32)).astype(BF)


def dispatch_kernel(t_ref, own_ref, a1, a2, b1, b2, g_ref, d_ref, h_ref, o_ref, normed, extra):
    half = a1.shape[0]
    width = t_ref.shape[1]
    part = width // SUB
    wide = o_ref.shape[0]
    blocks = wide // SUB
    for at, x, y in ((0, a1, a2), (half, b1, b2)):
        here = slice(at, at + half)
        attn_out = own_ref[here, :] + x[...].astype(F32) + y[...].astype(F32)
        hidden = (t_ref[here, :].astype(F32) + attn_out).astype(BF)
        h_ref[here, :] = hidden
        normed[here, :] = rms(hidden.astype(F32), g_ref[...]).astype(BF)
    for b in range(0, SUB, 2):
        x = normed[:, b * part : (b + 2) * part]
        o_ref[:, b * part : (b + 2) * part] = dot(d_ref[:wide, :], x).astype(BF)
        more = dot(d_ref[wide:, :], x)
        for n in range(2 * part // 128):
            row, i = divmod(n, part // 128)
            extra[i, pl.ds(b + row, blocks, stride=SUB), :] = more[:, n * 128 : (n + 1) * 128]
    for i in range(part // 128):
        o_ref[:, width + i * 128 : width + (i + 1) * 128] = extra[i].astype(BF)


def dispatch(tokens, *rest):
    args = (tokens, *rest)
    rows, width = tokens.shape
    part = width // SUB
    wide = rest[-1].shape[0] // (SUB + 1) * SUB
    return call(
        dispatch_kernel,
        (pltpu.HBM((rows, width), BF), pltpu.VMEM((wide, width + part), BF)),
        len(args),
        scratch_shapes=[
            pltpu.VMEM((rows, width), BF), pltpu.VMEM((part // 128, wide, 128), F32),
        ],
        name="dispatch",
    )(*args)


def ffn_kernel(group, order_ref, x_ref, *refs):
    weights = refs[:3], refs[3:6]
    o_ref, rows_ref, act, extra = refs[6:]
    senders, each = x_ref.shape[:2]
    width = rows_ref.shape[1]
    part = width // SUB
    wide = group * each
    blocks = wide // SUB
    hidden = act.shape[1] // 2
    steps = (order_ref[senders] + group - 1) // group

    def body(j, carry):
        for s in range(group):
            x = x_ref.at[order_ref[j * group + s]]
            here = slice(s * each, (s + 1) * each)
            rows_ref[here, :] = x[:, :width]
            for i in range(part // 128):
                extra[i, here, :] = x[:, width + i * 128 : width + (i + 1) * 128].astype(F32)
        for b in range(SUB):
            for i in range(part // 128):
                col = b * part + i * 128
                rows_ref[wide:, col : col + 128] = extra[i, pl.ds(b, blocks, stride=SUB), :].astype(
                    BF
                )
        for h, (g_ref, u_ref, _) in enumerate(weights):
            gate = dot(rows_ref[...], g_ref[...])
            silu = 0.5 * gate * (1.0 + jnp.tanh(0.5 * gate))
            upper = dot(rows_ref[...], u_ref[...])
            act[:, h * hidden : (h + 1) * hidden] = (silu * upper).astype(BF)
        total = dot(act[:, :hidden], weights[0][2][...])
        total += dot(act[:, hidden:], weights[1][2][...])
        for b in range(SUB):
            for i in range(part // 128):
                col = b * part + i * 128
                extra[i, pl.ds(b, blocks, stride=SUB), :] = total[wide:, col : col + 128]
        for s in range(group):
            o = o_ref.at[order_ref[j * group + s]]
            here = slice(s * each, (s + 1) * each)
            o[:, :width] = total[here].astype(BF)
            for i in range(part // 128):
                o[:, width + i * 128 : width + (i + 1) * 128] = extra[i, here, :].astype(BF)
        return carry

    lax.fori_loop(0, steps, body, 0)


def ffn(order, x, w0, w1):
    width, hidden = w0[0].shape
    each = x.shape[1]
    group = 16
    wide = group * each
    rows = wide + wide // SUB
    return pl.pallas_call(
        functools.partial(ffn_kernel, group),
        out_shape=pltpu.VMEM(x.shape, BF),
        in_specs=[smem()] + [vmem()] * 7,
        out_specs=vmem(),
        scratch_shapes=[
            pltpu.VMEM((rows, width), BF),
            pltpu.VMEM((rows, 2 * hidden), BF),
            pltpu.VMEM((width // SUB // 128, wide, 128), F32),
        ],
        compiler_params=limit(16),
        name="ffn",
    )(order, *map(near, (x, *w0, *w1)))


def combine_kernel(r_ref, wm_ref, wx_ref, h_ref, len_ref, o_ref, extra):
    rows, width = o_ref.shape
    part = width // SUB
    blocks = r_ref.shape[0] // SUB
    req, z, core = seat()
    live = len_ref[req] - (z * 2 + core) * rows
    for i in range(part // 128):
        extra[i] = r_ref[:, width + i * 128 : width + (i + 1) * 128].astype(F32)
    for b in range(0, SUB, 2):
        cols = slice(b * part, (b + 2) * part)
        more = [
            extra[i, pl.ds(b + n, blocks, stride=SUB), :]
            for n in range(2)
            for i in range(part // 128)
        ]
        more = jnp.concatenate(more, axis=1).astype(BF)
        both = dot(wm_ref[...], r_ref[:, cols]) + dot(wx_ref[...], more)
        out = h_ref[:, cols].astype(F32) + both[:rows] + both[rows:]
        row = lax.broadcasted_iota(jnp.int32, out.shape, 0)
        o_ref[:, cols] = jnp.where(row < live, out, 0.0).astype(BF)


def combine(lengths, back, wm, wx, hidden):
    part = hidden.shape[1] // SUB
    return call(
        combine_kernel,
        shape(hidden.shape, BF),
        4,
        lengths=1,
        scratch_shapes=[pltpu.VMEM((part // 128, back.shape[0], 128), F32)],
        name="combine",
    )(near(back), wm, wx, hidden, lengths)


def layer(
    tokens, attn_gain, w_query, w_key, w_value, w_out, prefix_cache, group_of, lengths,
    moe_gain, w_gate, w_up, w_down, routes, route_weights,
):
    rows, width = tokens.shape
    zs = lax.axis_size("z")
    reqs = lax.axis_size("x") * lax.axis_size("y")
    experts = reqs * zs
    local = w_query.shape[1]
    up = [(i, (i + 1) % zs) for i in range(zs)]
    down = [(i, (i - 1) % zs) for i in range(zs)]
    swap = lambda v: lax.ppermute(v, "c", [(0, 1), (1, 0)])
    to_up = lambda v: lax.ppermute(v, "z", up)
    to_down = lambda v: lax.ppermute(v, "z", down)
    half = rows // 2

    part = pltpu.HBM((half, width), BF)
    normed, first, last = call(
        norm_kernel, (pltpu.HBM((rows, width), BF), part, part), 2, name="norm"
    )(away(tokens), away(attn_gain[None]))
    low0 = to_up(first)
    high1 = to_down(last)
    low1 = to_up(last)
    high0 = to_down(first)
    own_b = swap(normed)
    far0 = to_up(low0)
    far1 = to_down(high1)
    near_a = (low0, low1, high0, high1)
    near_b = tuple(swap(v) for v in near_a)

    wk = (w_key, swap(w_key))
    wq = (w_query, swap(w_query))
    wv = (w_value, swap(w_value))
    out_b = swap(w_out)

    spread = prefix_cache.shape[1]
    outgoing = pl.pallas_call(
        prefix_kernel,
        out_shape=pltpu.HBM((reqs * spread, 2 * local), BF),
        in_specs=[pl.BlockSpec(memory_space=pltpu.SMEM), vmem()],
        out_specs=vmem(),
        compiler_params=limit(16),
        name="prefix",
    )(away(group_of), jnp.transpose(prefix_cache, (0, 2, 1, 3)))
    pre_a = lax.all_to_all(outgoing, ("x", "y"), split_axis=0, concat_axis=0, tiled=True)
    pre_b = swap(pre_a)

    own_w = (w_gate[0], w_up[0], w_down[0])
    other_w = tuple(swap(w) for w in own_w)

    far_b = swap(far0), swap(far1)


    slots = 2 * zs * rows
    pieces = (normed, *near_a, far0, far1, own_b, *near_b, *far_b)
    q, k, v = pl.pallas_call(
        lambda *refs: qkv_kernel(len(pieces), *refs),
        out_shape=(
            pltpu.VMEM((slots // 2, 2 * local), BF),
            pltpu.VMEM((slots, 2 * local), BF),
            pltpu.VMEM((slots, 2 * local), BF),
        ),
        in_specs=[pl.BlockSpec(memory_space=pl.ANY)] * (len(pieces) + 6) + [vmem()] * 4,
        out_specs=(vmem(),) * 3,
        scratch_shapes=[
            pltpu.VMEM((slots, width), BF),
            pltpu.VMEM((3, width, 2 * local), BF),
            pltpu.VMEM((slots, HD), F32),
            pltpu.VMEM((slots, HD), F32),
            pltpu.SemaphoreType.DMA((len(pieces),)),
            pltpu.SemaphoreType.DMA((6,)),
        ],
        compiler_params=limit(24),
        name="qkv",
    )(*map(away, (*pieces, *wk, *wq, *wv, *map(jnp.asarray, tables(rows, 2 * zs)))))
    cache = (near(q), near(k), near(v), pre_a, pre_b, w_out, out_b, lengths)
    scale = math.log2(math.e) / math.sqrt(HD)
    masks = pltpu.VMEM((1, slots), F32)
    tmp = [pltpu.VMEM((rows, 2 * local), BF), masks]

    sum1, sum2 = call(
        functools.partial(attn_far_kernel, scale, 3 * rows),
        [shape((half, width), BF)] * 2,
        7,
        lengths=1,
        scratch_shapes=tmp,
        name="attn_far",
    )(*cache)
    got1 = to_up(sum1)
    got2 = to_down(sum2)
    part = shape((half, width), BF)
    wide_part = shape((half, width), F32)
    low_free, low_need, high_need, high_free = call(
        functools.partial(attn_near_kernel, scale, rows),
        [part, wide_part, wide_part, part],
        7,
        lengths=1,
        scratch_shapes=[pltpu.VMEM((2 * rows, 2 * local), BF), masks],
        name="attn_near",
    )(*cache)
    low_free = to_down(low_free)
    high_free = to_up(high_free)
    low_need, high_need = call(add_kernel, [part] * 2, 4, name="add")(
        low_need, got2, high_need, got1
    )
    low_need = to_down(low_need)
    high_need = to_up(high_need)
    own = call(
        functools.partial(attn_own_kernel, scale, 0),
        shape((rows, width), F32),
        7,
        lengths=1,
        scratch_shapes=tmp,
        name="attn_own",
    )(*cache)
    own, other_w = lax.optimization_barrier((own, other_w))

    blocks = 2 * experts
    wide = blocks * SUB
    table, wm, wx, order = pl.pallas_call(
        functools.partial(route_kernel, zs),
        out_shape=[
            pltpu.VMEM((wide + blocks, rows), BF), pltpu.HBM((2 * rows, wide), BF),
            pltpu.HBM((2 * rows, blocks), BF), shape((experts + 1,), jnp.int32),
        ],
        in_specs=[smem(), vmem(), vmem()],
        out_specs=[vmem(), vmem(), vmem(), smem()],
        compiler_params=limit(16),
        name="route",
    )(lengths, away(routes.T), away(route_weights.T))
    hidden, send = dispatch(
        tokens, own, high_need, low_free, high_free, low_need, moe_gain[None], near(table)
    )

    def exchange(v):
        return lax.all_to_all(v, ("x", "y", "z"), 0, 0, tiled=True)

    got = exchange(send.reshape(experts, 2 * SUB, send.shape[1]))
    back = exchange(ffn(order, got, own_w, other_w)).reshape(send.shape)
    return combine(lengths, back, wm, wx, hidden)


def solution(mesh):
    side = math.isqrt(mesh.shape["req"])
    grid = Mesh(
        mesh.devices.reshape(side, side, mesh.shape["exp"] // 2, 2), ("x", "y", "z", "c")
    )
    req, exp = ("x", "y"), ("z", "c")
    every = req + exp

    return jax.shard_map(
        layer,
        mesh=grid,
        in_specs=(
            P(every, None), P(), P(None, exp), P(None, exp), P(None, exp), P(exp, None),
            P(None, req, None, exp), P(), P(), P(),
            P(every, None, None), P(every, None, None), P(every, None, None),
            P(every, None), P(every, None),
        ),
        out_specs=P(every, None),
        check_vma=False,
    )
```

```python
import functools
import math

import jax
import jax.numpy as jnp
import numpy as np
from jax import lax
from jax.experimental import pallas as pl
from jax.experimental.pallas import tpu as pltpu
from jax.sharding import Mesh
from jax.sharding import PartitionSpec as P


HD = 128
PREFIX = 1024
BF = jnp.bfloat16
F32 = jnp.float32
SUB = 8


def vmem():
    return pl.BlockSpec(memory_space=pltpu.VMEM)


def limit(mib):
    return pltpu.CompilerParams(vmem_limit_bytes=mib << 20)


def smem():
    return pl.BlockSpec(memory_space=pltpu.SMEM)


def call(kernel, out_shape, n_in, mib=16, **kw):
    outs = jax.tree.map(lambda _: vmem(), out_shape)
    return pl.pallas_call(
        kernel, out_shape=out_shape, in_specs=[vmem()] * n_in, out_specs=outs,
        compiler_params=limit(mib), **kw
    )


def near(a):
    return pltpu.with_memory_space_constraint(a, pltpu.VMEM)


def away(a):
    return pltpu.with_memory_space_constraint(a, pltpu.HBM)


def shape(dims, dtype):
    return jax.ShapeDtypeStruct(dims, dtype)


def dot(a, b):
    return jnp.dot(a, b, preferred_element_type=F32)


def rms(wide, gain):
    return wide * lax.rsqrt(jnp.mean(wide * wide, axis=-1, keepdims=True) + 1e-05) * gain


def norm_kernel(x_ref, g_ref, o_ref, first_ref, last_ref):
    normed = rms(x_ref[...].astype(F32), g_ref[...]).astype(BF)
    o_ref[...] = normed
    half = first_ref.shape[0]
    first_ref[...] = normed[:half]
    last_ref[...] = normed[half:]


def seat():
    req = lax.axis_index("x") * lax.axis_size("y") + lax.axis_index("y")
    return req, lax.axis_index("z"), lax.axis_index("c")


def held_blocks():
    _, z, core = seat()
    zs = lax.axis_size("z")
    chips = [lax.rem(z + d, zs) for d in (0, zs - 1, 1, 2)]
    return [chip * 2 + who for who in (core, 1 - core) for chip in chips]


def tables(rows, blocks):
    freqs = 10000.0 ** (-(np.arange(HD // 2) * 2.0) / HD)
    freqs = np.concatenate([freqs, freqs])
    first = (PREFIX + rows * np.arange(blocks))[:, None] * freqs
    within = np.arange(rows)[:, None] * freqs
    return [f(a).astype(np.float32) for a in (first, within) for f in (np.cos, np.sin)]


def slots_of(index):
    block = index // SUB
    return block // 2, (block % 2) * (SUB + 1) + index % SUB


def route_kernel(zs, len_ref, rt_ref, wt_ref, dt_ref, wm_ref, wx_ref, live_ref, order_ref):
    top, rows = rt_ref.shape
    req, z, core = seat()
    row = lax.broadcasted_iota(jnp.int32, live_ref.shape, 0)
    live_ref[...] = jnp.where(row < len_ref[req] - (z * 2 + core) * rows, 1.0, 0.0)
    senders = order_ref.shape[0] - 1

    def pick(wanted):
        def step(s, n):
            full = len_ref[s // zs] > (s % zs * 2 + core) * rows
            take = full == wanted

            @pl.when(take)
            def _():
                order_ref[n] = s

            return n + take.astype(jnp.int32)

        return step

    count = lax.fori_loop(0, senders, pick(True), jnp.int32(0))
    order_ref[senders] = count
    lax.fori_loop(0, senders, pick(False), count)
    blocks = wx_ref.shape[1]
    experts = blocks // 2
    wide = blocks * SUB
    iota = lambda dims, axis: lax.broadcasted_iota(jnp.int32, dims, axis)
    one = lambda hit: jnp.where(hit, 1.0, 0.0)
    row_i = iota((rows, rows), 0)
    col_i = iota((rows, rows), 1)
    e_t = iota((experts, rows), 0)
    named_t = jnp.zeros((experts, rows), F32)
    weight_t = jnp.zeros((experts, rows), F32)
    for k in range(top):
        hit = rt_ref[k : k + 1, :] == e_t
        named_t += one(hit)
        weight_t += jnp.where(hit, wt_ref[k : k + 1, :], 0.0)
    rank_t = dot(named_t.astype(BF), one(row_i < col_i).astype(BF))
    rank_t = jnp.where(named_t > 0.5, rank_t, -1.0).astype(BF)
    expert, _ = slots_of(iota((wide, experts), 0))
    spread = one(expert == iota((wide, experts), 1)).astype(BF)
    _, slot = slots_of(iota((wide, rows), 0))
    dt_ref[:wide, :] = one(dot(spread, rank_t) == slot.astype(F32)).astype(BF)
    block = iota((blocks, experts), 0)
    spread = one(block // 2 == iota((blocks, experts), 1)).astype(BF)
    slot = (iota((blocks, rows), 0) % 2) * (SUB + 1) + SUB
    dt_ref[wide:, :] = one(dot(spread, rank_t) == slot.astype(F32)).astype(BF)
    named = jnp.transpose(named_t)
    weight = jnp.transpose(weight_t)
    rank = dot(one(col_i < row_i).astype(BF), named.astype(BF))
    rank = jnp.where(named > 0.5, rank, -1.0).astype(BF)
    high = weight.astype(BF)
    low = (weight - high.astype(F32)).astype(BF)
    expert, _ = slots_of(iota((experts, wide), 1))
    spread = one(expert == iota((experts, wide), 0)).astype(BF)
    _, slot = slots_of(iota((rows, wide), 1))
    hit = dot(rank, spread) == slot.astype(F32)
    wm_ref[:rows, :] = jnp.where(hit, dot(high, spread), 0.0).astype(BF)
    wm_ref[rows:, :] = jnp.where(hit, dot(low, spread), 0.0).astype(BF)
    block = iota((experts, blocks), 1)
    spread = one(block // 2 == iota((experts, blocks), 0)).astype(BF)
    slot = (iota((rows, blocks), 1) % 2) * (SUB + 1) + SUB
    hit = dot(rank, spread) == slot.astype(F32)
    wx_ref[:rows, :] = jnp.where(hit, dot(high, spread), 0.0).astype(BF)
    wx_ref[rows:, :] = jnp.where(hit, dot(low, spread), 0.0).astype(BF)


def prefix_kernel(group_ref, x_ref, o_ref):
    rows, width = x_ref.shape[2:]
    for r in range(o_ref.shape[0] // rows):
        for j in range(2):
            o_ref[r * rows : (r + 1) * rows, j * width : (j + 1) * width] = x_ref[group_ref[r], j]


def qkv_kernel(count, *refs):
    pieces, weights, refs = refs[:count], refs[count : count + 6], refs[count + 6 :]
    len_hbm, c0_ref, s0_ref, c1_ref, s1_ref, q_ref, k_ref, v_ref, bias_ref = refs[:9]
    x_ref, w_ref, cos_ref, sin_ref, len_ref, x_sem, w_sem, len_sem = refs[9:]
    at = 0
    copies = []
    for i, piece in enumerate(pieces):
        n = piece.shape[0]
        copies.append(pltpu.make_async_copy(piece, x_ref.at[at : at + n], x_sem.at[i]))
        at += n
    local = w_ref.shape[2] // 2
    loads = [
        pltpu.make_async_copy(
            w, w_ref.at[i // 2, :, i % 2 * local : (i % 2 + 1) * local], w_sem.at[i]
        )
        for i, w in enumerate(weights)
    ]
    early = len(copies) // 2
    for copy in (*loads[:2], *copies[:early], *loads[2:], *copies[early:]):
        copy.start()
    facts = pltpu.make_async_copy(len_hbm, len_ref, len_sem)
    facts.start()
    n = c1_ref.shape[0]
    side = jnp.where(lax.broadcasted_iota(jnp.int32, (n, HD), 1) < HD // 2, -1.0, 1.0)
    for i, block in enumerate(held_blocks()):
        c0, s0 = c0_ref[pl.ds(block, 1), :], s0_ref[pl.ds(block, 1), :]
        here = slice(i * n, (i + 1) * n)
        if i == 0:
            facts.wait()
            req, _, _ = seat()
            lane = lax.broadcasted_iota(jnp.int32, (1, n), 1)
        bias_ref[:, here] = jnp.where(block * n + lane < len_ref[req], 0.0, -1e30)
        cos_ref[here, :] = c0 * c1_ref[...] - s0 * s1_ref[...]
        sin_ref[here, :] = side * (s0 * c1_ref[...] + c0 * s1_ref[...])
    half = q_ref.shape[0]
    at, left = 0, list(copies)
    for rows in (slice(0, half), slice(half, 2 * half)):
        while at < rows.stop:
            left.pop(0).wait()
            at += pieces[len(pieces) - len(left) - 1].shape[0]
        for i, o_ref in enumerate((k_ref, q_ref, v_ref)):
            if rows.start == 0:
                loads[2 * i].wait()
                loads[2 * i + 1].wait()
            elif o_ref is q_ref:
                continue
            mixed = dot(x_ref[rows, :], w_ref[i])
            if o_ref is v_ref:
                o_ref[rows, :] = mixed.astype(BF)
                continue
            for h in range(2 * local // HD):
                v = mixed[:, h * HD : (h + 1) * HD]
                turned = v * cos_ref[rows, :] + pltpu.roll(v, HD // 2, 1) * sin_ref[rows, :]
                o_ref[rows, h * HD : (h + 1) * HD] = turned.astype(BF)


def attend(scale, q_ref, k_ref, v_ref, pre_refs, bias_ref, o_ref, ranges):
    local = pre_refs[0].shape[1] // 2
    nt = (((1,), (1,)), ((), ()))
    for h in range(q_ref.shape[1] // HD):
        side, col = divmod(h * HD, local)
        pre_ref = pre_refs[side]
        cols = slice(h * HD, (h + 1) * HD)
        q = jnp.concatenate([q_ref[at : at + n, cols] for at, n in ranges], axis=0)
        s1 = lax.dot_general(q, pre_ref[:, col : col + HD], nt, preferred_element_type=F32)
        s2 = lax.dot_general(q, k_ref[:, cols], nt, preferred_element_type=F32) + bias_ref[...]
        top = jnp.maximum(
            jnp.max(s1, axis=-1, keepdims=True), jnp.max(s2, axis=-1, keepdims=True)
        )
        e1 = jnp.exp2((s1 - top) * scale)
        e2 = jnp.exp2((s2 - top) * scale)
        total = jnp.sum(e1, axis=-1, keepdims=True) + jnp.sum(e2, axis=-1, keepdims=True)
        out = dot(e1.astype(BF), pre_ref[:, local + col : local + col + HD])
        out += dot(e2.astype(BF), v_ref[:, cols])
        o_ref[:, cols] = (out / total).astype(BF)


def project(a_ref, wa_ref, wb_ref):
    local = wa_ref.shape[0]
    return dot(a_ref[:, :local], wa_ref[...]) + dot(a_ref[:, local:], wb_ref[...])


def attn_pair_kernel(scale, ranges, q, k, v, pa, pb, wa, wb, bias, o1, o2, tmp):
    attend(scale, q, k, v, (pa, pb), bias, tmp, ranges)
    total = project(tmp, wa, wb)
    rows = o1.shape[0]
    o1[...] = total[:rows].astype(o1.dtype)
    o2[...] = total[rows:].astype(o2.dtype)


def attn_own_kernel(scale, ranges, q, k, v, pa, pb, wa, wb, bias, o, tmp):
    attend(scale, q, k, v, (pa, pb), bias, tmp, ranges)
    o[...] = project(tmp, wa, wb)


def add_kernel(a_ref, a_got, b_ref, b_got, a_out, b_out):
    a_out[...] = (a_ref[...] + a_got[...].astype(F32)).astype(BF)
    b_out[...] = (b_ref[...] + b_got[...].astype(F32)).astype(BF)


def dispatch_kernel(t_ref, own_ref, a1, a2, b1, b2, g_ref, d_ref, h_ref, o_ref, normed, extra):
    half = a1.shape[0]
    width = t_ref.shape[1]
    part = width // SUB
    wide = o_ref.shape[0]
    blocks = wide // SUB
    for at, x, y in ((0, a1, a2), (half, b1, b2)):
        here = slice(at, at + half)
        attn_out = own_ref[here, :] + x[...].astype(F32) + y[...].astype(F32)
        hidden = (t_ref[here, :].astype(F32) + attn_out).astype(BF)
        h_ref[here, :] = hidden
        normed[here, :] = rms(hidden.astype(F32), g_ref[...]).astype(BF)
    for b in range(0, SUB, 2):
        x = normed[:, b * part : (b + 2) * part]
        o_ref[:, b * part : (b + 2) * part] = dot(d_ref[:wide, :], x).astype(BF)
        more = dot(d_ref[wide:, :], x)
        for n in range(2 * part // 128):
            row, i = divmod(n, part // 128)
            extra[i, pl.ds(b + row, blocks, stride=SUB), :] = more[:, n * 128 : (n + 1) * 128]
    for i in range(part // 128):
        o_ref[:, width + i * 128 : width + (i + 1) * 128] = extra[i].astype(BF)


def dispatch(tokens, *rest):
    args = (tokens, *rest)
    rows, width = tokens.shape
    part = width // SUB
    wide = rest[-1].shape[0] // (SUB + 1) * SUB
    return call(
        dispatch_kernel,
        (pltpu.HBM((rows, width), BF), pltpu.VMEM((wide, width + part), BF)),
        len(args),
        scratch_shapes=[
            pltpu.VMEM((rows, width), BF), pltpu.VMEM((part // 128, wide, 128), F32),
        ],
        name="dispatch",
    )(*args)


def ffn_kernel(group, order_ref, x_ref, *refs):
    weights = refs[:3], refs[3:6]
    o_ref, rows_ref, act, extra = refs[6:]
    senders, each = x_ref.shape[:2]
    width = rows_ref.shape[1]
    part = width // SUB
    wide = group * each
    blocks = wide // SUB
    hidden = act.shape[1] // 2
    steps = (order_ref[senders] + group - 1) // group

    def body(j, carry):
        for s in range(group):
            x = x_ref.at[order_ref[j * group + s]]
            here = slice(s * each, (s + 1) * each)
            rows_ref[here, :] = x[:, :width]
            for i in range(part // 128):
                extra[i, here, :] = x[:, width + i * 128 : width + (i + 1) * 128].astype(F32)
        for b in range(SUB):
            for i in range(part // 128):
                col = b * part + i * 128
                rows_ref[wide:, col : col + 128] = extra[i, pl.ds(b, blocks, stride=SUB), :].astype(
                    BF
                )
        for h, (g_ref, u_ref, _) in enumerate(weights):
            gate = dot(rows_ref[...], g_ref[...])
            silu = 0.5 * gate * (1.0 + jnp.tanh(0.5 * gate))
            upper = dot(rows_ref[...], u_ref[...])
            act[:, h * hidden : (h + 1) * hidden] = (silu * upper).astype(BF)
        total = dot(act[:, :hidden], weights[0][2][...])
        total += dot(act[:, hidden:], weights[1][2][...])
        for b in range(SUB):
            for i in range(part // 128):
                col = b * part + i * 128
                extra[i, pl.ds(b, blocks, stride=SUB), :] = total[wide:, col : col + 128]
        for s in range(group):
            o = o_ref.at[order_ref[j * group + s]]
            here = slice(s * each, (s + 1) * each)
            o[:, :width] = total[here].astype(BF)
            for i in range(part // 128):
                o[:, width + i * 128 : width + (i + 1) * 128] = extra[i, here, :].astype(BF)
        return carry

    lax.fori_loop(0, steps, body, 0)


def ffn(order, x, w0, w1):
    width, hidden = w0[0].shape
    each = x.shape[1]
    group = 16
    wide = group * each
    rows = wide + wide // SUB
    return pl.pallas_call(
        functools.partial(ffn_kernel, group),
        out_shape=pltpu.VMEM(x.shape, BF),
        in_specs=[smem()] + [vmem()] * 7,
        out_specs=vmem(),
        scratch_shapes=[
            pltpu.VMEM((rows, width), BF),
            pltpu.VMEM((rows, 2 * hidden), BF),
            pltpu.VMEM((width // SUB // 128, wide, 128), F32),
        ],
        compiler_params=limit(24),
        name="ffn",
    )(order, *map(near, (x, *w0, *w1)))


def combine_kernel(r_ref, wm_ref, wx_ref, h_ref, live_ref, o_ref, extra):
    rows, width = o_ref.shape
    part = width // SUB
    blocks = r_ref.shape[0] // SUB
    live = jnp.concatenate([live_ref[...]] * (2 * part // live_ref.shape[1]), axis=1) > 0.5
    for i in range(part // 128):
        extra[i] = r_ref[:, width + i * 128 : width + (i + 1) * 128].astype(F32)
    for b in range(0, SUB, 2):
        cols = slice(b * part, (b + 2) * part)
        more = [
            extra[i, pl.ds(b + n, blocks, stride=SUB), :]
            for n in range(2)
            for i in range(part // 128)
        ]
        more = jnp.concatenate(more, axis=1).astype(BF)
        both = dot(wm_ref[...], r_ref[:, cols]) + dot(wx_ref[...], more)
        out = h_ref[:, cols].astype(F32) + both[:rows] + both[rows:]
        o_ref[:, cols] = jnp.where(live, out, 0.0).astype(BF)


def combine(live, back, wm, wx, hidden):
    part = hidden.shape[1] // SUB
    return call(
        combine_kernel,
        shape(hidden.shape, BF),
        5,
        scratch_shapes=[pltpu.VMEM((part // 128, back.shape[0], 128), F32)],
        name="combine",
    )(near(back), wm, wx, hidden, live)


def layer(
    tokens, attn_gain, w_query, w_key, w_value, w_out, prefix_cache, group_of, lengths,
    moe_gain, w_gate, w_up, w_down, routes, route_weights,
):
    rows, width = tokens.shape
    zs = lax.axis_size("z")
    reqs = lax.axis_size("x") * lax.axis_size("y")
    experts = reqs * zs
    local = w_query.shape[1]
    up = [(i, (i + 1) % zs) for i in range(zs)]
    down = [(i, (i - 1) % zs) for i in range(zs)]
    swap = lambda v: lax.ppermute(v, "c", [(0, 1), (1, 0)])
    to_up = lambda v: lax.ppermute(v, "z", up)
    to_down = lambda v: lax.ppermute(v, "z", down)
    half = rows // 2

    part = pltpu.HBM((half, width), BF)
    normed, first, last = call(
        norm_kernel, (pltpu.HBM((rows, width), BF), part, part), 2, name="norm"
    )(away(tokens), away(attn_gain[None]))
    low0 = to_up(first)
    high1 = to_down(last)
    low1 = to_up(last)
    high0 = to_down(first)
    own_b = swap(normed)
    far0 = to_up(low0)
    far1 = to_down(high1)
    near_a = (low0, low1, high0, high1)
    near_b = tuple(swap(v) for v in near_a)

    wk = (w_key, swap(w_key))
    wq = (w_query, swap(w_query))
    wv = (w_value, swap(w_value))
    out_b = swap(w_out)

    spread = prefix_cache.shape[1]
    outgoing = pl.pallas_call(
        prefix_kernel,
        out_shape=pltpu.HBM((reqs * spread, 2 * local), BF),
        in_specs=[pl.BlockSpec(memory_space=pltpu.SMEM), vmem()],
        out_specs=vmem(),
        compiler_params=limit(16),
        name="prefix",
    )(away(group_of), jnp.transpose(prefix_cache, (0, 2, 1, 3)))
    pre_a = lax.all_to_all(outgoing, ("x", "y"), split_axis=0, concat_axis=0, tiled=True)
    pre_b = swap(pre_a)

    own_w = (w_gate[0], w_up[0], w_down[0])
    other_w = tuple(swap(w) for w in own_w)

    far_b = swap(far0), swap(far1)


    slots = 2 * zs * rows
    pieces = (normed, *near_a, far0, far1, own_b, *near_b, *far_b)
    q, k, v, bias = pl.pallas_call(
        lambda *refs: qkv_kernel(len(pieces), *refs),
        out_shape=(
            pltpu.VMEM((slots // 2, 2 * local), BF),
            pltpu.VMEM((slots, 2 * local), BF),
            pltpu.VMEM((slots, 2 * local), BF),
            pltpu.VMEM((1, slots), F32),
        ),
        in_specs=[pl.BlockSpec(memory_space=pl.ANY)] * (len(pieces) + 7) + [vmem()] * 4,
        out_specs=(vmem(),) * 4,
        scratch_shapes=[
            pltpu.VMEM((slots, width), BF),
            pltpu.VMEM((3, width, 2 * local), BF),
            pltpu.VMEM((slots, HD), F32),
            pltpu.VMEM((slots, HD), F32),
            pltpu.SMEM(lengths.shape, jnp.int32),
            pltpu.SemaphoreType.DMA((len(pieces),)),
            pltpu.SemaphoreType.DMA((6,)),
            pltpu.SemaphoreType.DMA(()),
        ],
        compiler_params=limit(24),
        name="qkv",
    )(*map(away, (*pieces, *wk, *wq, *wv, lengths, *map(jnp.asarray, tables(rows, 2 * zs)))))
    cache = (near(q), near(k), near(v), pre_a, pre_b, w_out, out_b, near(bias))
    scale = math.log2(math.e) / math.sqrt(HD)
    tmp = [pltpu.VMEM((rows, 2 * local), BF)]

    part = shape((half, width), BF)
    wide_part = shape((half, width), F32)

    def pair(starts, out, name):
        ranges = [(at, half) for at in starts]
        return call(
            functools.partial(attn_pair_kernel, scale, ranges), [out] * 2, 8,
            scratch_shapes=tmp, name=name,
        )(*cache)

    sum1, sum2 = pair((3 * rows, 3 * rows + half), part, "attn_far")
    got1 = to_up(sum1)
    got2 = to_down(sum2)
    low_free, high_free = pair((rows, 2 * rows + half), part, "attn_free")
    low_free = to_down(low_free)
    high_free = to_up(high_free)
    low_need, high_need = pair((rows + half, 2 * rows), wide_part, "attn_need")
    low_need, high_need = call(add_kernel, [part] * 2, 4, name="add")(
        low_need, got2, high_need, got1
    )
    low_need = to_down(low_need)
    high_need = to_up(high_need)
    own = call(
        functools.partial(attn_own_kernel, scale, [(0, rows)]),
        shape((rows, width), F32),
        8,
        scratch_shapes=tmp,
        name="attn_own",
    )(*cache)
    own, other_w = lax.optimization_barrier((own, other_w))

    blocks = 2 * experts
    wide = blocks * SUB
    table, wm, wx, live, order = pl.pallas_call(
        functools.partial(route_kernel, zs),
        out_shape=[
            pltpu.VMEM((wide + blocks, rows), BF), pltpu.HBM((2 * rows, wide), BF),
            pltpu.HBM((2 * rows, blocks), BF), pltpu.HBM((rows, HD), F32),
            shape((experts + 1,), jnp.int32),
        ],
        in_specs=[smem(), vmem(), vmem()],
        out_specs=[vmem(), vmem(), vmem(), vmem(), smem()],
        compiler_params=limit(16),
        name="route",
    )(lengths, away(routes.T), away(route_weights.T))
    hidden, send = dispatch(
        tokens, own, high_need, low_free, high_free, low_need, moe_gain[None], near(table)
    )

    def exchange(v):
        return lax.all_to_all(v, ("x", "y", "z"), 0, 0, tiled=True)

    got = exchange(send.reshape(experts, 2 * SUB, send.shape[1]))
    back = exchange(ffn(order, got, own_w, other_w)).reshape(send.shape)
    return combine(live, back, wm, wx, hidden)


def solution(mesh):
    side = math.isqrt(mesh.shape["req"])
    grid = Mesh(
        mesh.devices.reshape(side, side, mesh.shape["exp"] // 2, 2), ("x", "y", "z", "c")
    )
    req, exp = ("x", "y"), ("z", "c")
    every = req + exp

    return jax.shard_map(
        layer,
        mesh=grid,
        in_specs=(
            P(every, None), P(), P(None, exp), P(None, exp), P(None, exp), P(exp, None),
            P(None, req, None, exp), P(), P(), P(),
            P(every, None, None), P(every, None, None), P(every, None, None),
            P(every, None), P(every, None),
        ),
        out_specs=P(every, None),
        check_vma=False,
    )
```

```python
import functools
import math

import jax
import jax.numpy as jnp
import numpy as np
from jax import lax
from jax.experimental import pallas as pl
from jax.experimental.pallas import tpu as pltpu
from jax.sharding import Mesh
from jax.sharding import PartitionSpec as P


HD = 128
PREFIX = 1024
BF = jnp.bfloat16
F32 = jnp.float32
SUB = 8


def vmem():
    return pl.BlockSpec(memory_space=pltpu.VMEM)


def limit(mib):
    return pltpu.CompilerParams(vmem_limit_bytes=mib << 20)


def smem():
    return pl.BlockSpec(memory_space=pltpu.SMEM)


def call(kernel, out_shape, n_in, mib=16, **kw):
    outs = jax.tree.map(lambda _: vmem(), out_shape)
    return pl.pallas_call(
        kernel, out_shape=out_shape, in_specs=[vmem()] * n_in, out_specs=outs,
        compiler_params=limit(mib), **kw
    )


def near(a):
    return pltpu.with_memory_space_constraint(a, pltpu.VMEM)


def away(a):
    return pltpu.with_memory_space_constraint(a, pltpu.HBM)


def shape(dims, dtype):
    return jax.ShapeDtypeStruct(dims, dtype)


def dot(a, b):
    return jnp.dot(a, b, preferred_element_type=F32)


def rms(wide, gain):
    return wide * lax.rsqrt(jnp.mean(wide * wide, axis=-1, keepdims=True) + 1e-05) * gain


def norm_kernel(x_ref, g_ref, o_ref, first_ref, last_ref):
    normed = rms(x_ref[...].astype(F32), g_ref[...]).astype(BF)
    o_ref[...] = normed
    half = first_ref.shape[0]
    first_ref[...] = normed[:half]
    last_ref[...] = normed[half:]


def seat():
    req = lax.axis_index("x") * lax.axis_size("y") + lax.axis_index("y")
    return req, lax.axis_index("z"), lax.axis_index("c")


def held_blocks():
    _, z, core = seat()
    zs = lax.axis_size("z")
    chips = [lax.rem(z + d, zs) for d in (0, zs - 1, 1, 2)]
    return [chip * 2 + who for who in (core, 1 - core) for chip in chips]


def tables(rows, blocks):
    freqs = 10000.0 ** (-(np.arange(HD // 2) * 2.0) / HD)
    freqs = np.concatenate([freqs, freqs])
    first = (PREFIX + rows * np.arange(blocks))[:, None] * freqs
    within = np.arange(rows)[:, None] * freqs
    return [f(a).astype(np.float32) for a in (first, within) for f in (np.cos, np.sin)]


def slots_of(index):
    block = index // SUB
    return block // 2, (block % 2) * (SUB + 1) + index % SUB


def route_kernel(zs, len_ref, rt_ref, wt_ref, dt_ref, wm_ref, wx_ref, live_ref, order_ref):
    top, rows = rt_ref.shape
    req, z, core = seat()
    row = lax.broadcasted_iota(jnp.int32, live_ref.shape, 0)
    live_ref[...] = jnp.where(row < len_ref[req] - (z * 2 + core) * rows, 1.0, 0.0)
    senders = order_ref.shape[0] - 1

    def pick(wanted):
        def step(s, n):
            full = len_ref[s // zs] > (s % zs * 2 + core) * rows
            take = full == wanted

            @pl.when(take)
            def _():
                order_ref[n] = s

            return n + take.astype(jnp.int32)

        return step

    count = lax.fori_loop(0, senders, pick(True), jnp.int32(0))
    order_ref[senders] = count
    lax.fori_loop(0, senders, pick(False), count)
    blocks = wx_ref.shape[1]
    experts = blocks // 2
    wide = blocks * SUB
    iota = lambda dims, axis: lax.broadcasted_iota(jnp.int32, dims, axis)
    one = lambda hit: jnp.where(hit, 1.0, 0.0)
    row_i = iota((rows, rows), 0)
    col_i = iota((rows, rows), 1)
    e_t = iota((experts, rows), 0)
    named_t = jnp.zeros((experts, rows), F32)
    weight_t = jnp.zeros((experts, rows), F32)
    for k in range(top):
        hit = rt_ref[k : k + 1, :] == e_t
        named_t += one(hit)
        weight_t += jnp.where(hit, wt_ref[k : k + 1, :], 0.0)
    rank_t = dot(named_t.astype(BF), one(row_i < col_i).astype(BF))
    rank_t = jnp.where(named_t > 0.5, rank_t, -1.0).astype(BF)
    expert, _ = slots_of(iota((wide, experts), 0))
    spread = one(expert == iota((wide, experts), 1)).astype(BF)
    _, slot = slots_of(iota((wide, rows), 0))
    dt_ref[:wide, :] = one(dot(spread, rank_t) == slot.astype(F32)).astype(BF)
    block = iota((blocks, experts), 0)
    spread = one(block // 2 == iota((blocks, experts), 1)).astype(BF)
    slot = (iota((blocks, rows), 0) % 2) * (SUB + 1) + SUB
    dt_ref[wide:, :] = one(dot(spread, rank_t) == slot.astype(F32)).astype(BF)
    named = jnp.transpose(named_t)
    weight = jnp.transpose(weight_t)
    rank = dot(one(col_i < row_i).astype(BF), named.astype(BF))
    rank = jnp.where(named > 0.5, rank, -1.0).astype(BF)
    high = weight.astype(BF)
    low = (weight - high.astype(F32)).astype(BF)
    expert, _ = slots_of(iota((experts, wide), 1))
    spread = one(expert == iota((experts, wide), 0)).astype(BF)
    _, slot = slots_of(iota((rows, wide), 1))
    hit = dot(rank, spread) == slot.astype(F32)
    wm_ref[:rows, :] = jnp.where(hit, dot(high, spread), 0.0).astype(BF)
    wm_ref[rows:, :] = jnp.where(hit, dot(low, spread), 0.0).astype(BF)
    block = iota((experts, blocks), 1)
    spread = one(block // 2 == iota((experts, blocks), 0)).astype(BF)
    slot = (iota((rows, blocks), 1) % 2) * (SUB + 1) + SUB
    hit = dot(rank, spread) == slot.astype(F32)
    wx_ref[:rows, :] = jnp.where(hit, dot(high, spread), 0.0).astype(BF)
    wx_ref[rows:, :] = jnp.where(hit, dot(low, spread), 0.0).astype(BF)


def prefix_kernel(group_ref, x_ref, o_ref):
    rows, width = x_ref.shape[2:]
    for r in range(o_ref.shape[0] // rows):
        for j in range(2):
            o_ref[r * rows : (r + 1) * rows, j * width : (j + 1) * width] = x_ref[group_ref[r], j]


def qkv_kernel(count, *refs):
    pieces, weights, refs = refs[:count], refs[count : count + 6], refs[count + 6 :]
    len_hbm, c0_ref, s0_ref, c1_ref, s1_ref, q_ref, k_ref, v_ref, bias_ref = refs[:9]
    x_ref, w_ref, cos_ref, sin_ref, len_ref, x_sem, w_sem, len_sem = refs[9:]
    at = 0
    copies = []
    for i, piece in enumerate(pieces):
        n = piece.shape[0]
        copies.append(pltpu.make_async_copy(piece, x_ref.at[at : at + n], x_sem.at[i]))
        at += n
    local = w_ref.shape[2] // 2
    loads = [
        pltpu.make_async_copy(
            w, w_ref.at[i // 2, :, i % 2 * local : (i % 2 + 1) * local], w_sem.at[i]
        )
        for i, w in enumerate(weights)
    ]
    for load in loads[:2]:
        load.start()
    for copy in copies:
        copy.start()
    for load in loads[2:]:
        load.start()
    facts = pltpu.make_async_copy(len_hbm, len_ref, len_sem)
    facts.start()
    n = c1_ref.shape[0]
    side = jnp.where(lax.broadcasted_iota(jnp.int32, (n, HD), 1) < HD // 2, -1.0, 1.0)
    for i, block in enumerate(held_blocks()):
        c0, s0 = c0_ref[pl.ds(block, 1), :], s0_ref[pl.ds(block, 1), :]
        here = slice(i * n, (i + 1) * n)
        if i == 0:
            facts.wait()
            req, _, _ = seat()
            lane = lax.broadcasted_iota(jnp.int32, (1, n), 1)
        bias_ref[:, here] = jnp.where(block * n + lane < len_ref[req], 0.0, -1e30)
        cos_ref[here, :] = c0 * c1_ref[...] - s0 * s1_ref[...]
        sin_ref[here, :] = side * (s0 * c1_ref[...] + c0 * s1_ref[...])
    half = q_ref.shape[0]
    at, left = 0, list(copies)
    for rows in (slice(0, half), slice(half, 2 * half)):
        while at < rows.stop:
            left.pop(0).wait()
            at += pieces[len(pieces) - len(left) - 1].shape[0]
        for i, o_ref in enumerate((k_ref, q_ref, v_ref)):
            if rows.start == 0:
                loads[2 * i].wait()
                loads[2 * i + 1].wait()
            elif o_ref is q_ref:
                continue
            mixed = dot(x_ref[rows, :], w_ref[i])
            if o_ref is v_ref:
                o_ref[rows, :] = mixed.astype(BF)
                continue
            for h in range(2 * local // HD):
                v = mixed[:, h * HD : (h + 1) * HD]
                turned = v * cos_ref[rows, :] + pltpu.roll(v, HD // 2, 1) * sin_ref[rows, :]
                o_ref[rows, h * HD : (h + 1) * HD] = turned.astype(BF)


def attend(scale, q_ref, k_ref, v_ref, pre_refs, bias_ref, o_ref, first):
    local = pre_refs[0].shape[1] // 2
    rows = o_ref.shape[0]
    nt = (((1,), (1,)), ((), ()))
    for h in range(q_ref.shape[1] // HD):
        side, col = divmod(h * HD, local)
        pre_ref = pre_refs[side]
        cols = slice(h * HD, (h + 1) * HD)
        q = q_ref[first : first + rows, cols]
        s1 = lax.dot_general(q, pre_ref[:, col : col + HD], nt, preferred_element_type=F32)
        s2 = lax.dot_general(q, k_ref[:, cols], nt, preferred_element_type=F32) + bias_ref[...]
        top = jnp.maximum(
            jnp.max(s1, axis=-1, keepdims=True), jnp.max(s2, axis=-1, keepdims=True)
        )
        e1 = jnp.exp2((s1 - top) * scale)
        e2 = jnp.exp2((s2 - top) * scale)
        total = jnp.sum(e1, axis=-1, keepdims=True) + jnp.sum(e2, axis=-1, keepdims=True)
        out = dot(e1.astype(BF), pre_ref[:, local + col : local + col + HD])
        out += dot(e2.astype(BF), v_ref[:, cols])
        o_ref[:, cols] = (out / total).astype(BF)


def project(a_ref, wa_ref, wb_ref):
    local = wa_ref.shape[0]
    return dot(a_ref[:, :local], wa_ref[...]) + dot(a_ref[:, local:], wb_ref[...])


def attn_far_kernel(scale, first, q, k, v, pa, pb, wa, wb, bias, o1, o2, tmp):
    attend(scale, q, k, v, (pa, pb), bias, tmp, first)
    total = project(tmp, wa, wb).astype(BF)
    rows = o1.shape[0]
    o1[...] = total[:rows]
    o2[...] = total[rows:]


def attn_near_kernel(
    scale, first, q, k, v, pa, pb, wa, wb, bias, low_free, low_need, high_need, high_free,
    tmp,
):
    attend(scale, q, k, v, (pa, pb), bias, tmp, first)
    total = project(tmp, wa, wb)
    n = low_free.shape[0]
    for i, o_ref in enumerate((low_free, low_need, high_need, high_free)):
        o_ref[...] = total[i * n : (i + 1) * n].astype(o_ref.dtype)


def attn_own_kernel(scale, first, q, k, v, pa, pb, wa, wb, bias, o, tmp):
    attend(scale, q, k, v, (pa, pb), bias, tmp, first)
    o[...] = project(tmp, wa, wb)


def add_kernel(a_ref, a_got, b_ref, b_got, a_out, b_out):
    a_out[...] = (a_ref[...] + a_got[...].astype(F32)).astype(BF)
    b_out[...] = (b_ref[...] + b_got[...].astype(F32)).astype(BF)


def dispatch_kernel(t_ref, own_ref, a1, a2, b1, b2, g_ref, d_ref, h_ref, o_ref, normed, extra):
    half = a1.shape[0]
    width = t_ref.shape[1]
    part = width // SUB
    wide = o_ref.shape[0]
    blocks = wide // SUB
    for at, x, y in ((0, a1, a2), (half, b1, b2)):
        here = slice(at, at + half)
        attn_out = own_ref[here, :] + x[...].astype(F32) + y[...].astype(F32)
        hidden = (t_ref[here, :].astype(F32) + attn_out).astype(BF)
        h_ref[here, :] = hidden
        normed[here, :] = rms(hidden.astype(F32), g_ref[...]).astype(BF)
    for b in range(0, SUB, 2):
        x = normed[:, b * part : (b + 2) * part]
        o_ref[:, b * part : (b + 2) * part] = dot(d_ref[:wide, :], x).astype(BF)
        more = dot(d_ref[wide:, :], x)
        for n in range(2 * part // 128):
            row, i = divmod(n, part // 128)
            extra[i, pl.ds(b + row, blocks, stride=SUB), :] = more[:, n * 128 : (n + 1) * 128]
    for i in range(part // 128):
        o_ref[:, width + i * 128 : width + (i + 1) * 128] = extra[i].astype(BF)


def dispatch(tokens, *rest):
    args = (tokens, *rest)
    rows, width = tokens.shape
    part = width // SUB
    wide = rest[-1].shape[0] // (SUB + 1) * SUB
    return call(
        dispatch_kernel,
        (pltpu.HBM((rows, width), BF), pltpu.VMEM((wide, width + part), BF)),
        len(args),
        scratch_shapes=[
            pltpu.VMEM((rows, width), BF), pltpu.VMEM((part // 128, wide, 128), F32),
        ],
        name="dispatch",
    )(*args)


def ffn_kernel(group, order_ref, x_ref, *refs):
    weights = refs[:3], refs[3:6]
    o_ref, rows_ref, act, extra = refs[6:]
    senders, each = x_ref.shape[:2]
    width = rows_ref.shape[1]
    part = width // SUB
    wide = group * each
    blocks = wide // SUB
    hidden = act.shape[1] // 2
    steps = (order_ref[senders] + group - 1) // group

    def body(j, carry):
        for s in range(group):
            x = x_ref.at[order_ref[j * group + s]]
            here = slice(s * each, (s + 1) * each)
            rows_ref[here, :] = x[:, :width]
            for i in range(part // 128):
                extra[i, here, :] = x[:, width + i * 128 : width + (i + 1) * 128].astype(F32)
        for b in range(SUB):
            for i in range(part // 128):
                col = b * part + i * 128
                rows_ref[wide:, col : col + 128] = extra[i, pl.ds(b, blocks, stride=SUB), :].astype(
                    BF
                )
        for h, (g_ref, u_ref, _) in enumerate(weights):
            gate = dot(rows_ref[...], g_ref[...])
            silu = 0.5 * gate * (1.0 + jnp.tanh(0.5 * gate))
            upper = dot(rows_ref[...], u_ref[...])
            act[:, h * hidden : (h + 1) * hidden] = (silu * upper).astype(BF)
        total = dot(act[:, :hidden], weights[0][2][...])
        total += dot(act[:, hidden:], weights[1][2][...])
        for b in range(SUB):
            for i in range(part // 128):
                col = b * part + i * 128
                extra[i, pl.ds(b, blocks, stride=SUB), :] = total[wide:, col : col + 128]
        for s in range(group):
            o = o_ref.at[order_ref[j * group + s]]
            here = slice(s * each, (s + 1) * each)
            o[:, :width] = total[here].astype(BF)
            for i in range(part // 128):
                o[:, width + i * 128 : width + (i + 1) * 128] = extra[i, here, :].astype(BF)
        return carry

    lax.fori_loop(0, steps, body, 0)


def ffn(order, x, w0, w1):
    width, hidden = w0[0].shape
    each = x.shape[1]
    group = 16
    wide = group * each
    rows = wide + wide // SUB
    return pl.pallas_call(
        functools.partial(ffn_kernel, group),
        out_shape=pltpu.VMEM(x.shape, BF),
        in_specs=[smem()] + [vmem()] * 7,
        out_specs=vmem(),
        scratch_shapes=[
            pltpu.VMEM((rows, width), BF),
            pltpu.VMEM((rows, 2 * hidden), BF),
            pltpu.VMEM((width // SUB // 128, wide, 128), F32),
        ],
        compiler_params=limit(24),
        name="ffn",
    )(order, *map(near, (x, *w0, *w1)))


def combine_kernel(r_ref, wm_ref, wx_ref, h_ref, live_ref, o_ref, extra):
    rows, width = o_ref.shape
    part = width // SUB
    blocks = r_ref.shape[0] // SUB
    live = jnp.concatenate([live_ref[...]] * (2 * part // live_ref.shape[1]), axis=1) > 0.5
    for i in range(part // 128):
        extra[i] = r_ref[:, width + i * 128 : width + (i + 1) * 128].astype(F32)
    for b in range(0, SUB, 2):
        cols = slice(b * part, (b + 2) * part)
        more = [
            extra[i, pl.ds(b + n, blocks, stride=SUB), :]
            for n in range(2)
            for i in range(part // 128)
        ]
        more = jnp.concatenate(more, axis=1).astype(BF)
        both = dot(wm_ref[...], r_ref[:, cols]) + dot(wx_ref[...], more)
        out = h_ref[:, cols].astype(F32) + both[:rows] + both[rows:]
        o_ref[:, cols] = jnp.where(live, out, 0.0).astype(BF)


def combine(live, back, wm, wx, hidden):
    part = hidden.shape[1] // SUB
    return call(
        combine_kernel,
        shape(hidden.shape, BF),
        5,
        scratch_shapes=[pltpu.VMEM((part // 128, back.shape[0], 128), F32)],
        name="combine",
    )(near(back), wm, wx, hidden, live)


def layer(
    tokens, attn_gain, w_query, w_key, w_value, w_out, prefix_cache, group_of, lengths,
    moe_gain, w_gate, w_up, w_down, routes, route_weights,
):
    rows, width = tokens.shape
    zs = lax.axis_size("z")
    reqs = lax.axis_size("x") * lax.axis_size("y")
    experts = reqs * zs
    local = w_query.shape[1]
    up = [(i, (i + 1) % zs) for i in range(zs)]
    down = [(i, (i - 1) % zs) for i in range(zs)]
    swap = lambda v: lax.ppermute(v, "c", [(0, 1), (1, 0)])
    to_up = lambda v: lax.ppermute(v, "z", up)
    to_down = lambda v: lax.ppermute(v, "z", down)
    half = rows // 2

    part = pltpu.HBM((half, width), BF)
    normed, first, last = call(
        norm_kernel, (pltpu.HBM((rows, width), BF), part, part), 2, name="norm"
    )(away(tokens), away(attn_gain[None]))
    low0 = to_up(first)
    high1 = to_down(last)
    low1 = to_up(last)
    high0 = to_down(first)
    own_b = swap(normed)
    far0 = to_up(low0)
    far1 = to_down(high1)
    near_a = (low0, low1, high0, high1)
    near_b = tuple(swap(v) for v in near_a)

    wk = (w_key, swap(w_key))
    wq = (w_query, swap(w_query))
    wv = (w_value, swap(w_value))
    out_b = swap(w_out)

    spread = prefix_cache.shape[1]
    outgoing = pl.pallas_call(
        prefix_kernel,
        out_shape=pltpu.HBM((reqs * spread, 2 * local), BF),
        in_specs=[pl.BlockSpec(memory_space=pltpu.SMEM), vmem()],
        out_specs=vmem(),
        compiler_params=limit(16),
        name="prefix",
    )(away(group_of), jnp.transpose(prefix_cache, (0, 2, 1, 3)))
    pre_a = lax.all_to_all(outgoing, ("x", "y"), split_axis=0, concat_axis=0, tiled=True)
    pre_b = swap(pre_a)

    own_w = (w_gate[0], w_up[0], w_down[0])
    other_w = tuple(swap(w) for w in own_w)

    far0, far1 = lax.optimization_barrier((far0, far1))
    far_b = swap(far0), swap(far1)


    slots = 2 * zs * rows
    pieces = (normed, *near_a, far0, far1, own_b, *near_b, *far_b)
    q, k, v, bias = pl.pallas_call(
        lambda *refs: qkv_kernel(len(pieces), *refs),
        out_shape=(
            pltpu.VMEM((slots // 2, 2 * local), BF),
            pltpu.VMEM((slots, 2 * local), BF),
            pltpu.VMEM((slots, 2 * local), BF),
            pltpu.VMEM((1, slots), F32),
        ),
        in_specs=[pl.BlockSpec(memory_space=pl.ANY)] * (len(pieces) + 7) + [vmem()] * 4,
        out_specs=(vmem(),) * 4,
        scratch_shapes=[
            pltpu.VMEM((slots, width), BF),
            pltpu.VMEM((3, width, 2 * local), BF),
            pltpu.VMEM((slots, HD), F32),
            pltpu.VMEM((slots, HD), F32),
            pltpu.SMEM(lengths.shape, jnp.int32),
            pltpu.SemaphoreType.DMA((len(pieces),)),
            pltpu.SemaphoreType.DMA((6,)),
            pltpu.SemaphoreType.DMA(()),
        ],
        compiler_params=limit(24),
        name="qkv",
    )(*map(away, (*pieces, *wk, *wq, *wv, lengths, *map(jnp.asarray, tables(rows, 2 * zs)))))
    cache = (near(q), near(k), near(v), pre_a, pre_b, w_out, out_b, near(bias))
    scale = math.log2(math.e) / math.sqrt(HD)
    tmp = [pltpu.VMEM((rows, 2 * local), BF)]

    sum1, sum2 = call(
        functools.partial(attn_far_kernel, scale, 3 * rows),
        [shape((half, width), BF)] * 2,
        8,
        scratch_shapes=tmp,
        name="attn_far",
    )(*cache)
    got1 = to_up(sum1)
    got2 = to_down(sum2)
    part = shape((half, width), BF)
    wide_part = shape((half, width), F32)
    low_free, low_need, high_need, high_free = call(
        functools.partial(attn_near_kernel, scale, rows),
        [part, wide_part, wide_part, part],
        8,
        scratch_shapes=[pltpu.VMEM((2 * rows, 2 * local), BF)],
        name="attn_near",
    )(*cache)
    low_free = to_down(low_free)
    high_free = to_up(high_free)
    low_need, high_need = call(add_kernel, [part] * 2, 4, name="add")(
        low_need, got2, high_need, got1
    )
    low_need = to_down(low_need)
    high_need = to_up(high_need)
    own = call(
        functools.partial(attn_own_kernel, scale, 0),
        shape((rows, width), F32),
        8,
        scratch_shapes=tmp,
        name="attn_own",
    )(*cache)
    own, other_w = lax.optimization_barrier((own, other_w))

    blocks = 2 * experts
    wide = blocks * SUB
    table, wm, wx, live, order = pl.pallas_call(
        functools.partial(route_kernel, zs),
        out_shape=[
            pltpu.VMEM((wide + blocks, rows), BF), pltpu.HBM((2 * rows, wide), BF),
            pltpu.HBM((2 * rows, blocks), BF), pltpu.HBM((rows, HD), F32),
            shape((experts + 1,), jnp.int32),
        ],
        in_specs=[smem(), vmem(), vmem()],
        out_specs=[vmem(), vmem(), vmem(), vmem(), smem()],
        compiler_params=limit(16),
        name="route",
    )(lengths, away(routes.T), away(route_weights.T))
    hidden, send = dispatch(
        tokens, own, high_need, low_free, high_free, low_need, moe_gain[None], near(table)
    )

    def exchange(v):
        return lax.all_to_all(v, ("x", "y", "z"), 0, 0, tiled=True)

    got = exchange(send.reshape(experts, 2 * SUB, send.shape[1]))
    back = exchange(ffn(order, got, own_w, other_w)).reshape(send.shape)
    return combine(live, back, wm, wx, hidden)


def solution(mesh):
    side = math.isqrt(mesh.shape["req"])
    grid = Mesh(
        mesh.devices.reshape(side, side, mesh.shape["exp"] // 2, 2), ("x", "y", "z", "c")
    )
    req, exp = ("x", "y"), ("z", "c")
    every = req + exp

    return jax.shard_map(
        layer,
        mesh=grid,
        in_specs=(
            P(every, None), P(), P(None, exp), P(None, exp), P(None, exp), P(exp, None),
            P(None, req, None, exp), P(), P(), P(),
            P(every, None, None), P(every, None, None), P(every, None, None),
            P(every, None), P(every, None),
        ),
        out_specs=P(every, None),
        check_vma=False,
    )
```
